256 devices in a mesh: dp: 4 (over y), brick: 64 (over z, x, core).
Axes of the slice: x: 4, y: 4, z: 8, core: 2. Of those that a mesh axis runs over, the one named last changes fastest.
Arguments:
- features: bfloat16 [4, 512, 512, 64], P('dp', 'brick'), may hold values from -6 to 6
- occupancy: int32 [4, 512, 512], P('dp', 'brick'), may hold values 0 or 1
- neighbours: int32 [4, 512, 27], P('dp', 'brick'), may hold values from -1 to 511, as said below
- owners: int32 [4, 512], P('dp', 'brick'), may hold values from 0 to 511, as said below
- w_conv: bfloat16 [3, 3, 3, 64, 64], replicated, may hold values from -0.15625 to 0.15625
- w_down: bfloat16 [2, 2, 2, 64, 128], replicated, may hold values from -0.25 to 0.25
- w_point: bfloat16 [128, 256], replicated, may hold values from -0.5 to 0.5
- cotangent: bfloat16 [4, 512, 64, 256], P('dp', 'brick'), may hold values from -0.015625 to 0.015625
Outputs:
- grad_w_conv: float32 [3, 3, 3, 64, 64], replicated
- grad_w_down: float32 [2, 2, 2, 64, 128], replicated
- grad_w_point: float32 [128, 256], replicated
The draws below stay inside these ranges and needn't reach their ends.
Inputs may be any that keep to these rules, and one draw needn't show every extreme that they name: `neighbours`: bricks of a scene form a lattice of 128 x 4 x 1 bricks, 8 consecutive ids a device; an entry names the lattice neighbour at its column's offset or is -1; column 13 is the brick itself. Columns with first offset 0 name bricks of the same device, offset -1 of the same or the previous device, offset +1 of the same or the next. `owners`: within a scene a permutation of the coarse slots; a slot's device is slot // 8. A device hands exactly 1 bricks to each device it hands any to.
All inputs are finite; a program needn't handle non-finite values. No bound on the sum of `occupancy` on one device may be relied on, other than what follows from the above.
Results may differ from the reference program's by a relative error of at most 0.012.
Values may be sent and summed in bfloat16 or wider, within the bound.
A program may use at most 64 MiB of HBM per device.

```python
import jax
import jax.numpy as jnp
from jax import lax

C0 = 64
C1 = 128
C2 = 256
BY = 4
BZ = 1
NB = 8
NBT = 512
N_DP = 4
N_BRICK = 64


def draw_neighbours(key, part):
    cells = jnp.arange(NBT, dtype=jnp.int32)
    device_of = cells // NB
    inner = cells % NB
    xpos = device_of * 2 + inner // (BY * BZ)
    ypos = inner // BZ % BY
    zpos = inner % BZ
    columns = []
    for a in range(3):
        for b in range(3):
            for c in range(3):
                near_x = xpos + a - 1
                near_y = ypos + b - 1
                near_z = zpos + c - 1
                inside = (near_x >= 0) & (near_x < 2 * N_BRICK) & (near_y >= 0) & (near_y < BY) & (near_z >= 0) & (near_z < BZ)
                ident = near_x // 2 * NB + near_x % 2 * (BY * BZ) + near_y * BZ + near_z
                columns.append(jnp.where(inside, ident, -1))
    lattice = jnp.stack(columns, axis=1)
    keep = jax.random.randint(jax.random.fold_in(key, 3), (N_DP, NBT, 27), 0, 4) > 0
    centre = (jnp.arange(27) == 13)[None, None, :]
    return jnp.where(keep | centre, lattice[None], -1).astype(jnp.int32)


def place_value(order, where, wanted):
    found = jnp.argmax(order == wanted).astype(jnp.int32)
    held = order[where]
    return order.at[found].set(held).at[where].set(wanted)


def permute_bricks(subkey):
    order = jax.random.permutation(subkey, N_BRICK).astype(jnp.int32)
    order = place_value(order, 0, N_BRICK // 2)
    order = place_value(order, 1, 1)
    order = place_value(order, 2, N_BRICK - 1)
    return order


def permute_slots(subkey):
    return jax.random.permutation(subkey, NB)


def draw_owners(key, part):
    shift_keys = jax.random.split(jax.random.fold_in(key, 7), N_DP)
    shifts = jax.vmap(permute_bricks)(shift_keys)
    slot_keys = jax.random.split(jax.random.fold_in(key, 11), N_DP * N_BRICK)
    orders = jax.vmap(permute_slots)(slot_keys).reshape(N_DP, N_BRICK, NB)
    inner = jnp.arange(NB, dtype=jnp.int32)
    offsets = shifts[:, inner % N_BRICK]
    source = jnp.arange(N_BRICK, dtype=jnp.int32)[None, :, None]
    dest_dev = (source + offsets[:, None, :]) % N_BRICK
    group = jnp.arange(N_DP, dtype=jnp.int32)[:, None, None]
    slots_at = orders[group, dest_dev, inner[None, None, :]]
    return (dest_dev * NB + slots_at).reshape(N_DP, NBT).astype(jnp.int32)


def touch_ends(drawn, stream_key, smallest, top_value):
    extent = drawn.shape
    index_at = [jax.random.randint(jax.random.fold_in(stream_key, axis), (), 0, extent[axis]) for axis in range(len(extent))]
    drawn = drawn.at[tuple(index_at)].set(smallest)
    longest = extent.index(max(extent))
    index_at[longest] = (index_at[longest] + 1) % extent[longest]
    return drawn.at[tuple(index_at)].set(top_value)


def block_scale(rng, dims, cuts, low, high):
    factor_of = 1.0
    for dim, parts in cuts:
        steps = jax.random.uniform(jax.random.fold_in(jax.random.fold_in(rng, 6), dim), (parts,), jnp.float32, low / len(cuts), high / len(cuts))
        factor_of = factor_of * jnp.repeat(jnp.exp(steps), dims[dim] // parts).reshape((-1,) + (1,) * (len(dims) - 1 - dim))
    return factor_of


def bell_draw(stream_key, shape, deviation, reach, cuts=(), held_as=jnp.bfloat16):
    values = deviation * jax.random.normal(stream_key, shape, jnp.float32)
    if cuts:
        values = values * block_scale(stream_key, shape, cuts, -0.22, 0.18)
    return jnp.clip(values, -reach, reach).astype(held_as)


def setup_inputs(seed: int = 0) -> dict:
    keys = jax.random.split(jax.random.key(seed), 9)
    features = bell_draw(keys[0], (N_DP, NBT, 512, C0), 1.0, 6.0, ((0, 4), (1, 64)))
    occupancy = touch_ends((jax.random.randint(keys[1], (N_DP, NBT, 512), 0, 4) < 3).astype(jnp.int32), jax.random.fold_in(keys[1], 1), 0, 1)
    neighbours = draw_neighbours(jax.random.fold_in(keys[8], 71), 0)
    owners = draw_owners(jax.random.fold_in(keys[8], 71), 0)
    w_conv = bell_draw(keys[4], (3, 3, 3, C0, C0), (27 * C0) ** -0.5, 0.15625)
    w_down = bell_draw(keys[5], (2, 2, 2, C0, C1), (8 * C0) ** -0.5, 0.25)
    w_point = bell_draw(keys[6], (C1, C2), C1 ** -0.5, 0.5)
    cotangent = bell_draw(keys[7], (N_DP, NBT, 64, C2), ((N_DP * NBT * 64) ** -0.5), 0.015625, ((0, 4), (1, 64)))
    return dict(features=features, occupancy=occupancy, neighbours=neighbours, owners=owners, w_conv=w_conv, w_down=w_down, w_point=w_point, cotangent=cotangent)


SPANS = ((7, 8), (0, 8), (0, 1))


def assemble(pools, indices):
    planes = []
    for a in range(3):
        row_parts = []
        for b in range(3):
            col_parts = []
            for c in range(3):
                window_part = pools[a][:, :, SPANS[b][0]:SPANS[b][1], SPANS[c][0]:SPANS[c][1], :]
                col_parts.append(jnp.take(window_part, indices[a][:, 9 * a + 3 * b + c], axis=0, mode="clip"))
            row_parts.append(jnp.concatenate(col_parts, axis=3))
        planes.append(jnp.concatenate(row_parts, axis=2))
    return jnp.concatenate(planes, axis=1)


def silu_slope(signal):
    gate_value = jax.nn.sigmoid(signal)
    return gate_value * (1.0 + signal * (1.0 - gate_value))


def one_group(features, occupancy, neighbours, owners, w_conv, w_down, w_point, cotangent):
    brick_count = features.shape[0]
    in_width = features.shape[2]
    mid_width = w_point.shape[0]
    highest = lax.Precision.HIGHEST
    bricks = features.reshape(brick_count, 8, 8, 8, in_width)
    brick_pool = jnp.concatenate([bricks, jnp.zeros((1, 8, 8, 8, in_width), bricks.dtype)], axis=0)
    pool_index = jnp.where(neighbours >= 0, neighbours, brick_count).astype(jnp.int32)
    padded = assemble((brick_pool[:, 7:8], brick_pool, brick_pool[:, 0:1]), (pool_index, pool_index, pool_index))
    pre_act = lax.conv_general_dilated(padded.astype(jnp.float32), w_conv.astype(jnp.float32), (1, 1, 1), "VALID", dimension_numbers=("NDHWC", "DHWIO", "NDHWC"), precision=highest)
    occupied = occupancy.reshape(brick_count, 8, 8, 8, 1).astype(jnp.float32)
    hidden = (jax.nn.silu(pre_act) * occupied).astype(jnp.bfloat16)
    grouped = hidden.reshape(brick_count, 4, 2, 4, 2, 4, 2, in_width)
    down_act = jnp.einsum("bpiqjrkc,ijkcd->bpqrd", grouped.astype(jnp.float32), w_down.astype(jnp.float32), precision=highest)
    coarse = jax.nn.silu(down_act).astype(jnp.bfloat16).reshape(brick_count, -1)
    placed = jnp.zeros_like(coarse).at[owners].set(coarse)
    row_block = placed.reshape(-1, mid_width)
    point_act = jnp.dot(row_block, w_point, preferred_element_type=jnp.float32)
    grad_point = (cotangent.reshape(point_act.shape).astype(jnp.float32) * silu_slope(point_act)).astype(jnp.bfloat16)
    grad_w_point = jnp.dot(row_block.T, grad_point, preferred_element_type=jnp.float32)
    grad_placed = jnp.dot(grad_point, w_point.T, preferred_element_type=jnp.float32).astype(jnp.bfloat16)
    grad_coarse = grad_placed.reshape(brick_count, -1)[owners]
    grad_down = (grad_coarse.reshape(down_act.shape).astype(jnp.float32) * silu_slope(down_act)).astype(jnp.bfloat16)
    grad_w_down = jnp.einsum("bpiqjrkc,bpqrd->ijkcd", grouped.astype(jnp.float32), grad_down.astype(jnp.float32), precision=highest)
    grad_hidden = jnp.einsum("bpqrd,ijkcd->bpiqjrkc", grad_down.astype(jnp.float32), w_down.astype(jnp.float32), precision=highest)
    grad_hidden = grad_hidden.reshape(brick_count, 8, 8, 8, in_width)
    grad_pre = (grad_hidden * occupied * silu_slope(pre_act)).astype(jnp.bfloat16)
    flat_grad = grad_pre.reshape(-1, in_width).astype(jnp.float32)
    term_list = []
    for a in range(3):
        for b in range(3):
            for c in range(3):
                window_part = padded[:, a:a + 8, b:b + 8, c:c + 8, :].reshape(-1, in_width).astype(jnp.float32)
                term_list.append(jnp.dot(window_part.T, flat_grad, precision=highest))
    grad_w_conv = jnp.stack(term_list).reshape(3, 3, 3, in_width, in_width)
    return grad_w_conv, grad_w_down, grad_w_point


def reference(features, occupancy, neighbours, owners, w_conv, w_down, w_point, cotangent):
    totals = None
    for group in range(N_DP):
        result = one_group(features[group], occupancy[group], neighbours[group], owners[group], w_conv, w_down, w_point, cotangent[group])
        if totals is None:
            totals = result
        else:
            totals = tuple(left + right for left, right in zip(totals, result))
    return (totals[0], totals[1], totals[2])
```

```python
import jax
import jax.numpy as jnp
import numpy as np
from jax import lax
from jax.experimental import pallas as pl
from jax.experimental.pallas import tpu as pltpu
from jax.sharding import PartitionSpec as P

MESH = pl.DeviceIdType.MESH
NX = 4
NC = 2
NSUB = 4
BF = jnp.bfloat16
F32 = jnp.float32


def where_am_i():
    spot = lax.axis_index("brick")
    return spot // (NX * NC), spot // NC % NX, spot % NC


def brick_at(z, x, c):
    return (z * NX + x) * NC + c


def greet(mates):
    barrier = pltpu.get_barrier_semaphore()
    for mate in mates:
        pl.semaphore_signal(barrier, inc=1, device_id=mate, device_id_type=MESH)
    pl.semaphore_wait(barrier, len(mates))


def exchange_kernel(
    nz, up_ref, down_ref, cot_ref, dec_ref, before_ref, after_ref, out_ref,
    before_in, after_in, pool0, pool1, pool2, pool3, picked, landed, dec_in, dec_s,
    halo_send, halo_recv, dec_send, dec_recv, dec_sem,
    right_send, right_recv, left_send, left_recv, pair_send, pair_recv, row_send, row_recv,
):
    z, x, c = where_am_i()
    spot = lax.axis_index("brick")
    total = nz * NX * NC
    zr, zl = (z + 1) % nz, (z + nz - 1) % nz
    right, left = {"brick": brick_at(zr, x, c)}, {"brick": brick_at(zl, x, c)}
    pair = {"brick": brick_at(z, x, 1 - c)}
    row = [{"brick": brick_at(z, (x + g) % NX, c)} for g in range(1, NX)]
    ahead, behind = {"brick": (spot + 1) % total}, {"brick": (spot + total - 1) % total}
    greet([right, left, pair, ahead, behind] + row)

    pools = [pool0, pool1, pool2, pool3]
    pending = []

    def send(src, dst, ssem, rsem, mate):
        copy = pltpu.make_async_remote_copy(
            src_ref=src, dst_ref=dst, send_sem=ssem, recv_sem=rsem, device_id=mate, device_id_type=MESH
        )
        copy.start()
        pending.append(copy)
        return copy

    dec_copies = [
        send(dec_ref, dec_in.at[g], dec_send.at[g], dec_recv.at[g], row[g]) for g in range(NX - 1)
    ]
    halo_up = send(up_ref, before_in, halo_send.at[0], halo_recv.at[0], ahead)
    halo_down = send(down_ref, after_in, halo_send.at[1], halo_recv.at[1], behind)

    cells = cot_ref.shape[1] // NSUB

    def own(k):
        return cot_ref.at[:, pl.ds(k * cells, cells), :]

    far = nz // 2
    rights, lefts, pairs, rows = {}, {}, {}, {}

    def start_own(k):
        rights[1, k] = send(own(k), pools[k].at[c, z], right_send.at[0, k], right_recv.at[0, k], right)
        lefts[1, k] = send(own(k), pools[k].at[c, z], left_send.at[0, k], left_recv.at[0, k], left)
        pairs[0, k] = send(own(k), pools[k].at[c, z], pair_send.at[0, k], pair_recv.at[0, k], pair)
        pools[k][c, z] = cot_ref[:, k * cells : (k + 1) * cells, :]

    def goes_right(s, k):
        return s < far or (s == far and k % 2 == 0)

    def goes_left(s, k):
        return s < far or (s == far and k % 2 == 1)

    halves = [(0, 1), (2, 3)]
    for k in halves[0]:
        start_own(k)
    for g in range(NX - 1):
        dec_copies[g].wait_recv()
        local = pltpu.make_async_copy(dec_in.at[g], dec_s.at[g], dec_sem.at[g])
        local.start()
        local.wait()
    local = pltpu.make_async_copy(dec_ref, dec_s.at[NX - 1], dec_sem.at[NX - 1])
    local.start()
    local.wait()

    def pick(g, k, b):
        return pools[k][dec_s[g, 0, b], dec_s[g, 1, b], dec_s[g, 2, b]]

    for h, ks in enumerate(halves):
        for s in range(1, far + 1):
            if s == far and h + 1 < len(halves):
                for k in halves[h + 1]:
                    start_own(k)
            for k in ks:
                if goes_right(s, k):
                    rights[s, k].wait_recv()
                    home = pools[k].at[c, (z + nz - s) % nz]
                    if goes_right(s + 1, k):
                        rights[s + 1, k] = send(home, home, right_send.at[s, k], right_recv.at[s, k], right)
                    pairs[s, k] = send(home, home, pair_send.at[s, k], pair_recv.at[s, k], pair)
                if goes_left(s, k):
                    lefts[s, k].wait_recv()
                    home = pools[k].at[c, (z + s) % nz]
                    if goes_left(s + 1, k):
                        lefts[s + 1, k] = send(home, home, left_send.at[s, k], left_recv.at[s, k], left)
                    if s < far:
                        t = nz - s
                        pairs[t, k] = send(home, home, pair_send.at[t, k], pair_recv.at[t, k], pair)
                    else:
                        pairs[s, k] = send(home, home, pair_send.at[s, k], pair_recv.at[s, k], pair)
        for k in ks:
            for t in range(nz):
                pairs[t, k].wait_recv()
            for g in range(NX - 1):
                for b in range(8):
                    picked[g, k, b] = pick(NX - 2 - g, k, b)
                rows[g, k] = send(picked.at[g, k], landed.at[x, k], row_send.at[g, k], row_recv.at[g, k], row[g])
            for b in range(8):
                landed[x, k, b] = pick(NX - 1, k, b)

    halo_up.wait_recv()
    halo_down.wait_recv()
    before_ref[...] = before_in[...]
    after_ref[...] = after_in[...]
    for k in range(NSUB):
        for g in range(NX - 1):
            rows[g, k].wait_recv()
    for b in range(8):
        for k in range(NSUB):
            out_ref[b, k * cells : (k + 1) * cells, :] = landed[dec_s[NX - 1, 3, b], k, b]
    for copy in pending:
        copy.wait_send()


def exchange(nz, up_face, down_face, cot, dec):
    slots, cells, wide = cot.shape
    chunk = (slots, cells // NSUB, wide)
    dma = pltpu.SemaphoreType.DMA
    vmem = pl.BlockSpec(memory_space=pltpu.VMEM)
    far = nz // 2
    return pl.pallas_call(
        lambda *refs: exchange_kernel(nz, *refs),
        out_shape=(
            jax.ShapeDtypeStruct(up_face.shape, BF),
            jax.ShapeDtypeStruct(down_face.shape, BF),
            jax.ShapeDtypeStruct(cot.shape, BF),
        ),
        in_specs=[vmem] * 4,
        out_specs=(vmem,) * 3,
        scratch_shapes=[
            pltpu.VMEM(up_face.shape, BF),
            pltpu.VMEM(down_face.shape, BF),
            *[pltpu.VMEM((NC, nz) + chunk, BF)] * NSUB,
            pltpu.VMEM((NX - 1, NSUB) + chunk, BF),
            pltpu.VMEM((NX, NSUB) + chunk, BF),
            pltpu.VMEM((NX - 1, 8, 128), jnp.int32),
            pltpu.SMEM((NX, 8, 128), jnp.int32),
            dma((2,)), dma((2,)), dma((NX - 1,)), dma((NX - 1,)), dma((NX,)),
            dma((far, NSUB)), dma((far, NSUB)), dma((far, NSUB)), dma((far, NSUB)),
            dma((nz, NSUB)), dma((nz, NSUB)), dma((NX - 1, NSUB)), dma((NX - 1, NSUB)),
        ],
        compiler_params=pltpu.CompilerParams(collective_id=0, has_side_effects=True),
        name="exchange",
    )(up_face, down_face, cot, dec)


def slope_of(v):
    g = 1.0 / (1.0 + jnp.exp(-v))
    return g * (1.0 + v * (1.0 - g))


def silu_of(v):
    return v / (1.0 + jnp.exp(-v))


def dot(a, b, ca=1, cb=0):
    return lax.dot_general(a, b, (((ca,), (cb,)), ((), ())), preferred_element_type=F32)


def compute_kernel(
    src_ref, before_ref, after_ref, tgt_ref, occ_ref, u_ref, wd_ref, wp_ref, cot_ref, part_ref,
    source, taps, pre, hid_t, gpre_t, sums,
):
    source[0:512] = src_ref[...]
    source[512:544] = before_ref[...]
    source[544:576] = after_ref[...]
    pre[...] = jnp.zeros_like(pre)
    tgt = tgt_ref[...]
    which = lax.broadcasted_iota(jnp.int32, tgt.shape, 1)
    spots = lax.broadcasted_iota(jnp.int32, (512, 576), 1).astype(F32)

    def tap_step(tap, carry):
        column = jnp.sum(jnp.where(which == tap, tgt, 0.0), axis=1, keepdims=True)
        pick = jnp.where(spots == column, 1.0, 0.0).astype(BF)
        rows = dot(pick, source[...]).astype(BF)
        taps[tap] = rows
        for t in range(4):
            at = slice(128 * t, 128 * t + 128)
            pre[:, at] += dot(rows[:, 128 * t : 128 * t + 256], u_ref[tap])
        return carry

    lax.fori_loop(0, 9, tap_step, 0)

    spread = (
        lax.broadcasted_iota(jnp.int32, (8, 512), 1) // 64 == lax.broadcasted_iota(jnp.int32, (8, 512), 0)
    ).astype(F32).astype(BF)
    occ = dot(occ_ref[...], spread)
    hidden = (silu_of(pre[...]) * occ).astype(BF)
    for r in range(4):
        for ij in range(4):
            hid_t[128 * r : 128 * r + 128, 128 * ij : 128 * ij + 128] = hidden[
                128 * ij : 128 * ij + 128, 128 * r : 128 * r + 128
            ]
    down = dot(hid_t[...], wd_ref[...])
    coarse = silu_of(down).astype(BF)
    row = lax.broadcasted_iota(jnp.int32, (512, 512), 0)
    col = lax.broadcasted_iota(jnp.int32, (512, 512), 1)
    order = jnp.where(col == 4 * (row % 128) + row // 128, 1.0, 0.0).astype(BF)
    cot = dot(order, cot_ref[...])
    point = dot(coarse, wp_ref[...])
    gpoint = (cot * slope_of(point)).astype(BF)
    gwp = dot(coarse, gpoint, 0, 0)
    gplaced = dot(gpoint, wp_ref[...], 1, 1).astype(BF)
    gdown = (gplaced.astype(F32) * slope_of(down)).astype(BF)
    gwd = dot(hid_t[...], gdown, 0, 0)
    ghid = dot(gdown, wd_ref[...], 1, 1)
    for r in range(4):
        for ij in range(4):
            a = slice(128 * ij, 128 * ij + 128)
            b = slice(128 * r, 128 * r + 128)
            piece = (ghid[b, a] * occ[a, b] * slope_of(pre[a, b])).astype(BF)
            gpre_t[b, a] = piece.T

    def grad_step(tap, carry):
        total = jnp.zeros((128, 256), F32)
        for t in range(4):
            total += dot(gpre_t[128 * t : 128 * t + 128, :], taps[tap, :, 128 * t : 128 * t + 256])
        sums[tap] = total.T
        return carry

    for tap in range(9):
        grad_step(tap, 0)
    low = lax.broadcasted_iota(jnp.int32, (64, 128), 1) < 64

    def block(m):
        tap, c = m // 3, m % 3
        return sums[tap, 64 * c : 64 * c + 64, :], sums[tap, 64 * c + 64 : 64 * c + 128, :]

    for j in range(14):
        a0, a1 = block(2 * j)
        even = a0 + pltpu.roll(a1, 64, 1)
        if 2 * j + 1 < 27:
            b0, b1 = block(2 * j + 1)
            odd = pltpu.roll(b0, 64, 1) + b1
        else:
            odd = jnp.zeros_like(even)
        part_ref[j] = jnp.where(low, even, odd)
    for j in range(8):
        part_ref[14 + j] = gwd[64 * j : 64 * j + 64, :]
    for j in range(4):
        r, t = j % 2, j // 2
        part_ref[22 + j] = gwp[64 * r : 64 * r + 64, 128 * t : 128 * t + 128]
    for j in range(26, 32):
        part_ref[j] = jnp.zeros((64, 128), F32)


def compute(src, before, after, tgt, occ, u, wd, wp, cot):
    vmem = pl.BlockSpec(memory_space=pltpu.VMEM)
    return pl.pallas_call(
        compute_kernel,
        out_shape=jax.ShapeDtypeStruct((32, 64, 128), F32),
        in_specs=[vmem] * 9,
        out_specs=vmem,
        scratch_shapes=[
            pltpu.VMEM((576, 640), BF),
            pltpu.VMEM((9, 512, 640), BF),
            pltpu.VMEM((512, 512), F32),
            pltpu.VMEM((512, 512), BF),
            pltpu.VMEM((512, 512), BF),
            pltpu.VMEM((9, 256, 128), F32),
        ],
        name="compute",
    )(src, before, after, tgt, occ, u, wd, wp, cot)


def reduce_kernel(
    nz, ny, part_ref, gwc_ref, gwd_ref, gwp_ref,
    tosend, arrived, plane_out, plane_in, depth_out, depth_in, full,
    pair_send, pair_recv, plane_send, plane_recv, depth_send, depth_recv,
    back_send, back_recv, share_send, share_recv,
):
    z, x, c = where_am_i()
    y = lax.axis_index("dp")
    np_ = ny * NX
    me = y * NX + x
    pair = {"dp": y, "brick": brick_at(z, x, 1 - c)}
    plane = []
    for g in range(1, np_):
        yy, xx = (y + g // NX) % ny, (x + g % NX) % NX
        plane.append(({"dp": yy, "brick": brick_at(z, xx, c)}, yy * NX + xx, g))
    depth = [{"dp": y, "brick": brick_at((z + g) % nz, x, c)} for g in range(1, nz)]
    greet([pair] + [p[0] for p in plane] + depth)
    pending = []

    def send(src, dst, ssem, rsem, mate):
        copy = pltpu.make_async_remote_copy(
            src_ref=src, dst_ref=dst, send_sem=ssem, recv_sem=rsem, device_id=mate, device_id_type=MESH
        )
        copy.start()
        pending.append(copy)
        return copy

    pieces = 4
    size = np_ // pieces
    firsts = []
    for i in range(pieces):
        tosend[pl.ds(i * size, size)] = part_ref[pl.ds((1 - c) * np_ + i * size, size)].astype(BF)
        at = pl.ds(i * size, size)
        firsts.append(send(tosend.at[at], arrived.at[at], pair_send.at[i], pair_recv.at[i], pair))
    for i in range(pieces):
        firsts[i].wait_recv()
        at = pl.ds(i * size, size)
        plane_out[at] = (part_ref[pl.ds(c * np_ + i * size, size)] + arrived[at].astype(F32)).astype(BF)
    seconds = [
        send(plane_out.at[k], plane_in.at[g], plane_send.at[g], plane_recv.at[g], mate) for mate, k, g in plane
    ]
    total = plane_out[me].astype(F32)
    for g in range(1, np_):
        seconds[g - 1].wait_recv()
        total += plane_in[g].astype(F32)
    depth_out[...] = total.astype(BF)
    thirds = [
        send(depth_out, depth_in.at[z], depth_send.at[g], depth_recv.at[g], mate) for g, mate in enumerate(depth)
    ]
    depth_in[z] = total.astype(BF)
    for copy in thirds:
        copy.wait_recv()
    total = depth_in[0].astype(F32)
    for k in range(1, nz):
        total += depth_in[k].astype(F32)
    mine = full.at[c, me]
    full[c, me] = total.astype(BF)
    backs = [send(mine, mine, back_send.at[g], back_recv.at[g], mate) for mate, k, g in plane]
    shares = [send(mine, mine, share_send.at[0], share_recv.at[0], pair)]
    for g in range(1, np_):
        backs[g - 1].wait_recv()
        yy, xx = (y + ny - g // NX) % ny, (x + NX - g % NX) % NX
        home = full.at[c, yy * NX + xx]
        shares.append(send(home, home, share_send.at[g], share_recv.at[g], pair))
    for copy in shares:
        copy.wait_recv()
    for j in range(14):
        chunk = full[j // np_, j % np_].astype(F32)
        gwc_ref[2 * j] = chunk[:, :64]
        if 2 * j + 1 < 27:
            gwc_ref[2 * j + 1] = pltpu.roll(chunk, 64, 1)[:, :64]
    for j in range(8):
        k = 14 + j
        gwd_ref[64 * j : 64 * j + 64, :] = full[k // np_, k % np_].astype(F32)
    for j in range(4):
        r, t = j % 2, j // 2
        k = 22 + j
        gwp_ref[64 * r : 64 * r + 64, 128 * t : 128 * t + 128] = full[k // np_, k % np_].astype(F32)
    for copy in pending:
        copy.wait_send()


def reduce_all(nz, ny, part):
    vmem = pl.BlockSpec(memory_space=pltpu.VMEM)
    dma = pltpu.SemaphoreType.DMA
    np_ = ny * NX
    return pl.pallas_call(
        lambda *refs: reduce_kernel(nz, ny, *refs),
        out_shape=(
            jax.ShapeDtypeStruct((27, 64, 64), F32),
            jax.ShapeDtypeStruct((512, 128), F32),
            jax.ShapeDtypeStruct((128, 256), F32),
        ),
        in_specs=[vmem],
        out_specs=(vmem,) * 3,
        scratch_shapes=[
            pltpu.VMEM((np_, 64, 128), BF),
            pltpu.VMEM((np_, 64, 128), BF),
            pltpu.VMEM((np_, 64, 128), BF),
            pltpu.VMEM((np_, 64, 128), BF),
            pltpu.VMEM((64, 128), BF),
            pltpu.VMEM((nz, 64, 128), BF),
            pltpu.VMEM((NC, np_, 64, 128), BF),
            dma((4,)), dma((4,)), dma((np_,)), dma((np_,)), dma((nz,)), dma((nz,)),
            dma((np_,)), dma((np_,)), dma((np_,)), dma((np_,)),
        ],
        compiler_params=pltpu.CompilerParams(collective_id=1, has_side_effects=True),
        name="reduce",
    )(part)


def tap_tables():
    ids = np.arange(8)
    target = np.zeros((9, 2, 2, 8, 4, 4), np.float32)
    choose = np.zeros((9, 2, 2, 4, 4, 9), np.float32)
    for a in range(3):
        for b in range(3):
            for x in range(8):
                for y in range(8):
                    xx, yy = x + a - 1, y + b - 1
                    dx, dy = (xx + 8) // 8, (yy + 8) // 8
                    choose[3 * a + b, x % 2, y % 2, x // 2, y // 2, 3 * dx + dy] = 1.0
                    for n in ids:
                        px, py = n // 4 + dx - 1, n % 4 + dy - 1
                        if py < 0 or py > 3:
                            spot = -1
                        elif px < 0:
                            spot = 512 + py * 8 + yy % 8
                        elif px > 1:
                            spot = 544 + py * 8 + yy % 8
                        else:
                            spot = (px * 4 + py) * 64 + xx % 8 * 8 + yy % 8
                        target[3 * a + b, x % 2, y % 2, n, x // 2, y // 2] = spot
    return target, choose


def shards(features, occupancy, neighbours, owners, w_conv, w_down, w_point, cotangent):
    nz = lax.axis_size("brick") // (NX * NC)
    ny = lax.axis_size("dp")
    flat = jnp.pad(features[0].reshape(8, 8, 8, 512), ((0, 0), (0, 0), (0, 0), (64, 64)))
    up_face = flat[4:8, 7].reshape(32, 640)
    down_face = flat[0:4, 0].reshape(32, 640)
    source = flat.reshape(512, 640)

    target, choose = tap_tables()
    linked = (neighbours[0].reshape(8, 9, 3)[:, :, 1] >= 0).astype(F32)
    flags = jnp.sum(choose[:, :, :, None] * linked[None, None, None, :, None, None, :], axis=-1)
    tgt = jnp.where(flags > 0, target, -1.0)
    tgt = jnp.pad(tgt.reshape(9, 512).T, ((0, 0), (0, 7)))
    occ = occupancy[0].reshape(8, 4, 2, 4, 2, 8).transpose(2, 4, 0, 1, 3, 5).reshape(512, 8).astype(BF)
    w9 = w_conv.reshape(9, 192, 64)
    u = jnp.concatenate(
        [jnp.pad(w9, ((0, 0), (0, 64), (0, 0))), jnp.pad(w9, ((0, 0), (64, 0), (0, 0)))], axis=2
    )
    slot_dev = owners[0] // 8
    dec = jnp.stack([slot_dev % NC, slot_dev // (NX * NC), owners[0] % 8, slot_dev // NC % NX])
    dec = jnp.pad(dec, ((0, 4), (0, 120)))
    before, after, cot = exchange(nz, up_face, down_face, cotangent[0], dec)
    part = compute(
        source, before, after, tgt, occ, u, w_down.reshape(512, 128), w_point, cot.reshape(512, 256)
    )
    gwc, gwd, gwp = reduce_all(nz, ny, part)
    return gwc.reshape(3, 3, 3, 64, 64), gwd.reshape(2, 2, 2, 64, 128), gwp


def solution(mesh):
    in_specs = (
        P("dp", "brick", None, None),
        P("dp", "brick", None),
        P("dp", "brick", None),
        P("dp", "brick"),
        P(),
        P(),
        P(),
        P("dp", "brick", None, None),
    )
    return jax.shard_map(shards, mesh=mesh, in_specs=in_specs, out_specs=(P(), P(), P()), check_vma=False)
```

```python
import jax
import jax.numpy as jnp
import numpy as np
from jax import lax
from jax.experimental import pallas as pl
from jax.experimental.pallas import tpu as pltpu
from jax.sharding import PartitionSpec as P

MESH = pl.DeviceIdType.MESH
NX = 4
NC = 2
NSUB = 4
NB = 8
BF = jnp.bfloat16
F32 = jnp.float32


def where_am_i():
    spot = lax.axis_index("brick")
    return spot // (NX * NC), spot // NC % NX, spot % NC


def brick_at(z, x, c):
    return (z * NX + x) * NC + c


def greet(mates):
    barrier = pltpu.get_barrier_semaphore()
    for mate in mates:
        pl.semaphore_signal(barrier, inc=1, device_id=mate, device_id_type=MESH)
    pl.semaphore_wait(barrier, len(mates))


def slope_of(v):
    g = 1.0 / (1.0 + jnp.exp(-v))
    return g * (1.0 + v * (1.0 - g))


def silu_of(v):
    return v / (1.0 + jnp.exp(-v))


def dot(a, b, ca=1, cb=0):
    return lax.dot_general(a, b, (((ca,), (cb,)), ((), ())), preferred_element_type=F32)


RIGHT = ((1, 0), (1, 1), (1, 2), (2, 0), (2, 1), (2, 2), (1, 3), (3, 0), (3, 1), (3, 2), (2, 3), (4, 0), (4, 2), (3, 3))
LEFT = ((1, 1), (1, 0), (1, 3), (2, 1), (2, 0), (2, 3), (1, 2), (3, 1), (3, 0), (3, 3), (2, 2), (4, 1), (4, 3), (3, 2))
LAG = 3


def iota(shape, dim):
    return lax.broadcasted_iota(jnp.int32, shape, dim)


def ones_where(mask):
    return jnp.where(mask, 1.0, 0.0).astype(BF)


def tap_targets(near):
    row, tap = iota((512, 16), 0), iota((512, 16), 1)
    n = row // 16 % 8
    x = row // 4 % 4 * 2 + row // 256 + tap // 3 - 1
    y = row % 4 * 2 + row // 128 % 2 + tap % 3 - 1
    dx, dy = (x + 8) // 8, (y + 8) // 8
    px, py = n // 4 + dx - 1, n % 4 + dy - 1
    yy = (y + 8) % 8
    inner = (x + 8) % 8 * 64 + (px * 4 + py) * 8 + yy
    spot = jnp.where(px < 0, 512 + py * 8 + yy, jnp.where(px > 1, 544 + py * 8 + yy, inner))
    linked = ones_where(near >= 0)
    narrow = ones_where(iota((27, 16), 0) == 3 * iota((27, 16), 1) + 1)
    linked = dot(linked, narrow).astype(BF)
    brick = ones_where(iota((512, 8), 0) // 16 % 8 == iota((512, 8), 1))
    by_row = dot(brick, linked)
    code = 3 * dx + dy
    flag = jnp.zeros((512, 16), F32)
    for d in range(9):
        flag = flag + jnp.where(code == d, by_row[:, d : d + 1], 0.0)
    return jnp.where(flag > 0.5, spot.astype(F32), -1.0)


def occupied_at(occ):
    row, lane = iota((512, 512), 0), iota((512, 512), 1)
    brick = ones_where(iota((512, 8), 0) // 16 % 8 == iota((512, 8), 1))
    every = dot(brick, occ.astype(F32).astype(BF))
    mine = (row // 4 % 4 * 2 + row // 256) * 8 + row % 4 * 2 + row // 128 % 2
    own = jnp.where(lane // 8 == mine, every, 0.0).astype(BF)
    spread = ones_where(row % 8 == lane // 64)
    return dot(own, spread)


def step_kernel(
    nz, ny, src_ref, cot_ref, own_v, own_s, near_ref, occ_ref, w_ref, wd_ref, wp_ref,
    gwc_ref, gwd_ref, gwp_ref,
    source, halo_in, pool0, pool1, pool2, pool3, picked, landed, dec_in, dec_s,
    taps, pre, occ_at, hid_t, gpre_t, sums, part, cot_here,
    tosend, arrived, plane_out, plane_in, depth_out, depth_in, full,
    halo_send, halo_recv, dec_send, dec_recv, dec_sem,
    right_send, right_recv, left_send, left_recv, mate_send, mate_recv, row_send, row_recv,
    pair_send, pair_recv, plane_send, plane_recv, depth_send, depth_recv,
    back_send, back_recv, share_send, share_recv,
):
    z, x, c = where_am_i()
    y = lax.axis_index("dp")
    spot = lax.axis_index("brick")
    many = nz * NX * NC
    np_ = ny * NX
    me = y * NX + x

    def at(yy, brick):
        return {"dp": yy, "brick": brick}

    right, left = at(y, brick_at((z + 1) % nz, x, c)), at(y, brick_at((z + nz - 1) % nz, x, c))
    pair = at(y, brick_at(z, x, 1 - c))
    row = [at(y, brick_at(z, (x + g) % NX, c)) for g in range(1, NX)]
    ahead, behind = at(y, (spot + 1) % many), at(y, (spot + many - 1) % many)
    plane = []
    for g in range(1, np_):
        yy, xx = (y + g // NX) % ny, (x + g % NX) % NX
        plane.append((at(yy, brick_at(z, xx, c)), yy * NX + xx, g))
    depth = [at(y, brick_at((z + g) % nz, x, c)) for g in range(1, nz)]
    greet([pair, ahead, behind] + [p[0] for p in plane] + depth)

    pools = [pool0, pool1, pool2, pool3]
    pending = []

    def send(src, dst, ssem, rsem, mate):
        copy = pltpu.make_async_remote_copy(
            src_ref=src, dst_ref=dst, send_sem=ssem, recv_sem=rsem, device_id=mate, device_id_type=MESH
        )
        copy.start()
        pending.append(copy)
        return copy

    rows_src = src_ref.shape[0]
    halo_up = send(src_ref.at[pl.ds(rows_src - 32, 32)], halo_in.at[0], halo_send.at[0], halo_recv.at[0], ahead)
    halo_down = send(src_ref.at[pl.ds(0, 32)], halo_in.at[1], halo_send.at[1], halo_recv.at[1], behind)
    dec_copies = [send(own_v, dec_in.at[g], dec_send.at[g], dec_recv.at[g], row[g]) for g in range(NX - 1)]
    cells = cot_ref.shape[1] // NSUB
    rights, lefts, mates, rows = {}, {}, {}, {}

    def own(k):
        return cot_ref.at[:, pl.ds(k * cells, cells), :]

    def go_right(s, k):
        if s == 1:
            rights[1, k] = send(own(k), pools[k].at[c, z], right_send.at[0, k], right_recv.at[0, k], right)
            return
        rights[s - 1, k].wait_recv()
        home = pools[k].at[c, (z + nz - s + 1) % nz]
        rights[s, k] = send(home, home, right_send.at[s - 1, k], right_recv.at[s - 1, k], right)
        mates[s - 1, k] = send(home, home, mate_send.at[s - 1, k], mate_recv.at[s - 1, k], pair)

    def go_left(s, k):
        if s == 1:
            lefts[1, k] = send(own(k), pools[k].at[c, z], left_send.at[0, k], left_recv.at[0, k], left)
            return
        lefts[s - 1, k].wait_recv()
        home = pools[k].at[c, (z + s - 1) % nz]
        lefts[s, k] = send(home, home, left_send.at[s - 1, k], left_recv.at[s - 1, k], left)
        t = nz - s + 1
        mates[t, k] = send(home, home, mate_send.at[t, k], mate_recv.at[t, k], pair)

    def end_right(s, k):
        rights[s, k].wait_recv()
        home = pools[k].at[c, (z + nz - s) % nz]
        mates[s, k] = send(home, home, mate_send.at[s, k], mate_recv.at[s, k], pair)

    def end_left(s, k):
        lefts[s, k].wait_recv()
        home = pools[k].at[c, (z + s) % nz]
        t = nz - s
        mates[t, k] = send(home, home, mate_send.at[t, k], mate_recv.at[t, k], pair)

    def pick(g, k, b):
        o = dec_s[g, 0, b]
        return pools[k][o // NB % NC, o // (NB * NC * NX), o % NB]

    def start_rows(k):
        for t in range(nz):
            mates[t, k].wait_recv()
        for g in range(NX - 1):
            for b in range(NB):
                picked[g, k, b] = pick(NX - 2 - g, k, b)
            rows[g, k] = send(picked.at[g, k], landed.at[x, k], row_send.at[g, k], row_recv.at[g, k], row[g])
        for b in range(NB):
            landed[x, k, b] = pick(NX - 1, k, b)

    hold = {}

    def ready():
        for k in range(NSUB):
            mates[0, k] = send(own(k), pools[k].at[c, z], mate_send.at[0, k], mate_recv.at[0, k], pair)
            pools[k][c, z] = cot_ref[:, k * cells : (k + 1) * cells, :]
        source[0:512] = src_ref[...]
        hold["tgt"] = tap_targets(near_ref[...])
        occ_at[...] = occupied_at(occ_ref[...])

    def asks():
        for g in range(NX - 1):
            dec_copies[g].wait_recv()
        local = [pltpu.make_async_copy(dec_in.at[g], dec_s.at[g], dec_sem.at[g]) for g in range(NX - 1)]
        local.append(pltpu.make_async_copy(own_v, dec_s.at[NX - 1], dec_sem.at[NX - 1]))
        for copy in local:
            copy.start()
        for copy in local:
            copy.wait()

    def halo():
        halo_up.wait_recv()
        halo_down.wait_recv()
        source[512:544] = halo_in[0]
        source[544:576] = halo_in[1]

    def tap_step(tap):
        spots = iota((512, 576), 1).astype(F32)
        take = jnp.where(spots == hold["tgt"][:, tap : tap + 1], 1.0, 0.0).astype(BF)
        moved = dot(take, source[...]).astype(BF)
        taps[tap] = moved
        w = w_ref[tap]
        low = dot(w, ones_where(iota((64, 128), 0) == iota((64, 128), 1)))
        high = dot(w, ones_where(iota((64, 128), 0) + 64 == iota((64, 128), 1)))
        blank = jnp.zeros((64, 128), F32)
        u = (jnp.concatenate([low, blank], axis=0) + jnp.concatenate([blank, high], axis=0)).astype(BF)
        for t in range(4):
            lanes = slice(128 * t, 128 * t + 128)
            got = dot(moved[:, 128 * t : 128 * t + 256], u)
            pre[:, lanes] = got if tap == 0 else pre[:, lanes] + got

    def hide(ij):
        a = slice(128 * ij, 128 * ij + 128)
        hidden = (silu_of(pre[a, :]) * occ_at[a, :]).astype(BF)
        for r in range(4):
            hid_t[128 * r : 128 * r + 128, a] = hidden[:, 128 * r : 128 * r + 128]

    def coarsen():
        down = dot(hid_t[...], wd_ref[...])
        coarse = silu_of(down).astype(BF)
        hold["slope"] = slope_of(down)
        hold["coarse"] = coarse
        hold["point"] = slope_of(dot(coarse, wp_ref[...]))

    def reslope(ij):
        a = slice(128 * ij, 128 * ij + 128)
        pre[a, :] = occ_at[a, :] * slope_of(pre[a, :])

    jobs = [asks, halo]
    jobs += [lambda tap=tap: tap_step(tap) for tap in range(9)]
    jobs += [lambda ij=ij: hide(ij) for ij in range(4)]
    jobs += [coarsen]
    jobs += [lambda ij=ij: reslope(ij) for ij in range(4)]

    def work():
        if jobs:
            jobs.pop(0)()

    ends = {}
    for i, (s, k) in enumerate(RIGHT):
        if (s + 1, k) not in RIGHT:
            ends.setdefault(i + LAG, []).append((end_right, s, k))
    for i, (s, k) in enumerate(LEFT):
        if (s + 1, k) not in LEFT:
            ends.setdefault(i + LAG, []).append((end_left, s, k))
    left_over = {k: 0 for k in range(NSUB)}
    for group in ends.values():
        for _, s, k in group:
            left_over[k] += 1
    done, started = dict(left_over), []
    waiting = []
    for i in range(len(RIGHT) + LAG):
        if i < len(RIGHT):
            go_right(*RIGHT[i])
            go_left(*LEFT[i])
        for f, s, k in ends.get(i, []):
            f(s, k)
            done[k] -= 1
            if done[k] == 0:
                waiting.append((i, k))
        if i == 2:
            ready()
        if i >= 3:
            work()
            work()
        while waiting and waiting[0][0] < i:
            start_rows(waiting.pop(0)[1])
    while waiting:
        start_rows(waiting.pop(0)[1])
    while jobs:
        work()

    order_row, order_col = iota((512, 512), 0), iota((512, 512), 1)
    order = ones_where(order_col == 4 * (order_row % 128) + order_row // 128)
    for k in range(NSUB):
        for g in range(NX - 1):
            rows[g, k].wait_recv()
    for b in range(NB):
        o = dec_s[NX - 1, 0, b]
        for k in range(NSUB):
            lo = b * NSUB * cells + k * cells
            cot_here[lo : lo + cells, :] = landed[o // (NB * NC) % NX, k, b]

    cot = dot(order, cot_here[...])
    gpoint = (cot * hold["point"]).astype(BF)
    gwp = dot(hold["coarse"], gpoint, 0, 0)
    gplaced = dot(gpoint, wp_ref[...], 1, 1).astype(BF)
    gdown = (gplaced.astype(F32) * hold["slope"]).astype(BF)
    gwd = dot(hid_t[...], gdown, 0, 0)
    ghid = dot(gdown, wd_ref[...], 1, 1)
    for r in range(4):
        for ij in range(4):
            a = slice(128 * ij, 128 * ij + 128)
            b = slice(128 * r, 128 * r + 128)
            gpre_t[b, a] = (ghid[b, a] * pre[a, b]).astype(BF).T
    for j in range(8):
        part[14 + j] = gwd[64 * j : 64 * j + 64, :]
    for j in range(4):
        r, t = j % 2, j // 2
        part[22 + j] = gwp[64 * r : 64 * r + 64, 128 * t : 128 * t + 128]
    for tap in range(9):
        total = jnp.zeros((128, 256), F32)
        for t in range(4):
            total += dot(gpre_t[128 * t : 128 * t + 128, :], taps[tap, :, 128 * t : 128 * t + 256])
        sums[tap] = total.T
    low = iota((64, 128), 1) < 64

    def block(m):
        tap, c3 = m // 3, m % 3
        return sums[tap, 64 * c3 : 64 * c3 + 64, :], sums[tap, 64 * c3 + 64 : 64 * c3 + 128, :]

    for j in range(14):
        a0, a1 = block(2 * j)
        even = a0 + pltpu.roll(a1, 64, 1)
        if 2 * j + 1 < 27:
            b0, b1 = block(2 * j + 1)
            odd = pltpu.roll(b0, 64, 1) + b1
        else:
            odd = jnp.zeros_like(even)
        part[j] = jnp.where(low, even, odd)
    for j in range(26, 32):
        part[j] = jnp.zeros((64, 128), F32)

    pieces = 4
    size = np_ // pieces
    firsts = []
    for i in range(pieces):
        tosend[pl.ds(i * size, size)] = part[pl.ds((1 - c) * np_ + i * size, size)].astype(BF)
        at = pl.ds(i * size, size)
        firsts.append(send(tosend.at[at], arrived.at[at], pair_send.at[i], pair_recv.at[i], pair))
    for i in range(pieces):
        firsts[i].wait_recv()
        at = pl.ds(i * size, size)
        plane_out[at] = (part[pl.ds(c * np_ + i * size, size)] + arrived[at].astype(F32)).astype(BF)
    seconds = [
        send(plane_out.at[k], plane_in.at[g], plane_send.at[g], plane_recv.at[g], mate) for mate, k, g in plane
    ]
    total = plane_out[me].astype(F32)
    for g in range(1, np_):
        seconds[g - 1].wait_recv()
        total += plane_in[g].astype(F32)
    depth_out[...] = total.astype(BF)
    thirds = [
        send(depth_out, depth_in.at[z], depth_send.at[g], depth_recv.at[g], mate) for g, mate in enumerate(depth)
    ]
    depth_in[z] = total.astype(BF)
    for copy in thirds:
        copy.wait_recv()
    total = depth_in[0].astype(F32)
    for k in range(1, nz):
        total += depth_in[k].astype(F32)
    mine = full.at[c, me]
    full[c, me] = total.astype(BF)
    backs = [send(mine, mine, back_send.at[g], back_recv.at[g], mate) for mate, k, g in plane]
    shares = [send(mine, mine, share_send.at[0], share_recv.at[0], pair)]
    for g in range(1, np_):
        backs[g - 1].wait_recv()
        yy, xx = (y + ny - g // NX) % ny, (x + NX - g % NX) % NX
        home = full.at[c, yy * NX + xx]
        shares.append(send(home, home, share_send.at[g], share_recv.at[g], pair))
    for copy in shares:
        copy.wait_recv()
    for j in range(14):
        chunk = full[j // np_, j % np_].astype(F32)
        gwc_ref[2 * j] = chunk[:, :64]
        if 2 * j + 1 < 27:
            gwc_ref[2 * j + 1] = pltpu.roll(chunk, 64, 1)[:, :64]
    for j in range(8):
        k = 14 + j
        gwd_ref[64 * j : 64 * j + 64, :] = full[k // np_, k % np_].astype(F32)
    for j in range(4):
        r, t = j % 2, j // 2
        k = 22 + j
        gwp_ref[64 * r : 64 * r + 64, 128 * t : 128 * t + 128] = full[k // np_, k % np_].astype(F32)
    for copy in pending:
        copy.wait_send()


def step(nz, ny, src, cot, owners, near, occ, w, wd, wp):
    slots, cells, wide = cot.shape
    chunk = (slots, cells // NSUB, wide)
    dma = pltpu.SemaphoreType.DMA
    vmem = pl.BlockSpec(memory_space=pltpu.VMEM)
    smem = pl.BlockSpec(memory_space=pltpu.SMEM)
    far = nz // 2
    np_ = ny * NX
    return pl.pallas_call(
        lambda *refs: step_kernel(nz, ny, *refs),
        out_shape=(
            jax.ShapeDtypeStruct((27, 64, 64), F32),
            jax.ShapeDtypeStruct((512, 128), F32),
            jax.ShapeDtypeStruct((128, 256), F32),
        ),
        in_specs=[vmem, vmem, vmem, smem] + [vmem] * 5,
        out_specs=(vmem,) * 3,
        scratch_shapes=[
            pltpu.VMEM((576, 640), BF),
            pltpu.VMEM((2, 32, 640), BF),
            *[pltpu.VMEM((NC, nz) + chunk, BF)] * NSUB,
            pltpu.VMEM((NX - 1, NSUB) + chunk, BF),
            pltpu.VMEM((NX, NSUB) + chunk, BF),
            pltpu.VMEM((NX - 1,) + owners.shape, jnp.int32),
            pltpu.SMEM((NX,) + owners.shape, jnp.int32),
            pltpu.VMEM((9, 512, 640), BF),
            pltpu.VMEM((512, 512), F32),
            pltpu.VMEM((512, 512), F32),
            pltpu.VMEM((512, 512), BF),
            pltpu.VMEM((512, 512), BF),
            pltpu.VMEM((9, 256, 128), F32),
            pltpu.VMEM((2 * np_, 64, 128), F32),
            pltpu.VMEM((slots * cells, wide), BF),
            pltpu.VMEM((np_, 64, 128), BF),
            pltpu.VMEM((np_, 64, 128), BF),
            pltpu.VMEM((np_, 64, 128), BF),
            pltpu.VMEM((np_, 64, 128), BF),
            pltpu.VMEM((64, 128), BF),
            pltpu.VMEM((nz, 64, 128), BF),
            pltpu.VMEM((NC, np_, 64, 128), BF),
            dma((2,)), dma((2,)), dma((NX - 1,)), dma((NX - 1,)), dma((NX,)),
            dma((far, NSUB)), dma((far, NSUB)), dma((far, NSUB)), dma((far, NSUB)),
            dma((nz, NSUB)), dma((nz, NSUB)), dma((NX - 1, NSUB)), dma((NX - 1, NSUB)),
            dma((4,)), dma((4,)), dma((np_,)), dma((np_,)), dma((nz,)), dma((nz,)),
            dma((np_,)), dma((np_,)), dma((np_,)), dma((np_,)),
        ],
        compiler_params=pltpu.CompilerParams(collective_id=0, has_side_effects=True),
        name="step",
    )(src, cot, owners, owners, near, occ, w, wd, wp)


def shards(features, occupancy, neighbours, owners, w_conv, w_down, w_point, cotangent):
    nz = lax.axis_size("brick") // (NX * NC)
    ny = lax.axis_size("dp")
    flat = features[0].reshape(8, 8, 8, 512).transpose(1, 0, 2, 3).reshape(512, 512)
    source = jnp.pad(flat, ((0, 0), (64, 64)))
    gwc, gwd, gwp = step(
        nz, ny, source, cotangent[0], owners, neighbours[0], occupancy[0],
        w_conv.reshape(9, 192, 64), w_down.reshape(512, 128), w_point,
    )
    return gwc.reshape(3, 3, 3, 64, 64), gwd.reshape(2, 2, 2, 64, 128), gwp


def solution(mesh):
    in_specs = (
        P("dp", "brick", None, None),
        P("dp", "brick", None),
        P("dp", "brick", None),
        P("dp", "brick"),
        P(),
        P(),
        P(),
        P("dp", "brick", None, None),
    )
    return jax.shard_map(shards, mesh=mesh, in_specs=in_specs, out_specs=(P(), P(), P()), check_vma=False)
```

```python
import jax
import jax.numpy as jnp
import numpy as np
from jax import lax
from jax.experimental import pallas as pl
from jax.experimental.pallas import tpu as pltpu
from jax.sharding import PartitionSpec as P

MESH = pl.DeviceIdType.MESH
NX = 4
NC = 2
NSUB = 4
NB = 8
BF = jnp.bfloat16
F32 = jnp.float32


def where_am_i():
    spot = lax.axis_index("brick")
    return spot // (NX * NC), spot // NC % NX, spot % NC


def brick_at(z, x, c):
    return (z * NX + x) * NC + c


def slope_of(v):
    g = 1.0 / (1.0 + jnp.exp(-v))
    return g * (1.0 + v * (1.0 - g))


def silu_of(v):
    return v / (1.0 + jnp.exp(-v))


def dot(a, b, ca=1, cb=0):
    return lax.dot_general(a, b, (((ca,), (cb,)), ((), ())), preferred_element_type=F32)


RIGHT = ((1, 0), (1, 1), (1, 2), (2, 0), (2, 1), (2, 2), (3, 0), (3, 1), (1, 3), (4, 0), (3, 2), (2, 3), (4, 2), (3, 3))
LEFT = tuple((s, k ^ 1) for s, k in RIGHT)
LAG = 3


def iota(shape, dim):
    return lax.broadcasted_iota(jnp.int32, shape, dim)


def ones_where(mask):
    return jnp.where(mask, 1.0, 0.0).astype(BF)


def brick_rows():
    return ones_where((iota((512, 8), 0) >> 4 & 7) == iota((512, 8), 1))


def tap_targets(near):
    row, tap = iota((512, 1), 0), iota((1, 16), 1)
    n = row >> 4 & 7
    third = (tap * 11) >> 5
    x = ((row >> 2 & 3) * 2 + (row >> 8)) + (third - 1)
    y = ((row & 3) * 2 + (row >> 7 & 1)) + (tap - 3 * third - 1)
    dx, dy = (x + 8) >> 3, (y + 8) >> 3
    px, py = (n >> 2) + dx - 1, (n & 3) + dy - 1
    side = py * 8 + (y & 7)
    spot = side + jnp.where(px < 0, 512, jnp.where(px > 1, 544, (x & 7) * 64 + px * 32))
    linked = ones_where(near >= 0)
    narrow = ones_where(iota((27, 16), 0) == 3 * iota((27, 16), 1) + 1)
    by_row = dot(brick_rows(), dot(linked, narrow).astype(BF))
    code = 3 * dx + dy
    flag = jnp.zeros((512, 16), F32)
    for d in range(9):
        flag = jnp.where(code == d, by_row[:, d : d + 1], flag)
    return jnp.where(flag > 0.5, spot.astype(F32), -1.0)


def occupied_at(occ):
    row, lane = iota((512, 1), 0), iota((1, 512), 1)
    every = dot(brick_rows(), occ.astype(F32).astype(BF))
    mine = ((row >> 2 & 3) * 2 + (row >> 8)) * 8 + (row & 3) * 2 + (row >> 7 & 1)
    own = jnp.where((lane >> 3) == mine, every, 0.0).astype(BF)
    spread = ones_where((row & 7) == (lane >> 6))
    return dot(own, spread)


def step_kernel(
    nz, ny, src_ref, cot_ref, own_v, own_s, near_ref, occ_ref, w_ref, wd_ref, wp_ref,
    gwc_ref, gwd_ref, gwp_ref,
    source, halo_in, pool0, pool1, pool2, pool3, picked, far_in, land0, land1, land2, land3, dec_in, dec_s,
    taps, pre, occ_at, hid_t, gpre_t, sums, part, cot_here, order_at,
    tosend, arrived, plane_out, plane_in, depth_out, depth_in, full,
    halo_send, halo_recv, dec_send, dec_recv, dec_sem,
    right_send, right_recv, left_send, left_recv, mate_send, mate_recv, row_send, row_recv,
    pair_send, pair_recv, plane_send, plane_recv, depth_send, depth_recv,
    back_send, back_recv, share_send, share_recv,
):
    z, x, c = where_am_i()
    y = lax.axis_index("dp")
    spot = lax.axis_index("brick")
    many = nz * NX * NC
    np_ = ny * NX
    me = y * NX + x

    def at(yy, brick):
        return {"dp": yy, "brick": brick}

    right, left = at(y, brick_at((z + 1) % nz, x, c)), at(y, brick_at((z + nz - 1) % nz, x, c))
    pair = at(y, brick_at(z, x, 1 - c))
    row = [at(y, brick_at(z, (x + g) % NX, c)) for g in range(1, NX)]
    ahead, behind = at(y, (spot + 1) % many), at(y, (spot + many - 1) % many)
    plane = []
    for g in range(1, np_):
        yy, xx = (y + g // NX) % ny, (x + g % NX) % NX
        plane.append((at(yy, brick_at(z, xx, c)), yy * NX + xx, g))
    depth = [at(y, brick_at((z + g) % nz, x, c)) for g in range(1, nz)]
    mates_all = [pair, ahead, behind] + [p[0] for p in plane] + depth
    barrier = pltpu.get_barrier_semaphore()
    for mate in mates_all:
        pl.semaphore_signal(barrier, inc=1, device_id=mate, device_id_type=MESH)
    for k in range(NSUB):
        quarter = cot_ref.shape[1] // NSUB
        (pool0, pool1, pool2, pool3)[k][c, z] = cot_ref[:, k * quarter : (k + 1) * quarter, :]
    tgt = tap_targets(near_ref[...])
    pl.semaphore_wait(barrier, len(mates_all))

    lands = [land0, land1, land2, land3]
    pools = [pool0, pool1, pool2, pool3]
    pending = []

    def send(src, dst, ssem, rsem, mate):
        copy = pltpu.make_async_remote_copy(
            src_ref=src, dst_ref=dst, send_sem=ssem, recv_sem=rsem, device_id=mate, device_id_type=MESH
        )
        copy.start()
        pending.append(copy)
        return copy

    rows_src = src_ref.shape[0]
    halo_up = send(src_ref.at[pl.ds(rows_src - 32, 32)], halo_in.at[0], halo_send.at[0], halo_recv.at[0], ahead)
    halo_down = send(src_ref.at[pl.ds(0, 32)], halo_in.at[1], halo_send.at[1], halo_recv.at[1], behind)
    dec_copies = [send(own_v, dec_in.at[g], dec_send.at[g], dec_recv.at[g], row[g]) for g in range(NX - 1)]
    cells = cot_ref.shape[1] // NSUB
    rights, lefts, mates, rows = {}, {}, {}, {}

    def own(k):
        return cot_ref.at[:, pl.ds(k * cells, cells), :]

    def go_right(s, k):
        if s == 1:
            rights[1, k] = send(own(k), pools[k].at[c, z], right_send.at[0, k], right_recv.at[0, k], right)
            return
        rights[s - 1, k].wait_recv()
        home = pools[k].at[c, (z + nz - s + 1) % nz]
        rights[s, k] = send(home, home, right_send.at[s - 1, k], right_recv.at[s - 1, k], right)
        mates[s - 1, k] = send(home, home, mate_send.at[s - 1, k], mate_recv.at[s - 1, k], pair)

    def go_left(s, k):
        if s == 1:
            lefts[1, k] = send(own(k), pools[k].at[c, z], left_send.at[0, k], left_recv.at[0, k], left)
            return
        lefts[s - 1, k].wait_recv()
        home = pools[k].at[c, (z + s - 1) % nz]
        lefts[s, k] = send(home, home, left_send.at[s - 1, k], left_recv.at[s - 1, k], left)
        t = nz - s + 1
        mates[t, k] = send(home, home, mate_send.at[t, k], mate_recv.at[t, k], pair)

    def end_right(s, k):
        rights[s, k].wait_recv()
        home = pools[k].at[c, (z + nz - s) % nz]
        mates[s, k] = send(home, home, mate_send.at[s, k], mate_recv.at[s, k], pair)

    def end_left(s, k):
        lefts[s, k].wait_recv()
        home = pools[k].at[c, (z + s) % nz]
        t = nz - s
        mates[t, k] = send(home, home, mate_send.at[t, k], mate_recv.at[t, k], pair)

    def pick(g, k, b):
        o = dec_s[g, 0, b]
        return pools[k][o // NB % NC, o // (NB * NC * NX), o % NB]

    fars, nears = {}, {}

    def start_rows(k):
        for t in range(nz):
            mates[t, k].wait_recv()
        hop = 1 if k % 2 == 0 else NX - 1
        for b in range(NB):
            picked[0, k, b] = pick(NX - 1 - NX // 2, k, b)
        fars[k] = send(picked.at[0, k], far_in.at[k], row_send.at[0, k], row_recv.at[0, k], row[hop - 1])
        back = NX - hop
        for b in range(NB):
            picked[1, k, b] = pick(NX - 1 - back, k, b)
        nears[k] = send(picked.at[1, k], lands[k].at[2], row_send.at[1, k], row_recv.at[1, k], row[back - 1])
        for b in range(NB):
            lands[k][0, b] = pick(NX - 1, k, b)

    def relay(k):
        fars[k].wait_recv()
        hop = 1 if k % 2 == 0 else NX - 1
        g = NX - 1 - hop
        for b in range(NB):
            mine = dec_s[g, 0, b] // (NB * NC) % NX == x
            picked[2, k, b] = jnp.where(mine, pick(g, k, b).astype(F32), far_in[k, b].astype(F32)).astype(BF)
        rows[k] = send(picked.at[2, k], lands[k].at[1], row_send.at[2, k], row_recv.at[2, k], row[hop - 1])

    def finish(k):
        rows[k].wait_recv()
        nears[k].wait_recv()
        behind_x = (x + NX - 1) % NX if k % 2 == 1 else (x + 1) % NX
        for b in range(NB):
            source_x = dec_s[NX - 1, 0, b] // (NB * NC) % NX
            which = jnp.where(source_x == x, 0, jnp.where(source_x == behind_x, 2, 1))
            lo = b * NSUB * cells + k * cells
            cot_here[lo : lo + cells, :] = lands[k][which, b]

    hold = {}

    def ready():
        for k in range(NSUB):
            mates[0, k] = send(own(k), pools[k].at[c, z], mate_send.at[0, k], mate_recv.at[0, k], pair)

    def asks():
        for g in range(NX - 1):
            dec_copies[g].wait_recv()
        local = [pltpu.make_async_copy(dec_in.at[g], dec_s.at[g], dec_sem.at[g]) for g in range(NX - 1)]
        local.append(pltpu.make_async_copy(own_v, dec_s.at[NX - 1], dec_sem.at[NX - 1]))
        for copy in local:
            copy.start()
        for copy in local:
            copy.wait()

    def halo():
        halo_up.wait_recv()
        halo_down.wait_recv()
        low = iota((1, 128), 1) < 64

        def shifted(lo, block):
            size = block.shape[0]
            last = jnp.zeros((size, 128), F32)
            for t in range(5):
                now = pltpu.roll(block[:, 128 * t : 128 * t + 128].astype(F32), 64, 1) if t < 4 else jnp.zeros((size, 128), F32)
                source[lo : lo + size, 128 * t : 128 * t + 128] = jnp.where(low, last, now).astype(BF)
                last = now

        shifted(0, src_ref[...])
        shifted(512, halo_in[0])
        shifted(544, halo_in[1])

    def tap_step(tap):
        spots = iota((1, 576), 1).astype(F32)
        take = jnp.where(spots == tgt[:, tap : tap + 1], 1.0, 0.0).astype(BF)
        moved = dot(take, source[...]).astype(BF)
        taps[tap] = moved
        w = w_ref[tap]
        low = dot(w, ones_where(iota((64, 128), 0) == iota((64, 128), 1)))
        high = dot(w, ones_where(iota((64, 128), 0) + 64 == iota((64, 128), 1)))
        blank = jnp.zeros((64, 128), F32)
        u = (jnp.concatenate([low, blank], axis=0) + jnp.concatenate([blank, high], axis=0)).astype(BF)
        for t in range(4):
            lanes = slice(128 * t, 128 * t + 128)
            got = dot(moved[:, 128 * t : 128 * t + 256], u)
            pre[:, lanes] = got if tap == 0 else pre[:, lanes] + got

    def hide(ij):
        a = slice(128 * ij, 128 * ij + 128)
        hidden = (silu_of(pre[a, :]) * occ_at[a, :]).astype(BF)
        for r in range(4):
            hid_t[128 * r : 128 * r + 128, a] = hidden[:, 128 * r : 128 * r + 128]

    def coarsen():
        down = dot(hid_t[...], wd_ref[...])
        coarse = silu_of(down).astype(BF)
        hold["slope"] = slope_of(down)
        hold["coarse"] = coarse
        hold["point"] = slope_of(dot(coarse, wp_ref[...]))

    def reslope(ij):
        a = slice(128 * ij, 128 * ij + 128)
        pre[a, :] = occ_at[a, :] * slope_of(pre[a, :])

    def occupy():
        occ_at[...] = occupied_at(occ_ref[...])

    def ordering():
        r = iota((512, 1), 0)
        order_at[...] = ones_where(iota((1, 512), 1) == 4 * (r & 127) + (r >> 7))

    jobs = [asks, halo]
    jobs += [lambda tap=tap: tap_step(tap) for tap in range(9)]
    jobs += [occupy]
    jobs += [lambda ij=ij: hide(ij) for ij in range(4)]
    jobs += [coarsen]
    jobs += [lambda ij=ij: reslope(ij) for ij in range(4)]
    jobs += [ordering]

    def work():
        if jobs:
            jobs.pop(0)()

    ends = {}
    for i, (s, k) in enumerate(RIGHT):
        if (s + 1, k) not in RIGHT:
            ends.setdefault(i + LAG, []).append((end_right, s, k))
    for i, (s, k) in enumerate(LEFT):
        if (s + 1, k) not in LEFT:
            ends.setdefault(i + LAG, []).append((end_left, s, k))
    left_over = {k: 0 for k in range(NSUB)}
    for group in ends.values():
        for _, s, k in group:
            left_over[k] += 1
    done = dict(left_over)
    waiting, relays, finishes = [], [], []
    for i in range(len(RIGHT) + LAG):
        if i < len(RIGHT):
            go_right(*RIGHT[i])
            go_left(*LEFT[i])
        for f, s, k in ends.get(i, []):
            f(s, k)
            done[k] -= 1
            if done[k] == 0:
                waiting.append((i, k))
        if i == 2:
            ready()
        if i >= 3:
            work()
            work()
        while waiting and waiting[0][0] < i:
            k = waiting.pop(0)[1]
            start_rows(k)
            relays.append((i + LAG, k))
        while relays and relays[0][0] <= i:
            k = relays.pop(0)[1]
            relay(k)
            finishes.append(k)
    while waiting:
        k = waiting.pop(0)[1]
        start_rows(k)
        relays.append((0, k))
    for _, k in relays:
        work()
        relay(k)
        finishes.append(k)
    while jobs:
        work()
    for k in finishes:
        finish(k)

    cot = dot(order_at[...], cot_here[...])
    gpoint = (cot * hold["point"]).astype(BF)
    gwp = dot(hold["coarse"], gpoint, 0, 0)
    gplaced = dot(gpoint, wp_ref[...], 1, 1).astype(BF)
    gdown = (gplaced.astype(F32) * hold["slope"]).astype(BF)
    gwd = dot(hid_t[...], gdown, 0, 0)
    ghid = dot(gdown, wd_ref[...], 1, 1)
    for r in range(4):
        for ij in range(4):
            a = slice(128 * ij, 128 * ij + 128)
            b = slice(128 * r, 128 * r + 128)
            gpre_t[b, a] = (ghid[b, a] * pre[a, b]).astype(BF).T
    for j in range(8):
        part[14 + j] = gwd[64 * j : 64 * j + 64, :]
    for j in range(4):
        r, t = j % 2, j // 2
        part[22 + j] = gwp[64 * r : 64 * r + 64, 128 * t : 128 * t + 128]
    for tap in range(9):
        total = jnp.zeros((128, 256), F32)
        for t in range(4):
            total += dot(gpre_t[128 * t : 128 * t + 128, :], taps[tap, :, 128 * t : 128 * t + 256])
        sums[tap] = total.T
    low = iota((64, 128), 1) < 64

    def block(m):
        tap, c3 = m // 3, m % 3
        return sums[tap, 64 * c3 : 64 * c3 + 64, :], sums[tap, 64 * c3 + 64 : 64 * c3 + 128, :]

    for j in range(14):
        a0, a1 = block(2 * j)
        even = a0 + pltpu.roll(a1, 64, 1)
        if 2 * j + 1 < 27:
            b0, b1 = block(2 * j + 1)
            odd = pltpu.roll(b0, 64, 1) + b1
        else:
            odd = jnp.zeros_like(even)
        part[j] = jnp.where(low, even, odd)
    for j in range(26, 32):
        part[j] = jnp.zeros((64, 128), F32)

    pieces = 4
    size = np_ // pieces
    firsts = []
    for i in range(pieces):
        tosend[pl.ds(i * size, size)] = part[pl.ds((1 - c) * np_ + i * size, size)].astype(BF)
        at = pl.ds(i * size, size)
        firsts.append(send(tosend.at[at], arrived.at[at], pair_send.at[i], pair_recv.at[i], pair))
    for i in range(pieces):
        firsts[i].wait_recv()
        at = pl.ds(i * size, size)
        plane_out[at] = (part[pl.ds(c * np_ + i * size, size)] + arrived[at].astype(F32)).astype(BF)
    seconds = [
        send(plane_out.at[k], plane_in.at[g], plane_send.at[g], plane_recv.at[g], mate) for mate, k, g in plane
    ]
    total = plane_out[me].astype(F32)
    for g in range(1, np_):
        seconds[g - 1].wait_recv()
        total += plane_in[g].astype(F32)
    depth_out[...] = total.astype(BF)
    thirds = [
        send(depth_out, depth_in.at[z], depth_send.at[g], depth_recv.at[g], mate) for g, mate in enumerate(depth)
    ]
    depth_in[z] = total.astype(BF)
    for copy in thirds:
        copy.wait_recv()
    total = depth_in[0].astype(F32)
    for k in range(1, nz):
        total += depth_in[k].astype(F32)
    mine = full.at[c, me]
    full[c, me] = total.astype(BF)
    backs = [send(mine, mine, back_send.at[g], back_recv.at[g], mate) for mate, k, g in plane]
    shares = [send(mine, mine, share_send.at[0], share_recv.at[0], pair)]
    for g in range(1, np_):
        backs[g - 1].wait_recv()
        yy, xx = (y + ny - g // NX) % ny, (x + NX - g % NX) % NX
        home = full.at[c, yy * NX + xx]
        shares.append(send(home, home, share_send.at[g], share_recv.at[g], pair))
    for copy in shares:
        copy.wait_recv()
    for j in range(14):
        chunk = full[j // np_, j % np_].astype(F32)
        gwc_ref[2 * j] = chunk[:, :64]
        if 2 * j + 1 < 27:
            gwc_ref[2 * j + 1] = pltpu.roll(chunk, 64, 1)[:, :64]
    for j in range(8):
        k = 14 + j
        gwd_ref[64 * j : 64 * j + 64, :] = full[k // np_, k % np_].astype(F32)
    for j in range(4):
        r, t = j % 2, j // 2
        k = 22 + j
        gwp_ref[64 * r : 64 * r + 64, 128 * t : 128 * t + 128] = full[k // np_, k % np_].astype(F32)
    for copy in pending:
        copy.wait_send()


def step(nz, ny, src, cot, owners, near, occ, w, wd, wp):
    slots, cells, wide = cot.shape
    chunk = (slots, cells // NSUB, wide)
    dma = pltpu.SemaphoreType.DMA
    vmem = pl.BlockSpec(memory_space=pltpu.VMEM)
    smem = pl.BlockSpec(memory_space=pltpu.SMEM)
    far = nz // 2
    np_ = ny * NX
    return pl.pallas_call(
        lambda *refs: step_kernel(nz, ny, *refs),
        out_shape=(
            jax.ShapeDtypeStruct((27, 64, 64), F32),
            jax.ShapeDtypeStruct((512, 128), F32),
            jax.ShapeDtypeStruct((128, 256), F32),
        ),
        in_specs=[vmem, vmem, vmem, smem] + [vmem] * 5,
        out_specs=(vmem,) * 3,
        scratch_shapes=[
            pltpu.VMEM((576, 640), BF),
            pltpu.VMEM((2, 32, 512), BF),
            *[pltpu.VMEM((NC, nz) + chunk, BF)] * NSUB,
            pltpu.VMEM((3, NSUB) + chunk, BF),
            pltpu.VMEM((NSUB,) + chunk, BF),
            *[pltpu.VMEM((3,) + chunk, BF)] * NSUB,
            pltpu.VMEM((NX - 1,) + owners.shape, jnp.int32),
            pltpu.SMEM((NX,) + owners.shape, jnp.int32),
            pltpu.VMEM((9, 512, 640), BF),
            pltpu.VMEM((512, 512), F32),
            pltpu.VMEM((512, 512), F32),
            pltpu.VMEM((512, 512), BF),
            pltpu.VMEM((512, 512), BF),
            pltpu.VMEM((9, 256, 128), F32),
            pltpu.VMEM((2 * np_, 64, 128), F32),
            pltpu.VMEM((slots * cells, wide), BF),
            pltpu.VMEM((512, 512), BF),
            pltpu.VMEM((np_, 64, 128), BF),
            pltpu.VMEM((np_, 64, 128), BF),
            pltpu.VMEM((np_, 64, 128), BF),
            pltpu.VMEM((np_, 64, 128), BF),
            pltpu.VMEM((64, 128), BF),
            pltpu.VMEM((nz, 64, 128), BF),
            pltpu.VMEM((NC, np_, 64, 128), BF),
            dma((2,)), dma((2,)), dma((NX - 1,)), dma((NX - 1,)), dma((NX,)),
            dma((far, NSUB)), dma((far, NSUB)), dma((far, NSUB)), dma((far, NSUB)),
            dma((nz, NSUB)), dma((nz, NSUB)), dma((NX - 1, NSUB)), dma((NX - 1, NSUB)),
            dma((4,)), dma((4,)), dma((np_,)), dma((np_,)), dma((nz,)), dma((nz,)),
            dma((np_,)), dma((np_,)), dma((np_,)), dma((np_,)),
        ],
        compiler_params=pltpu.CompilerParams(collective_id=0, has_side_effects=True),
        name="step",
    )(src, cot, owners, owners, near, occ, w, wd, wp)


def shards(features, occupancy, neighbours, owners, w_conv, w_down, w_point, cotangent):
    nz = lax.axis_size("brick") // (NX * NC)
    ny = lax.axis_size("dp")
    flat = features[0].reshape(8, 8, 8, 512).transpose(1, 0, 2, 3).reshape(512, 512)
    gwc, gwd, gwp = step(
        nz, ny, flat, cotangent[0], owners, neighbours[0], occupancy[0],
        w_conv.reshape(9, 192, 64), w_down.reshape(512, 128), w_point,
    )
    return gwc.reshape(3, 3, 3, 64, 64), gwd.reshape(2, 2, 2, 64, 128), gwp


def solution(mesh):
    in_specs = (
        P("dp", "brick", None, None),
        P("dp", "brick", None),
        P("dp", "brick", None),
        P("dp", "brick"),
        P(),
        P(),
        P(),
        P("dp", "brick", None, None),
    )
    return jax.shard_map(shards, mesh=mesh, in_specs=in_specs, out_specs=(P(), P(), P()), check_vma=False)
```

```python
import jax
import jax.numpy as jnp
import numpy as np
from jax import lax
from jax.experimental import pallas as pl
from jax.experimental.pallas import tpu as pltpu
from jax.sharding import PartitionSpec as P

MESH = pl.DeviceIdType.MESH
NX = 4
NC = 2
NSUB = 4
NB = 8
BF = jnp.bfloat16
F32 = jnp.float32


def where_am_i():
    spot = lax.axis_index("brick")
    return spot // (NX * NC), spot // NC % NX, spot % NC


def brick_at(z, x, c):
    return (z * NX + x) * NC + c


def slope_of(v):
    g = 1.0 / (1.0 + jnp.exp(-v))
    return g * (1.0 + v * (1.0 - g))


def silu_of(v):
    return v / (1.0 + jnp.exp(-v))


def dot(a, b, ca=1, cb=0):
    return lax.dot_general(a, b, (((ca,), (cb,)), ((), ())), preferred_element_type=F32)


RIGHT = ((1, 0), (1, 1), (1, 2), (2, 0), (2, 1), (2, 2), (3, 0), (3, 1), (1, 3), (4, 0), (3, 2), (2, 3), (4, 2), (3, 3))
LEFT = tuple((s, k ^ 1) for s, k in RIGHT)
LAG = 3


def iota(shape, dim):
    return lax.broadcasted_iota(jnp.int32, shape, dim)


def ones_where(mask):
    return jnp.where(mask, 1.0, 0.0).astype(BF)


def brick_rows():
    return ones_where((iota((512, 8), 0) >> 4 & 7) == iota((512, 8), 1))


def tap_targets(near):
    row, tap = iota((512, 1), 0), iota((1, 16), 1)
    n = row >> 4 & 7
    third = (tap * 11) >> 5
    x = ((row >> 2 & 3) * 2 + (row >> 8)) + (third - 1)
    y = ((row & 3) * 2 + (row >> 7 & 1)) + (tap - 3 * third - 1)
    dx, dy = (x + 8) >> 3, (y + 8) >> 3
    px, py = (n >> 2) + dx - 1, (n & 3) + dy - 1
    side = py * 8 + (y & 7)
    spot = side + jnp.where(px < 0, 512, jnp.where(px > 1, 544, (x & 7) * 8 + px * 256 + py * 56))
    linked = ones_where(near >= 0)
    narrow = ones_where(iota((27, 16), 0) == 3 * iota((27, 16), 1) + 1)
    by_row = dot(brick_rows(), dot(linked, narrow).astype(BF))
    code = 3 * dx + dy
    flag = jnp.zeros((512, 16), F32)
    for d in range(9):
        flag = jnp.where(code == d, by_row[:, d : d + 1], flag)
    return jnp.where(flag > 0.5, spot.astype(F32), -1.0)


def occupied_at(occ):
    row, lane = iota((512, 1), 0), iota((1, 512), 1)
    every = dot(brick_rows(), occ.astype(F32).astype(BF))
    mine = ((row >> 2 & 3) * 2 + (row >> 8)) * 8 + (row & 3) * 2 + (row >> 7 & 1)
    own = jnp.where((lane >> 3) == mine, every, 0.0).astype(BF)
    spread = ones_where((row & 7) == (lane >> 6))
    return dot(own, spread)


def step_kernel(
    nz, ny, feat_any, cot_ref, own_v, near_ref, occ_ref, w_any, wd_any, wp_any,
    full_ref,
    feat_ref, w_ref, wd_ref, wp_ref, load_sem, fill_sem, source, halo_out, halo_in, pool0, pool1, pool2, pool3, picked, far_in, land0, land1, land2, land3, dec_in, dec_s,
    taps, pre, occ_at, hid_t, gpre_t, sums, part, cot_here, order_at,
    tosend, arrived, plane_out, plane_in, depth_out, depth_in, full,
    halo_send, halo_recv, dec_send, dec_recv, dec_sem,
    right_send, right_recv, left_send, left_recv, mate_send, mate_recv, row_send, row_recv,
    pair_send, pair_recv, plane_send, plane_recv, depth_send, depth_recv,
    back_send, back_recv, share_send, share_recv,
):
    z, x, c = where_am_i()
    y = lax.axis_index("dp")
    spot = lax.axis_index("brick")
    many = nz * NX * NC
    np_ = ny * NX
    me = y * NX + x

    def at(yy, brick):
        return {"dp": yy, "brick": brick}

    right, left = at(y, brick_at((z + 1) % nz, x, c)), at(y, brick_at((z + nz - 1) % nz, x, c))
    pair = at(y, brick_at(z, x, 1 - c))
    row = [at(y, brick_at(z, (x + g) % NX, c)) for g in range(1, NX)]
    ahead, behind = at(y, (spot + 1) % many), at(y, (spot + many - 1) % many)
    plane = []
    for g in range(1, np_):
        yy, xx = (y + g // NX) % ny, (x + g % NX) % NX
        plane.append((at(yy, brick_at(z, xx, c)), yy * NX + xx, g))
    depth = [at(y, brick_at((z + g) % nz, x, c)) for g in range(1, nz)]
    mates_all = [pair, ahead, behind] + [p[0] for p in plane] + depth
    barrier = pltpu.get_barrier_semaphore()
    for mate in mates_all:
        pl.semaphore_signal(barrier, inc=1, device_id=mate, device_id_type=MESH)
    fills = []
    for k in range(NSUB):
        quarter = cot_ref.shape[1] // NSUB
        home = (pool0, pool1, pool2, pool3)[k].at[c, z]
        fills.append(pltpu.make_async_copy(cot_ref.at[:, pl.ds(k * quarter, quarter), :], home, fill_sem.at[k]))
    pairs_in = ((feat_any, feat_ref), (w_any, w_ref), (wd_any, wd_ref), (wp_any, wp_ref))
    loads = [pltpu.make_async_copy(src, dst, load_sem.at[i]) for i, (src, dst) in enumerate(pairs_in)]
    for copy in fills + loads:
        copy.start()
    tgt = tap_targets(near_ref[...])
    pl.semaphore_wait(barrier, len(mates_all))

    lands = [land0, land1, land2, land3]
    pools = [pool0, pool1, pool2, pool3]
    pending = []

    def send(src, dst, ssem, rsem, mate):
        copy = pltpu.make_async_remote_copy(
            src_ref=src, dst_ref=dst, send_sem=ssem, recv_sem=rsem, device_id=mate, device_id_type=MESH
        )
        copy.start()
        pending.append(copy)
        return copy

    dec_copies = [send(own_v, dec_in.at[g], dec_send.at[g], dec_recv.at[g], row[g]) for g in range(NX - 1)]
    cells = cot_ref.shape[1] // NSUB
    rights, lefts, mates, rows = {}, {}, {}, {}

    def own(k):
        return cot_ref.at[:, pl.ds(k * cells, cells), :]

    def go_right(s, k):
        if s == 1:
            rights[1, k] = send(own(k), pools[k].at[c, z], right_send.at[0, k], right_recv.at[0, k], right)
            return
        rights[s - 1, k].wait_recv()
        home = pools[k].at[c, (z + nz - s + 1) % nz]
        rights[s, k] = send(home, home, right_send.at[s - 1, k], right_recv.at[s - 1, k], right)
        mates[s - 1, k] = send(home, home, mate_send.at[s - 1, k], mate_recv.at[s - 1, k], pair)

    def go_left(s, k):
        if s == 1:
            lefts[1, k] = send(own(k), pools[k].at[c, z], left_send.at[0, k], left_recv.at[0, k], left)
            return
        lefts[s - 1, k].wait_recv()
        home = pools[k].at[c, (z + s - 1) % nz]
        lefts[s, k] = send(home, home, left_send.at[s - 1, k], left_recv.at[s - 1, k], left)
        t = nz - s + 1
        mates[t, k] = send(home, home, mate_send.at[t, k], mate_recv.at[t, k], pair)

    def end_right(s, k):
        rights[s, k].wait_recv()
        home = pools[k].at[c, (z + nz - s) % nz]
        mates[s, k] = send(home, home, mate_send.at[s, k], mate_recv.at[s, k], pair)

    def end_left(s, k):
        lefts[s, k].wait_recv()
        home = pools[k].at[c, (z + s) % nz]
        t = nz - s
        mates[t, k] = send(home, home, mate_send.at[t, k], mate_recv.at[t, k], pair)

    def pick(g, k, b):
        o = dec_s[g, 0, b]
        return pools[k][o // NB % NC, o // (NB * NC * NX), o % NB]

    fars, nears = {}, {}

    def start_rows(k):
        fills[k].wait()
        for t in range(nz):
            mates[t, k].wait_recv()
        hop = 1 if k % 2 == 0 else NX - 1
        for b in range(NB):
            picked[0, k, b] = pick(NX - 1 - NX // 2, k, b)
        fars[k] = send(picked.at[0, k], far_in.at[k], row_send.at[0, k], row_recv.at[0, k], row[hop - 1])
        back = NX - hop
        for b in range(NB):
            picked[1, k, b] = pick(NX - 1 - back, k, b)
        nears[k] = send(picked.at[1, k], lands[k].at[2], row_send.at[1, k], row_recv.at[1, k], row[back - 1])
        for b in range(NB):
            lands[k][0, b] = pick(NX - 1, k, b)

    def relay(k):
        fars[k].wait_recv()
        hop = 1 if k % 2 == 0 else NX - 1
        g = NX - 1 - hop
        for b in range(NB):
            mine = dec_s[g, 0, b] // (NB * NC) % NX == x
            picked[2, k, b] = jnp.where(mine, pick(g, k, b).astype(F32), far_in[k, b].astype(F32)).astype(BF)
        rows[k] = send(picked.at[2, k], lands[k].at[1], row_send.at[2, k], row_recv.at[2, k], row[hop - 1])

    def finish(k):
        rows[k].wait_recv()
        nears[k].wait_recv()
        behind_x = (x + NX - 1) % NX if k % 2 == 1 else (x + 1) % NX
        for b in range(NB):
            source_x = dec_s[NX - 1, 0, b] // (NB * NC) % NX
            which = jnp.where(source_x == x, 0, jnp.where(source_x == behind_x, 2, 1))
            lo = b * NSUB * cells + k * cells
            cot_here[lo : lo + cells, :] = lands[k][which, b]

    hold = {}

    def ready():
        for k in range(NSUB):
            mates[0, k] = send(own(k), pools[k].at[c, z], mate_send.at[0, k], mate_recv.at[0, k], pair)

    def asks():
        for g in range(NX - 1):
            dec_copies[g].wait_recv()
        local = [pltpu.make_async_copy(dec_in.at[g], dec_s.at[g], dec_sem.at[g]) for g in range(NX - 1)]
        local.append(pltpu.make_async_copy(own_v, dec_s.at[NX - 1], dec_sem.at[NX - 1]))
        for copy in local:
            copy.start()
        for copy in local:
            copy.wait()

    def unfold(b):
        if b == 0:
            for copy in loads:
                copy.wait()
        r, q = iota((512, 1), 0), iota((1, 512), 1)
        by_z = ones_where(q == ((r & 63) << 3) + (r >> 6))
        got = dot(by_z, feat_ref[b], 1, 1)
        blank = jnp.zeros((64, 64), F32)
        for t in range(5):
            first = got[128 * t - 64 : 128 * t] if t > 0 else blank
            second = got[128 * t : 128 * t + 64] if t < 4 else blank
            tile = jnp.concatenate([first, second], axis=1).astype(BF)
            source[64 * b : 64 * b + 64, 128 * t : 128 * t + 128] = tile

    halos = []

    def faces():
        r, q = iota((32, 1), 0), iota((1, 512), 1)
        base = ((r >> 3) << 6) + (r & 7)
        for side, start in ((0, 4 * 64 + 56), (1, 0)):
            halo_out[side] = dot(ones_where(q == base + start), source[0:512]).astype(BF)
        halos.append(send(halo_out.at[0], halo_in.at[0], halo_send.at[0], halo_recv.at[0], ahead))
        halos.append(send(halo_out.at[1], halo_in.at[1], halo_send.at[1], halo_recv.at[1], behind))
        source[512:576] = jnp.zeros((64, 640), BF)

    def halo():
        for copy in halos:
            copy.wait_recv()
        source[512:544] = halo_in[0]
        source[544:576] = halo_in[1]

    def tap_step(tap):
        spots = iota((1, 576), 1).astype(F32)
        take = jnp.where(spots == tgt[:, tap : tap + 1], 1.0, 0.0).astype(BF)
        moved = dot(take, source[...]).astype(BF)
        taps[tap] = moved
        w = w_ref[tap]
        low = dot(w, ones_where(iota((64, 128), 0) == iota((64, 128), 1)))
        high = dot(w, ones_where(iota((64, 128), 0) + 64 == iota((64, 128), 1)))
        blank = jnp.zeros((64, 128), F32)
        u = (jnp.concatenate([low, blank], axis=0) + jnp.concatenate([blank, high], axis=0)).astype(BF)
        for t in range(4):
            lanes = slice(128 * t, 128 * t + 128)
            got = dot(moved[:, 128 * t : 128 * t + 256], u)
            pre[:, lanes] = got if tap == 3 else pre[:, lanes] + got

    def hide(ij):
        a = slice(128 * ij, 128 * ij + 128)
        hidden = (silu_of(pre[a, :]) * occ_at[a, :]).astype(BF)
        for r in range(4):
            hid_t[128 * r : 128 * r + 128, a] = hidden[:, 128 * r : 128 * r + 128]

    def coarsen():
        down = dot(hid_t[...], wd_ref[...])
        coarse = silu_of(down).astype(BF)
        hold["slope"] = slope_of(down)
        hold["coarse"] = coarse
        hold["point"] = slope_of(dot(coarse, wp_ref[...]))

    def reslope(ij):
        a = slice(128 * ij, 128 * ij + 128)
        pre[a, :] = occ_at[a, :] * slope_of(pre[a, :])

    def occupy():
        occ_at[...] = occupied_at(occ_ref[...])

    def ordering():
        r = iota((512, 1), 0)
        order_at[...] = ones_where(iota((1, 512), 1) == 4 * (r & 127) + (r >> 7))

    jobs = [lambda b=b: unfold(b) for b in range(8)]
    jobs += [faces, asks, occupy, ordering]
    jobs += [lambda tap=tap: tap_step(tap) for tap in (3, 4, 5)]
    jobs += [halo]
    jobs += [lambda tap=tap: tap_step(tap) for tap in (0, 1, 2, 6, 7, 8)]
    jobs += [lambda ij=ij: hide(ij) for ij in range(4)]
    jobs += [coarsen]
    jobs += [lambda ij=ij: reslope(ij) for ij in range(4)]

    def work():
        if jobs:
            jobs.pop(0)()

    ends = {}
    for i, (s, k) in enumerate(RIGHT):
        if (s + 1, k) not in RIGHT:
            ends.setdefault(i + LAG, []).append((end_right, s, k))
    for i, (s, k) in enumerate(LEFT):
        if (s + 1, k) not in LEFT:
            ends.setdefault(i + LAG, []).append((end_left, s, k))
    left_over = {k: 0 for k in range(NSUB)}
    for group in ends.values():
        for _, s, k in group:
            left_over[k] += 1
    done = dict(left_over)
    waiting, relays, finishes = [], [], []
    for i in range(len(RIGHT) + LAG):
        if i < len(RIGHT):
            go_right(*RIGHT[i])
            go_left(*LEFT[i])
        for f, s, k in ends.get(i, []):
            f(s, k)
            done[k] -= 1
            if done[k] == 0:
                waiting.append((i, k))
        if i == 2:
            ready()
        if i >= 3:
            work()
            work()
        while waiting and waiting[0][0] < i:
            k = waiting.pop(0)[1]
            start_rows(k)
            relays.append((i + LAG, k))
        while relays and relays[0][0] <= i:
            k = relays.pop(0)[1]
            relay(k)
            finishes.append(k)
    while waiting:
        k = waiting.pop(0)[1]
        start_rows(k)
        relays.append((0, k))
    for _, k in relays:
        work()
        relay(k)
        finishes.append(k)
    while jobs:
        work()
    for k in finishes:
        finish(k)

    cot = dot(order_at[...], cot_here[...])
    gpoint = (cot * hold["point"]).astype(BF)
    gwp = dot(hold["coarse"], gpoint, 0, 0)
    gplaced = dot(gpoint, wp_ref[...], 1, 1).astype(BF)
    gdown = (gplaced.astype(F32) * hold["slope"]).astype(BF)
    gwd = dot(hid_t[...], gdown, 0, 0)
    ghid = dot(gdown, wd_ref[...], 1, 1)
    for r in range(4):
        for ij in range(4):
            a = slice(128 * ij, 128 * ij + 128)
            b = slice(128 * r, 128 * r + 128)
            gpre_t[b, a] = (ghid[b, a] * pre[a, b]).astype(BF).T
    for j in range(8):
        part[14 + j] = gwd[64 * j : 64 * j + 64, :]
    for j in range(4):
        r, t = j % 2, j // 2
        part[22 + j] = gwp[64 * r : 64 * r + 64, 128 * t : 128 * t + 128]
    for tap in range(9):
        total = jnp.zeros((128, 256), F32)
        for t in range(4):
            total += dot(gpre_t[128 * t : 128 * t + 128, :], taps[tap, :, 128 * t : 128 * t + 256])
        sums[tap] = total.T
    low = iota((64, 128), 1) < 64

    def block(m):
        tap, c3 = m // 3, m % 3
        return sums[tap, 64 * c3 : 64 * c3 + 64, :], sums[tap, 64 * c3 + 64 : 64 * c3 + 128, :]

    for j in range(14):
        a0, a1 = block(2 * j)
        even = a0 + pltpu.roll(a1, 64, 1)
        if 2 * j + 1 < 27:
            b0, b1 = block(2 * j + 1)
            odd = pltpu.roll(b0, 64, 1) + b1
        else:
            odd = jnp.zeros_like(even)
        part[j] = jnp.where(low, even, odd)
    for j in range(26, 32):
        part[j] = jnp.zeros((64, 128), F32)

    pieces = 4
    size = np_ // pieces
    firsts = []
    for i in range(pieces):
        tosend[pl.ds(i * size, size)] = part[pl.ds((1 - c) * np_ + i * size, size)].astype(BF)
        at = pl.ds(i * size, size)
        firsts.append(send(tosend.at[at], arrived.at[at], pair_send.at[i], pair_recv.at[i], pair))
    for i in range(pieces):
        firsts[i].wait_recv()
        at = pl.ds(i * size, size)
        plane_out[at] = (part[pl.ds(c * np_ + i * size, size)] + arrived[at].astype(F32)).astype(BF)
    seconds = [
        send(plane_out.at[k], plane_in.at[g], plane_send.at[g], plane_recv.at[g], mate) for mate, k, g in plane
    ]
    total = plane_out[me].astype(F32)
    for g in range(1, np_):
        seconds[g - 1].wait_recv()
        total += plane_in[g].astype(F32)
    depth_out[...] = total.astype(BF)
    thirds = [
        send(depth_out, depth_in.at[z], depth_send.at[g], depth_recv.at[g], mate) for g, mate in enumerate(depth)
    ]
    depth_in[z] = total.astype(BF)
    for copy in thirds:
        copy.wait_recv()
    total = depth_in[0].astype(F32)
    for k in range(1, nz):
        total += depth_in[k].astype(F32)
    mine = full.at[c, me]
    full[c, me] = total.astype(BF)
    backs = [send(mine, mine, back_send.at[g], back_recv.at[g], mate) for mate, k, g in plane]
    shares = [send(mine, mine, share_send.at[0], share_recv.at[0], pair)]
    for g in range(1, np_):
        backs[g - 1].wait_recv()
        yy, xx = (y + ny - g // NX) % ny, (x + NX - g % NX) % NX
        home = full.at[c, yy * NX + xx]
        shares.append(send(home, home, share_send.at[g], share_recv.at[g], pair))
    for copy in shares:
        copy.wait_recv()
    full_ref[...] = full[...]
    for copy in pending:
        copy.wait_send()


def unpack_kernel(full_ref, gwc_ref, gwd_ref, gwp_ref):
    np_ = full_ref.shape[1]
    for j in range(14):
        chunk = full_ref[j // np_, j % np_].astype(F32)
        gwc_ref[2 * j] = chunk[:, :64]
        if 2 * j + 1 < 27:
            gwc_ref[2 * j + 1] = pltpu.roll(chunk, 64, 1)[:, :64]
    for j in range(8):
        k = 14 + j
        gwd_ref[64 * j : 64 * j + 64, :] = full_ref[k // np_, k % np_].astype(F32)
    for j in range(4):
        r, t = j % 2, j // 2
        k = 22 + j
        gwp_ref[64 * r : 64 * r + 64, 128 * t : 128 * t + 128] = full_ref[k // np_, k % np_].astype(F32)


def unpack(full):
    vmem = pl.BlockSpec(memory_space=pltpu.VMEM)
    return pl.pallas_call(
        unpack_kernel,
        out_shape=(
            jax.ShapeDtypeStruct((27, 64, 64), F32),
            jax.ShapeDtypeStruct((512, 128), F32),
            jax.ShapeDtypeStruct((128, 256), F32),
        ),
        in_specs=[vmem],
        out_specs=(vmem,) * 3,
        name="unpack",
    )(full)


def step(nz, ny, feat, cot, owners, near, occ, w, wd, wp):
    slots, cells, wide = cot.shape
    chunk = (slots, cells // NSUB, wide)
    dma = pltpu.SemaphoreType.DMA
    vmem = pl.BlockSpec(memory_space=pltpu.VMEM)
    hbm = pl.BlockSpec(memory_space=pl.ANY)
    far = nz // 2
    np_ = ny * NX
    return pl.pallas_call(
        lambda *refs: step_kernel(nz, ny, *refs),
        out_shape=jax.ShapeDtypeStruct((NC, np_, 64, 128), BF),
        in_specs=[hbm, hbm] + [vmem] * 3 + [hbm] * 3,
        out_specs=vmem,
        scratch_shapes=[
            pltpu.VMEM(feat.shape, BF),
            pltpu.VMEM(w.shape, BF),
            pltpu.VMEM(wd.shape, BF),
            pltpu.VMEM(wp.shape, BF),
            dma((4,)), dma((NSUB,)),
            pltpu.VMEM((576, 640), BF),
            pltpu.VMEM((2, 32, 640), BF),
            pltpu.VMEM((2, 32, 640), BF),
            *[pltpu.VMEM((NC, nz) + chunk, BF)] * NSUB,
            pltpu.VMEM((3, NSUB) + chunk, BF),
            pltpu.VMEM((NSUB,) + chunk, BF),
            *[pltpu.VMEM((3,) + chunk, BF)] * NSUB,
            pltpu.VMEM((NX - 1,) + owners.shape, jnp.int32),
            pltpu.SMEM((NX,) + owners.shape, jnp.int32),
            pltpu.VMEM((9, 512, 640), BF),
            pltpu.VMEM((512, 512), F32),
            pltpu.VMEM((512, 512), F32),
            pltpu.VMEM((512, 512), BF),
            pltpu.VMEM((512, 512), BF),
            pltpu.VMEM((9, 256, 128), F32),
            pltpu.VMEM((2 * np_, 64, 128), F32),
            pltpu.VMEM((slots * cells, wide), BF),
            pltpu.VMEM((512, 512), BF),
            pltpu.VMEM((np_, 64, 128), BF),
            pltpu.VMEM((np_, 64, 128), BF),
            pltpu.VMEM((np_, 64, 128), BF),
            pltpu.VMEM((np_, 64, 128), BF),
            pltpu.VMEM((64, 128), BF),
            pltpu.VMEM((nz, 64, 128), BF),
            pltpu.VMEM((NC, np_, 64, 128), BF),
            dma((2,)), dma((2,)), dma((NX - 1,)), dma((NX - 1,)), dma((NX,)),
            dma((far, NSUB)), dma((far, NSUB)), dma((far, NSUB)), dma((far, NSUB)),
            dma((nz, NSUB)), dma((nz, NSUB)), dma((NX - 1, NSUB)), dma((NX - 1, NSUB)),
            dma((4,)), dma((4,)), dma((np_,)), dma((np_,)), dma((nz,)), dma((nz,)),
            dma((np_,)), dma((np_,)), dma((np_,)), dma((np_,)),
        ],
        compiler_params=pltpu.CompilerParams(collective_id=0, has_side_effects=True),
        name="step",
    )(feat, cot, owners, near, occ, w, wd, wp)


def shards(features, occupancy, neighbours, owners, w_conv, w_down, w_point, cotangent):
    nz = lax.axis_size("brick") // (NX * NC)
    ny = lax.axis_size("dp")
    full = step(
        nz, ny, jnp.swapaxes(features[0], 1, 2), cotangent[0], owners, neighbours[0], occupancy[0],
        w_conv.reshape(9, 192, 64), w_down.reshape(512, 128), w_point,
    )
    gwc, gwd, gwp = unpack(full)
    return gwc.reshape(3, 3, 3, 64, 64), gwd.reshape(2, 2, 2, 64, 128), gwp


def solution(mesh):
    in_specs = (
        P("dp", "brick", None, None),
        P("dp", "brick", None),
        P("dp", "brick", None),
        P("dp", "brick"),
        P(),
        P(),
        P(),
        P("dp", "brick", None, None),
    )
    return jax.shard_map(shards, mesh=mesh, in_specs=in_specs, out_specs=(P(), P(), P()), check_vma=False)
```

```python
import jax
import jax.numpy as jnp
import numpy as np
from jax import lax
from jax.experimental import pallas as pl
from jax.experimental.pallas import tpu as pltpu
from jax.sharding import PartitionSpec as P

MESH = pl.DeviceIdType.MESH
NX = 4
NC = 2
NSUB = 4
NB = 8
BF = jnp.bfloat16
F32 = jnp.float32


def where_am_i():
    spot = lax.axis_index("brick")
    return spot // (NX * NC), spot // NC % NX, spot % NC


def brick_at(z, x, c):
    return (z * NX + x) * NC + c


def slope_of(v):
    g = 1.0 / (1.0 + jnp.exp(-v))
    return g * (1.0 + v * (1.0 - g))


def silu_of(v):
    return v / (1.0 + jnp.exp(-v))


def dot(a, b, ca=1, cb=0):
    return lax.dot_general(a, b, (((ca,), (cb,)), ((), ())), preferred_element_type=F32)


RIGHT = ((1, 0), (1, 1), (1, 2), (2, 0), (2, 1), (2, 2), (1, 3), (3, 0), (3, 1), (3, 2), (2, 3), (4, 0), (4, 2), (3, 3))
LEFT = tuple((s, k ^ 1) for s, k in RIGHT)
LAG = 3
EARLY = 6
USED = 13


def iota(shape, dim):
    return lax.broadcasted_iota(jnp.int32, shape, dim)


def ones_where(mask):
    return jnp.where(mask, 1.0, 0.0).astype(BF)


def brick_rows():
    return ones_where((iota((512, 8), 0) >> 4 & 7) == iota((512, 8), 1))


def tap_targets(near):
    row, tap = iota((512, 1), 0), iota((1, 16), 1)
    n = row >> 4 & 7
    third = (tap * 11) >> 5
    x = ((row >> 2 & 3) * 2 + (row >> 8)) + (third - 1)
    y = ((row & 3) * 2 + (row >> 7 & 1)) + (tap - 3 * third - 1)
    dx, dy = (x + 8) >> 3, (y + 8) >> 3
    px, py = (n >> 2) + dx - 1, (n & 3) + dy - 1
    side = py * 8 + (y & 7)
    spot = side + jnp.where(px < 0, 512, jnp.where(px > 1, 544, (x & 7) * 8 + px * 256 + py * 56))
    linked = ones_where(near >= 0)
    narrow = ones_where(iota((27, 16), 0) == 3 * iota((27, 16), 1) + 1)
    by_row = dot(brick_rows(), dot(linked, narrow).astype(BF))
    code = 3 * dx + dy
    flag = jnp.zeros((512, 16), F32)
    for d in range(9):
        flag = jnp.where(code == d, by_row[:, d : d + 1], flag)
    return jnp.where(flag > 0.5, spot.astype(F32), -1.0)


def occupied_at(occ):
    row, lane = iota((512, 1), 0), iota((1, 512), 1)
    every = dot(brick_rows(), occ.astype(F32).astype(BF))
    mine = ((row >> 2 & 3) * 2 + (row >> 8)) * 8 + (row & 3) * 2 + (row >> 7 & 1)
    own = jnp.where((lane >> 3) == mine, every, 0.0).astype(BF)
    spread = ones_where((row & 7) == (lane >> 6))
    return dot(own, spread)


def step_kernel(
    nz, ny, feat_any, cot_ref, own_v, near_ref, occ_ref, w_any, wd_any, wp_any,
    full_ref,
    feat_ref, w_ref, wd_ref, wp_ref, load_sem, fill_sem, source, halo_out, halo_in, pool0, pool1, pool2, pool3, picked, far_in, land0, land1, land2, land3, dec_in, dec_s,
    taps, pre, occ_at, hid_t, gpre_t, sums, part, cot_here, order_at,
    tosend, arrived, plane_out, plane_in, depth_out, depth_in, full,
    halo_send, halo_recv, dec_send, dec_recv, dec_sem,
    right_send, right_recv, left_send, left_recv, mate_send, mate_recv, row_send, row_recv,
    pair_send, pair_recv, plane_send, plane_recv, depth_send, depth_recv,
    back_send, back_recv, share_send, share_recv,
):
    z, x, c = where_am_i()
    y = lax.axis_index("dp")
    spot = lax.axis_index("brick")
    many = nz * NX * NC
    np_ = ny * NX
    me = y * NX + x

    def at(yy, brick):
        return {"dp": yy, "brick": brick}

    right, left = at(y, brick_at((z + 1) % nz, x, c)), at(y, brick_at((z + nz - 1) % nz, x, c))
    pair = at(y, brick_at(z, x, 1 - c))
    row = [at(y, brick_at(z, (x + g) % NX, c)) for g in range(1, NX)]
    ahead, behind = at(y, (spot + 1) % many), at(y, (spot + many - 1) % many)
    plane = []
    for g in range(1, np_):
        yy, xx = (y + g // NX) % ny, (x + g % NX) % NX
        plane.append((at(yy, brick_at(z, xx, c)), yy * NX + xx, g))
    depth = [at(y, brick_at((z + g) % nz, x, c)) for g in range(1, nz)]
    mates_all = [pair, ahead, behind] + [p[0] for p in plane] + depth
    barrier = pltpu.get_barrier_semaphore()
    for mate in mates_all:
        pl.semaphore_signal(barrier, inc=1, device_id=mate, device_id_type=MESH)
    fills = []
    for k in range(NSUB):
        quarter = cot_ref.shape[1] // NSUB
        home = (pool0, pool1, pool2, pool3)[k].at[c, z]
        fills.append(pltpu.make_async_copy(cot_ref.at[:, pl.ds(k * quarter, quarter), :], home, fill_sem.at[k]))
    pairs_in = ((feat_any, feat_ref), (w_any, w_ref), (wd_any, wd_ref), (wp_any, wp_ref))
    loads = [pltpu.make_async_copy(src, dst, load_sem.at[i]) for i, (src, dst) in enumerate(pairs_in)]
    for copy in fills + loads:
        copy.start()
    tgt = tap_targets(near_ref[...])
    pl.semaphore_wait(barrier, len(mates_all))

    lands = [land0, land1, land2, land3]
    pools = [pool0, pool1, pool2, pool3]
    pending = []

    def send(src, dst, ssem, rsem, mate):
        copy = pltpu.make_async_remote_copy(
            src_ref=src, dst_ref=dst, send_sem=ssem, recv_sem=rsem, device_id=mate, device_id_type=MESH
        )
        copy.start()
        pending.append(copy)
        return copy

    dec_copies = [send(own_v, dec_in.at[g], dec_send.at[g], dec_recv.at[g], row[g]) for g in range(NX - 1)]
    cells = cot_ref.shape[1] // NSUB
    rights, lefts, mates, rows = {}, {}, {}, {}

    def own(k):
        return cot_ref.at[:, pl.ds(k * cells, cells), :]

    def go_right(s, k):
        if s == 1:
            rights[1, k] = send(own(k), pools[k].at[c, z], right_send.at[0, k], right_recv.at[0, k], right)
            return
        rights[s - 1, k].wait_recv()
        home = pools[k].at[c, (z + nz - s + 1) % nz]
        rights[s, k] = send(home, home, right_send.at[s - 1, k], right_recv.at[s - 1, k], right)
        mates[s - 1, k] = send(home, home, mate_send.at[s - 1, k], mate_recv.at[s - 1, k], pair)

    def go_left(s, k):
        if s == 1:
            lefts[1, k] = send(own(k), pools[k].at[c, z], left_send.at[0, k], left_recv.at[0, k], left)
            return
        lefts[s - 1, k].wait_recv()
        home = pools[k].at[c, (z + s - 1) % nz]
        lefts[s, k] = send(home, home, left_send.at[s - 1, k], left_recv.at[s - 1, k], left)
        t = nz - s + 1
        mates[t, k] = send(home, home, mate_send.at[t, k], mate_recv.at[t, k], pair)

    def end_right(s, k):
        rights[s, k].wait_recv()
        home = pools[k].at[c, (z + nz - s) % nz]
        mates[s, k] = send(home, home, mate_send.at[s, k], mate_recv.at[s, k], pair)

    def end_left(s, k):
        lefts[s, k].wait_recv()
        home = pools[k].at[c, (z + s) % nz]
        t = nz - s
        mates[t, k] = send(home, home, mate_send.at[t, k], mate_recv.at[t, k], pair)

    def pick(g, k, b):
        o = dec_s[g, 0, b]
        return pools[k][o // NB % NC, o // (NB * NC * NX), o % NB]

    fars, nears = {}, {}

    def start_rows(k):
        fills[k].wait()
        for t in range(nz):
            mates[t, k].wait_recv()
        hop = 1 if k % 2 == 0 else NX - 1
        for b in range(NB):
            picked[0, k, b] = pick(NX - 1 - NX // 2, k, b)
        fars[k] = send(picked.at[0, k], far_in.at[k], row_send.at[0, k], row_recv.at[0, k], row[hop - 1])
        back = NX - hop
        for b in range(NB):
            picked[1, k, b] = pick(NX - 1 - back, k, b)
        nears[k] = send(picked.at[1, k], lands[k].at[2], row_send.at[1, k], row_recv.at[1, k], row[back - 1])
        for b in range(NB):
            lands[k][0, b] = pick(NX - 1, k, b)

    def relay(k):
        fars[k].wait_recv()
        hop = 1 if k % 2 == 0 else NX - 1
        g = NX - 1 - hop
        for b in range(NB):
            mine = dec_s[g, 0, b] // (NB * NC) % NX == x
            picked[2, k, b] = jnp.where(mine, pick(g, k, b).astype(F32), far_in[k, b].astype(F32)).astype(BF)
        rows[k] = send(picked.at[2, k], lands[k].at[1], row_send.at[2, k], row_recv.at[2, k], row[hop - 1])

    def finish(k):
        rows[k].wait_recv()
        nears[k].wait_recv()
        behind_x = (x + NX - 1) % NX if k % 2 == 1 else (x + 1) % NX
        for b in range(NB):
            source_x = dec_s[NX - 1, 0, b] // (NB * NC) % NX
            which = jnp.where(source_x == x, 0, jnp.where(source_x == behind_x, 2, 1))
            lo = b * NSUB * cells + k * cells
            cot_here[lo : lo + cells, :] = lands[k][which, b]

    hold = {}

    def ready():
        for k in range(NSUB):
            mates[0, k] = send(own(k), pools[k].at[c, z], mate_send.at[0, k], mate_recv.at[0, k], pair)

    def asks():
        for g in range(NX - 1):
            dec_copies[g].wait_recv()
        local = [pltpu.make_async_copy(dec_in.at[g], dec_s.at[g], dec_sem.at[g]) for g in range(NX - 1)]
        local.append(pltpu.make_async_copy(own_v, dec_s.at[NX - 1], dec_sem.at[NX - 1]))
        for copy in local:
            copy.start()
        for copy in local:
            copy.wait()

    def unfold(b):
        if b == 0:
            for copy in loads:
                copy.wait()
        r, q = iota((512, 1), 0), iota((1, 512), 1)
        by_z = ones_where(q == ((r & 63) << 3) + (r >> 6))
        got = dot(by_z, feat_ref[b], 1, 1)
        blank = jnp.zeros((64, 64), F32)
        for t in range(5):
            first = got[128 * t - 64 : 128 * t] if t > 0 else blank
            second = got[128 * t : 128 * t + 64] if t < 4 else blank
            tile = jnp.concatenate([first, second], axis=1).astype(BF)
            source[64 * b : 64 * b + 64, 128 * t : 128 * t + 128] = tile

    halos = []

    def faces():
        r, q = iota((32, 1), 0), iota((1, 512), 1)
        base = ((r >> 3) << 6) + (r & 7)
        for side, start in ((0, 4 * 64 + 56), (1, 0)):
            halo_out[side] = dot(ones_where(q == base + start), source[0:512]).astype(BF)
        halos.append(send(halo_out.at[0], halo_in.at[0], halo_send.at[0], halo_recv.at[0], ahead))
        halos.append(send(halo_out.at[1], halo_in.at[1], halo_send.at[1], halo_recv.at[1], behind))
        source[512:576] = jnp.zeros((64, 640), BF)

    def halo():
        for copy in halos:
            copy.wait_recv()
        source[512:544] = halo_in[0]
        source[544:576] = halo_in[1]

    def tap_step(tap):
        spots = iota((1, 576), 1).astype(F32)
        take = jnp.where(spots == tgt[:, tap : tap + 1], 1.0, 0.0).astype(BF)
        moved = dot(take, source[...]).astype(BF)
        taps[tap] = moved
        w = w_ref[tap]
        low = dot(w, ones_where(iota((64, 128), 0) == iota((64, 128), 1)))
        high = dot(w, ones_where(iota((64, 128), 0) + 64 == iota((64, 128), 1)))
        blank = jnp.zeros((64, 128), F32)
        u = (jnp.concatenate([low, blank], axis=0) + jnp.concatenate([blank, high], axis=0)).astype(BF)
        for t in range(4):
            lanes = slice(128 * t, 128 * t + 128)
            got = dot(moved[:, 128 * t : 128 * t + 256], u)
            pre[:, lanes] = got if tap == 3 else pre[:, lanes] + got

    def hide(ij):
        a = slice(128 * ij, 128 * ij + 128)
        hidden = (silu_of(pre[a, :]) * occ_at[a, :]).astype(BF)
        for r in range(4):
            hid_t[128 * r : 128 * r + 128, a] = hidden[:, 128 * r : 128 * r + 128]

    def coarsen():
        down = dot(hid_t[...], wd_ref[...])
        coarse = silu_of(down).astype(BF)
        hold["slope"] = slope_of(down)
        hold["coarse"] = coarse
        hold["point"] = slope_of(dot(coarse, wp_ref[...]))

    def reslope(ij):
        a = slice(128 * ij, 128 * ij + 128)
        pre[a, :] = occ_at[a, :] * slope_of(pre[a, :])

    def occupy():
        occ_at[...] = occupied_at(occ_ref[...])

    def ordering():
        r = iota((512, 1), 0)
        order_at[...] = ones_where(iota((1, 512), 1) == 4 * (r & 127) + (r >> 7))

    jobs = [lambda b=b: unfold(b) for b in range(8)]
    jobs += [faces, asks, occupy, ordering]
    jobs += [lambda tap=tap: tap_step(tap) for tap in (3, 4, 5)]
    jobs += [halo]
    jobs += [lambda tap=tap: tap_step(tap) for tap in (0, 1, 2, 6, 7, 8)]
    jobs += [lambda ij=ij: hide(ij) for ij in range(4)]
    jobs += [coarsen]
    jobs += [lambda ij=ij: reslope(ij) for ij in range(4)]

    def work():
        if jobs:
            jobs.pop(0)()

    ends = {}
    for i, (s, k) in enumerate(RIGHT):
        if (s + 1, k) not in RIGHT:
            ends.setdefault(i + LAG, []).append((end_right, s, k))
    for i, (s, k) in enumerate(LEFT):
        if (s + 1, k) not in LEFT:
            ends.setdefault(i + LAG, []).append((end_left, s, k))
    left_over = {k: 0 for k in range(NSUB)}
    for group in ends.values():
        for _, s, k in group:
            left_over[k] += 1
    done = dict(left_over)
    waiting, relays, finishes = [], [], []
    for i in range(len(RIGHT) + LAG):
        if i < len(RIGHT):
            go_right(*RIGHT[i])
            go_left(*LEFT[i])
        for f, s, k in ends.get(i, []):
            f(s, k)
            done[k] -= 1
            if done[k] == 0:
                waiting.append((i, k))
        if i == 2:
            ready()
        if i >= 3:
            work()
            work()
        while waiting and waiting[0][0] < i:
            k = waiting.pop(0)[1]
            start_rows(k)
            relays.append((i + LAG, k))
        while relays and relays[0][0] <= i:
            k = relays.pop(0)[1]
            relay(k)
            finishes.append(k)
    while waiting:
        k = waiting.pop(0)[1]
        start_rows(k)
        relays.append((0, k))
    for _, k in relays:
        work()
        relay(k)
        finishes.append(k)
    while jobs:
        work()
    for k in finishes:
        finish(k)

    cot = dot(order_at[...], cot_here[...])
    gpoint = (cot * hold["point"]).astype(BF)
    gwp = dot(hold["coarse"], gpoint, 0, 0)
    gplaced = dot(gpoint, wp_ref[...], 1, 1).astype(BF)
    gdown = (gplaced.astype(F32) * hold["slope"]).astype(BF)
    gwd = dot(hid_t[...], gdown, 0, 0)
    ghid = dot(gdown, wd_ref[...], 1, 1)
    for r in range(4):
        for ij in range(4):
            a = slice(128 * ij, 128 * ij + 128)
            b = slice(128 * r, 128 * r + 128)
            gpre_t[b, a] = (ghid[b, a] * pre[a, b]).astype(BF).T
    for e in range(12):
        if e < 8:
            piece = gwd[64 * e : 64 * e + 64, :]
        else:
            r, t = e % 2, (e - 8) // 2
            piece = gwp[64 * r : 64 * r + 64, 128 * t : 128 * t + 128]
        part[e // EARLY * np_ + e % EARLY] = piece

    firsts = []

    def share_part(lo, n):
        i = len(firsts)
        at_ = pl.ds(lo, n)
        tosend[at_] = part[pl.ds((1 - c) * np_ + lo, n)].astype(BF)
        firsts.append(send(tosend.at[at_], arrived.at[at_], pair_send.at[i], pair_recv.at[i], pair))

    def add_part(i, lo, n):
        firsts[i].wait_recv()
        at_ = pl.ds(lo, n)
        plane_out[at_] = (part[pl.ds(c * np_ + lo, n)] + arrived[at_].astype(F32)).astype(BF)

    def later(src, dst, ssem, rsem, mate):
        return pltpu.make_async_remote_copy(
            src_ref=src, dst_ref=dst, send_sem=ssem, recv_sem=rsem, device_id=mate, device_id_type=MESH
        )

    seconds = [
        later(plane_out.at[k], plane_in.at[g], plane_send.at[g], plane_recv.at[g], mate) for mate, k, g in plane
    ]

    def start_plane(lo, hi):
        for (_, k, g), copy in zip(plane, seconds):
            pl.when((k >= lo) & (k < hi))(copy.start)

    share_part(0, EARLY)
    for tap in range(9):
        if tap == 4:
            add_part(0, 0, EARLY)
            start_plane(0, EARLY)
        total = jnp.zeros((128, 256), F32)
        for t in range(4):
            total += dot(gpre_t[128 * t : 128 * t + 128, :], taps[tap, :, 128 * t : 128 * t + 256])
        sums[tap] = total.T
    low = iota((64, 128), 1) < 64

    def block(m):
        tap, c3 = m // 3, m % 3
        return sums[tap, 64 * c3 : 64 * c3 + 64, :], sums[tap, 64 * c3 + 64 : 64 * c3 + 128, :]

    for j in range(14):
        a0, a1 = block(2 * j)
        even = a0 + pltpu.roll(a1, 64, 1)
        if 2 * j + 1 < 27:
            b0, b1 = block(2 * j + 1)
            odd = pltpu.roll(b0, 64, 1) + b1
        else:
            odd = jnp.zeros_like(even)
        part[j // 7 * np_ + EARLY + j % 7] = jnp.where(low, even, odd)
    share_part(EARLY, 4)
    share_part(EARLY + 4, USED - EARLY - 4)
    add_part(1, EARLY, 4)
    start_plane(EARLY, EARLY + 4)
    add_part(2, EARLY + 4, USED - EARLY - 4)
    start_plane(EARLY + 4, USED)

    mine = full.at[c, me]
    thirds = [
        later(depth_out, depth_in.at[z], depth_send.at[g], depth_recv.at[g], mate) for g, mate in enumerate(depth)
    ]
    backs = [later(mine, mine, back_send.at[g], back_recv.at[g], mate) for mate, k, g in plane]
    first_share = later(mine, mine, share_send.at[0], share_recv.at[0], pair)

    @pl.when(me < USED)
    def _():
        total = plane_out[me].astype(F32)
        for g in range(1, np_):
            seconds[g - 1].wait_recv()
            total += plane_in[g].astype(F32)
        depth_out[...] = total.astype(BF)
        for copy in thirds:
            copy.start()
        depth_in[z] = total.astype(BF)
        for copy in thirds:
            copy.wait_recv()
        total = depth_in[0].astype(F32)
        for k in range(1, nz):
            total += depth_in[k].astype(F32)
        full[c, me] = total.astype(BF)
        for copy in backs:
            copy.start()
        first_share.start()

    shares = []
    for g in range(1, np_):
        k = (y + ny - g // NX) % ny * NX + (x + NX - g % NX) % NX
        home = full.at[c, k]
        share = later(home, home, share_send.at[g], share_recv.at[g], pair)
        shares.append((k, share))

        @pl.when(k < USED)
        def _(g=g, share=share):
            backs[g - 1].wait_recv()
            share.start()

    for k, share in [(me, first_share)] + shares:
        pl.when(k < USED)(share.wait)
    full_ref[...] = full[:, :USED]

    @pl.when(me < USED)
    def _():
        for copy in thirds + backs:
            copy.wait_send()

    for (_, k, g), copy in zip(plane, seconds):
        pl.when(k < USED)(copy.wait_send)
    for copy in pending:
        copy.wait_send()


def unpack_kernel(full_ref, gwc_ref, gwd_ref, gwp_ref):
    for j in range(14):
        chunk = full_ref[j // 7, EARLY + j % 7].astype(F32)
        gwc_ref[2 * j] = chunk[:, :64]
        if 2 * j + 1 < 27:
            gwc_ref[2 * j + 1] = pltpu.roll(chunk, 64, 1)[:, :64]
    for e in range(12):
        chunk = full_ref[e // EARLY, e % EARLY].astype(F32)
        if e < 8:
            gwd_ref[64 * e : 64 * e + 64, :] = chunk
        else:
            r, t = e % 2, (e - 8) // 2
            gwp_ref[64 * r : 64 * r + 64, 128 * t : 128 * t + 128] = chunk


def unpack(full):
    vmem = pl.BlockSpec(memory_space=pltpu.VMEM)
    return pl.pallas_call(
        unpack_kernel,
        out_shape=(
            jax.ShapeDtypeStruct((27, 64, 64), F32),
            jax.ShapeDtypeStruct((512, 128), F32),
            jax.ShapeDtypeStruct((128, 256), F32),
        ),
        in_specs=[vmem],
        out_specs=(vmem,) * 3,
        name="unpack",
    )(full)


def step(nz, ny, feat, cot, owners, near, occ, w, wd, wp):
    slots, cells, wide = cot.shape
    chunk = (slots, cells // NSUB, wide)
    dma = pltpu.SemaphoreType.DMA
    vmem = pl.BlockSpec(memory_space=pltpu.VMEM)
    hbm = pl.BlockSpec(memory_space=pl.ANY)
    far = nz // 2
    np_ = ny * NX
    return pl.pallas_call(
        lambda *refs: step_kernel(nz, ny, *refs),
        out_shape=jax.ShapeDtypeStruct((NC, USED, 64, 128), BF),
        in_specs=[hbm, hbm] + [vmem] * 3 + [hbm] * 3,
        out_specs=vmem,
        scratch_shapes=[
            pltpu.VMEM(feat.shape, BF),
            pltpu.VMEM(w.shape, BF),
            pltpu.VMEM(wd.shape, BF),
            pltpu.VMEM(wp.shape, BF),
            dma((4,)), dma((NSUB,)),
            pltpu.VMEM((576, 640), BF),
            pltpu.VMEM((2, 32, 640), BF),
            pltpu.VMEM((2, 32, 640), BF),
            *[pltpu.VMEM((NC, nz) + chunk, BF)] * NSUB,
            pltpu.VMEM((3, NSUB) + chunk, BF),
            pltpu.VMEM((NSUB,) + chunk, BF),
            *[pltpu.VMEM((3,) + chunk, BF)] * NSUB,
            pltpu.VMEM((NX - 1,) + owners.shape, jnp.int32),
            pltpu.SMEM((NX,) + owners.shape, jnp.int32),
            pltpu.VMEM((9, 512, 640), BF),
            pltpu.VMEM((512, 512), F32),
            pltpu.VMEM((512, 512), F32),
            pltpu.VMEM((512, 512), BF),
            pltpu.VMEM((512, 512), BF),
            pltpu.VMEM((9, 256, 128), F32),
            pltpu.VMEM((2 * np_, 64, 128), F32),
            pltpu.VMEM((slots * cells, wide), BF),
            pltpu.VMEM((512, 512), BF),
            pltpu.VMEM((np_, 64, 128), BF),
            pltpu.VMEM((np_, 64, 128), BF),
            pltpu.VMEM((np_, 64, 128), BF),
            pltpu.VMEM((np_, 64, 128), BF),
            pltpu.VMEM((64, 128), BF),
            pltpu.VMEM((nz, 64, 128), BF),
            pltpu.VMEM((NC, np_, 64, 128), BF),
            dma((2,)), dma((2,)), dma((NX - 1,)), dma((NX - 1,)), dma((NX,)),
            dma((far, NSUB)), dma((far, NSUB)), dma((far, NSUB)), dma((far, NSUB)),
            dma((nz, NSUB)), dma((nz, NSUB)), dma((NX - 1, NSUB)), dma((NX - 1, NSUB)),
            dma((4,)), dma((4,)), dma((np_,)), dma((np_,)), dma((nz,)), dma((nz,)),
            dma((np_,)), dma((np_,)), dma((np_,)), dma((np_,)),
        ],
        compiler_params=pltpu.CompilerParams(collective_id=0, has_side_effects=True),
        name="step",
    )(feat, cot, owners, near, occ, w, wd, wp)


def shards(features, occupancy, neighbours, owners, w_conv, w_down, w_point, cotangent):
    nz = lax.axis_size("brick") // (NX * NC)
    ny = lax.axis_size("dp")
    full = step(
        nz, ny, jnp.swapaxes(features[0], 1, 2), cotangent[0], owners, neighbours[0], occupancy[0],
        w_conv.reshape(9, 192, 64), w_down.reshape(512, 128), w_point,
    )
    gwc, gwd, gwp = unpack(full)
    return gwc.reshape(3, 3, 3, 64, 64), gwd.reshape(2, 2, 2, 64, 128), gwp


def solution(mesh):
    in_specs = (
        P("dp", "brick", None, None),
        P("dp", "brick", None),
        P("dp", "brick", None),
        P("dp", "brick"),
        P(),
        P(),
        P(),
        P("dp", "brick", None, None),
    )
    return jax.shard_map(shards, mesh=mesh, in_specs=in_specs, out_specs=(P(), P(), P()), check_vma=False)
```

```python
import jax
import jax.numpy as jnp
import numpy as np
from jax import lax
from jax.experimental import pallas as pl
from jax.experimental.pallas import tpu as pltpu
from jax.sharding import PartitionSpec as P

MESH = pl.DeviceIdType.MESH
NX = 4
NC = 2
NSUB = 4
NB = 8
BF = jnp.bfloat16
F32 = jnp.float32


def where_am_i():
    spot = lax.axis_index("brick")
    return spot // (NX * NC), spot // NC % NX, spot % NC


def brick_at(z, x, c):
    return (z * NX + x) * NC + c


def slope_of(v):
    g = 1.0 / (1.0 + jnp.exp(-v))
    return g * (1.0 + v * (1.0 - g))


def silu_of(v):
    return v / (1.0 + jnp.exp(-v))


def dot(a, b, ca=1, cb=0):
    return lax.dot_general(a, b, (((ca,), (cb,)), ((), ())), preferred_element_type=F32)


RIGHT = ((1, 0), (1, 1), (1, 2), (2, 0), (2, 1), (2, 2), (1, 3), (3, 0), (3, 1), (3, 2), (2, 3), (4, 0), (4, 2), (3, 3))
LEFT = tuple((s, k ^ 1) for s, k in RIGHT)
LAG = 3
EARLY = 6
USED = 13


def iota(shape, dim):
    return lax.broadcasted_iota(jnp.int32, shape, dim)


def ones_where(mask):
    return jnp.where(mask, 1.0, 0.0).astype(BF)


def brick_rows():
    return ones_where((iota((512, 8), 0) >> 4 & 7) == iota((512, 8), 1))


def tap_targets(near):
    row, tap = iota((512, 1), 0), iota((1, 16), 1)
    n = row >> 4 & 7
    third = (tap * 11) >> 5
    x = ((row >> 2 & 3) * 2 + (row >> 8)) + (third - 1)
    y = ((row & 3) * 2 + (row >> 7 & 1)) + (tap - 3 * third - 1)
    dx, dy = (x + 8) >> 3, (y + 8) >> 3
    px, py = (n >> 2) + dx - 1, (n & 3) + dy - 1
    side = py * 8 + (y & 7)
    spot = side + jnp.where(px < 0, 512, jnp.where(px > 1, 544, (x & 7) * 8 + px * 256 + py * 56))
    linked = ones_where(near >= 0)
    narrow = ones_where(iota((27, 16), 0) == 3 * iota((27, 16), 1) + 1)
    by_row = dot(brick_rows(), dot(linked, narrow).astype(BF))
    code = 3 * dx + dy
    flag = jnp.zeros((512, 16), F32)
    for d in range(9):
        flag = jnp.where(code == d, by_row[:, d : d + 1], flag)
    return jnp.where(flag > 0.5, spot.astype(F32), -1.0)


def occupied_at(occ):
    row, lane = iota((512, 1), 0), iota((1, 512), 1)
    every = dot(brick_rows(), occ.astype(F32).astype(BF))
    mine = ((row >> 2 & 3) * 2 + (row >> 8)) * 8 + (row & 3) * 2 + (row >> 7 & 1)
    own = jnp.where((lane >> 3) == mine, every, 0.0).astype(BF)
    spread = ones_where((row & 7) == (lane >> 6))
    return dot(own, spread)


def step_kernel(
    nz, ny, feat_any, cot_ref, own_v, near_ref, occ_ref, w_any, wd_any, wp_any,
    full_ref,
    feat_ref, w_ref, wd_ref, wp_ref, load_sem, fill_sem, source, halo_out, halo_in, pool0, pool1, pool2, pool3, picked, far_in, land0, land1, land2, land3, dec_in, dec_s,
    taps, pre, occ_at, hid_t, gpre_t, sums, part, cot_here, order_at,
    tosend, arrived, plane_out, plane_in, depth_out, depth_in, full,
    halo_send, halo_recv, dec_send, dec_recv, dec_sem,
    right_send, right_recv, left_send, left_recv, mate_send, mate_recv, row_send, row_recv,
    pair_send, pair_recv, plane_send, plane_recv, depth_send, depth_recv,
    back_send, back_recv, share_send, share_recv,
):
    z, x, c = where_am_i()
    y = lax.axis_index("dp")
    spot = lax.axis_index("brick")
    many = nz * NX * NC
    np_ = ny * NX
    me = y * NX + x

    def at(yy, brick):
        return {"dp": yy, "brick": brick}

    right, left = at(y, brick_at((z + 1) % nz, x, c)), at(y, brick_at((z + nz - 1) % nz, x, c))
    pair = at(y, brick_at(z, x, 1 - c))
    row = [at(y, brick_at(z, (x + g) % NX, c)) for g in range(1, NX)]
    ahead, behind = at(y, (spot + 1) % many), at(y, (spot + many - 1) % many)
    plane = []
    for g in range(1, np_):
        yy, xx = (y + g // NX) % ny, (x + g % NX) % NX
        plane.append((at(yy, brick_at(z, xx, c)), yy * NX + xx, g))
    depth = [at(y, brick_at((z + g) % nz, x, c)) for g in range(1, nz)]
    mates_all = [pair, ahead, behind] + [p[0] for p in plane] + depth
    barrier = pltpu.get_barrier_semaphore()
    for mate in mates_all:
        pl.semaphore_signal(barrier, inc=1, device_id=mate, device_id_type=MESH)
    fills = []
    for k in range(NSUB):
        quarter = cot_ref.shape[1] // NSUB
        home = (pool0, pool1, pool2, pool3)[k].at[c, z]
        fills.append(pltpu.make_async_copy(cot_ref.at[:, pl.ds(k * quarter, quarter), :], home, fill_sem.at[k]))
    pairs_in = ((feat_any, feat_ref), (w_any, w_ref), (wd_any, wd_ref), (wp_any, wp_ref))
    loads = [pltpu.make_async_copy(src, dst, load_sem.at[i]) for i, (src, dst) in enumerate(pairs_in)]
    for copy in fills + loads:
        copy.start()
    tgt = tap_targets(near_ref[...])
    pl.semaphore_wait(barrier, len(mates_all))

    lands = [land0, land1, land2, land3]
    pools = [pool0, pool1, pool2, pool3]
    pending = []

    def send(src, dst, ssem, rsem, mate):
        copy = pltpu.make_async_remote_copy(
            src_ref=src, dst_ref=dst, send_sem=ssem, recv_sem=rsem, device_id=mate, device_id_type=MESH
        )
        copy.start()
        pending.append(copy)
        return copy

    dec_copies = [send(own_v, dec_in.at[g], dec_send.at[g], dec_recv.at[g], row[g]) for g in range(NX - 1)]
    cells = cot_ref.shape[1] // NSUB
    rights, lefts, mates, rows = {}, {}, {}, {}

    def own(k):
        return cot_ref.at[:, pl.ds(k * cells, cells), :]

    def go_right(s, k):
        if s == 1:
            rights[1, k] = send(own(k), pools[k].at[c, z], right_send.at[0, k], right_recv.at[0, k], right)
            return
        rights[s - 1, k].wait_recv()
        home = pools[k].at[c, (z + nz - s + 1) % nz]
        rights[s, k] = send(home, home, right_send.at[s - 1, k], right_recv.at[s - 1, k], right)
        mates[s - 1, k] = send(home, home, mate_send.at[s - 1, k], mate_recv.at[s - 1, k], pair)

    def go_left(s, k):
        if s == 1:
            lefts[1, k] = send(own(k), pools[k].at[c, z], left_send.at[0, k], left_recv.at[0, k], left)
            return
        lefts[s - 1, k].wait_recv()
        home = pools[k].at[c, (z + s - 1) % nz]
        lefts[s, k] = send(home, home, left_send.at[s - 1, k], left_recv.at[s - 1, k], left)
        t = nz - s + 1
        mates[t, k] = send(home, home, mate_send.at[t, k], mate_recv.at[t, k], pair)

    def end_right(s, k):
        rights[s, k].wait_recv()
        home = pools[k].at[c, (z + nz - s) % nz]
        mates[s, k] = send(home, home, mate_send.at[s, k], mate_recv.at[s, k], pair)

    def end_left(s, k):
        lefts[s, k].wait_recv()
        home = pools[k].at[c, (z + s) % nz]
        t = nz - s
        mates[t, k] = send(home, home, mate_send.at[t, k], mate_recv.at[t, k], pair)

    def pick(g, k, b):
        o = dec_s[g, 0, b]
        return pools[k][o // NB % NC, o // (NB * NC * NX), o % NB]

    fars, nears = {}, {}

    def start_rows(k):
        fills[k].wait()
        for t in range(nz):
            mates[t, k].wait_recv()
        hop = 1 if k % 2 == 0 else NX - 1
        for b in range(NB):
            picked[0, k, b] = pick(NX - 1 - NX // 2, k, b)
        fars[k] = send(picked.at[0, k], far_in.at[k], row_send.at[0, k], row_recv.at[0, k], row[hop - 1])
        back = NX - hop
        for b in range(NB):
            picked[1, k, b] = pick(NX - 1 - back, k, b)
        nears[k] = send(picked.at[1, k], lands[k].at[2], row_send.at[1, k], row_recv.at[1, k], row[back - 1])
        for b in range(NB):
            lands[k][0, b] = pick(NX - 1, k, b)

    def relay(k):
        fars[k].wait_recv()
        hop = 1 if k % 2 == 0 else NX - 1
        g = NX - 1 - hop
        for b in range(NB):
            mine = dec_s[g, 0, b] // (NB * NC) % NX == x
            picked[2, k, b] = jnp.where(mine, pick(g, k, b).astype(F32), far_in[k, b].astype(F32)).astype(BF)
        rows[k] = send(picked.at[2, k], lands[k].at[1], row_send.at[2, k], row_recv.at[2, k], row[hop - 1])

    def finish(k):
        rows[k].wait_recv()
        nears[k].wait_recv()
        behind_x = (x + NX - 1) % NX if k % 2 == 1 else (x + 1) % NX
        for b in range(NB):
            source_x = dec_s[NX - 1, 0, b] // (NB * NC) % NX
            which = jnp.where(source_x == x, 0, jnp.where(source_x == behind_x, 2, 1))
            lo = b * NSUB * cells + k * cells
            cot_here[lo : lo + cells, :] = lands[k][which, b]

    hold = {}

    def ready():
        for k in range(NSUB):
            mates[0, k] = send(own(k), pools[k].at[c, z], mate_send.at[0, k], mate_recv.at[0, k], pair)

    def asks():
        for g in range(NX - 1):
            dec_copies[g].wait_recv()
        local = [pltpu.make_async_copy(dec_in.at[g], dec_s.at[g], dec_sem.at[g]) for g in range(NX - 1)]
        local.append(pltpu.make_async_copy(own_v, dec_s.at[NX - 1], dec_sem.at[NX - 1]))
        for copy in local:
            copy.start()
        for copy in local:
            copy.wait()

    def unfold(b):
        if b == 0:
            for copy in loads:
                copy.wait()
        r, q = iota((512, 1), 0), iota((1, 512), 1)
        by_z = ones_where(q == ((r & 63) << 3) + (r >> 6))
        got = dot(by_z, feat_ref[b], 1, 1)
        blank = jnp.zeros((64, 64), F32)
        for t in range(5):
            first = got[128 * t - 64 : 128 * t] if t > 0 else blank
            second = got[128 * t : 128 * t + 64] if t < 4 else blank
            tile = jnp.concatenate([first, second], axis=1).astype(BF)
            source[64 * b : 64 * b + 64, 128 * t : 128 * t + 128] = tile

    halos = []

    def faces():
        r, q = iota((32, 1), 0), iota((1, 512), 1)
        base = ((r >> 3) << 6) + (r & 7)
        for side, start in ((0, 4 * 64 + 56), (1, 0)):
            halo_out[side] = dot(ones_where(q == base + start), source[0:512]).astype(BF)
        halos.append(send(halo_out.at[0], halo_in.at[0], halo_send.at[0], halo_recv.at[0], ahead))
        halos.append(send(halo_out.at[1], halo_in.at[1], halo_send.at[1], halo_recv.at[1], behind))
        source[512:576] = jnp.zeros((64, 640), BF)

    def halo():
        for copy in halos:
            copy.wait_recv()
        source[512:544] = halo_in[0]
        source[544:576] = halo_in[1]

    def tap_step(tap):
        spots = iota((1, 576), 1).astype(F32)
        take = jnp.where(spots == tgt[:, tap : tap + 1], 1.0, 0.0).astype(BF)
        moved = dot(take, source[...]).astype(BF)
        taps[tap] = moved
        w = w_ref[tap]
        low = dot(w, ones_where(iota((64, 128), 0) == iota((64, 128), 1)))
        high = dot(w, ones_where(iota((64, 128), 0) + 64 == iota((64, 128), 1)))
        blank = jnp.zeros((64, 128), F32)
        u = (jnp.concatenate([low, blank], axis=0) + jnp.concatenate([blank, high], axis=0)).astype(BF)
        for t in range(4):
            lanes = slice(128 * t, 128 * t + 128)
            got = dot(moved[:, 128 * t : 128 * t + 256], u)
            pre[:, lanes] = got if tap == 3 else pre[:, lanes] + got

    def hide(ij):
        a = slice(128 * ij, 128 * ij + 128)
        hidden = (silu_of(pre[a, :]) * occ_at[a, :]).astype(BF)
        for r in range(4):
            hid_t[128 * r : 128 * r + 128, a] = hidden[:, 128 * r : 128 * r + 128]

    def coarsen():
        down = dot(hid_t[...], wd_ref[...])
        coarse = silu_of(down).astype(BF)
        hold["slope"] = slope_of(down)
        hold["coarse"] = coarse
        hold["point"] = slope_of(dot(coarse, wp_ref[...]))

    def reslope(ij):
        a = slice(128 * ij, 128 * ij + 128)
        pre[a, :] = occ_at[a, :] * slope_of(pre[a, :])

    def occupy():
        occ_at[...] = occupied_at(occ_ref[...])

    def ordering():
        r = iota((512, 1), 0)
        order_at[...] = ones_where(iota((1, 512), 1) == 4 * (r & 127) + (r >> 7))

    jobs = [lambda b=b: unfold(b) for b in range(8)]
    jobs += [faces, asks, occupy, ordering]
    jobs += [lambda tap=tap: tap_step(tap) for tap in (3, 4, 5)]
    jobs += [halo]
    jobs += [lambda tap=tap: tap_step(tap) for tap in (0, 1, 2, 6, 7, 8)]
    jobs += [lambda ij=ij: hide(ij) for ij in range(4)]
    jobs += [coarsen]
    jobs += [lambda ij=ij: reslope(ij) for ij in range(4)]

    def work():
        if jobs:
            jobs.pop(0)()

    ends = {}
    for i, (s, k) in enumerate(RIGHT):
        if (s + 1, k) not in RIGHT:
            ends.setdefault(i + LAG, []).append((end_right, s, k))
    for i, (s, k) in enumerate(LEFT):
        if (s + 1, k) not in LEFT:
            ends.setdefault(i + LAG, []).append((end_left, s, k))
    left_over = {k: 0 for k in range(NSUB)}
    for group in ends.values():
        for _, s, k in group:
            left_over[k] += 1
    done = dict(left_over)
    waiting, relays, finishes = [], [], []
    for i in range(len(RIGHT) + LAG):
        if i < len(RIGHT):
            go_right(*RIGHT[i])
            go_left(*LEFT[i])
        for f, s, k in ends.get(i, []):
            f(s, k)
            done[k] -= 1
            if done[k] == 0:
                waiting.append((i, k))
        if i == 2:
            ready()
        if i >= 2:
            work()
        while waiting and waiting[0][0] < i:
            k = waiting.pop(0)[1]
            start_rows(k)
            relays.append((i + LAG, k))
        while relays and relays[0][0] <= i:
            k = relays.pop(0)[1]
            relay(k)
            finishes.append(k)
    while waiting:
        k = waiting.pop(0)[1]
        start_rows(k)
        relays.append((0, k))
    for _, k in relays:
        work()
        relay(k)
        finishes.append(k)
    while jobs:
        work()
    for k in finishes:
        finish(k)

    cot = dot(order_at[...], cot_here[...])
    gpoint = (cot * hold["point"]).astype(BF)
    gwp = dot(hold["coarse"], gpoint, 0, 0)
    gplaced = dot(gpoint, wp_ref[...], 1, 1).astype(BF)
    gdown = (gplaced.astype(F32) * hold["slope"]).astype(BF)
    gwd = dot(hid_t[...], gdown, 0, 0)
    ghid = dot(gdown, wd_ref[...], 1, 1)
    for r in range(4):
        for ij in range(4):
            a = slice(128 * ij, 128 * ij + 128)
            b = slice(128 * r, 128 * r + 128)
            gpre_t[b, a] = (ghid[b, a] * pre[a, b]).astype(BF).T
    for e in range(12):
        if e < 8:
            piece = gwd[64 * e : 64 * e + 64, :]
        else:
            r, t = e % 2, (e - 8) // 2
            piece = gwp[64 * r : 64 * r + 64, 128 * t : 128 * t + 128]
        part[e // EARLY * np_ + e % EARLY] = piece

    firsts = []

    def share_part(lo, n):
        i = len(firsts)
        at_ = pl.ds(lo, n)
        tosend[at_] = part[pl.ds((1 - c) * np_ + lo, n)].astype(BF)
        firsts.append(send(tosend.at[at_], arrived.at[at_], pair_send.at[i], pair_recv.at[i], pair))

    def add_part(i, lo, n):
        firsts[i].wait_recv()
        at_ = pl.ds(lo, n)
        plane_out[at_] = (part[pl.ds(c * np_ + lo, n)] + arrived[at_].astype(F32)).astype(BF)

    def later(src, dst, ssem, rsem, mate):
        return pltpu.make_async_remote_copy(
            src_ref=src, dst_ref=dst, send_sem=ssem, recv_sem=rsem, device_id=mate, device_id_type=MESH
        )

    seconds = [
        later(plane_out.at[k], plane_in.at[g], plane_send.at[g], plane_recv.at[g], mate) for mate, k, g in plane
    ]

    def start_plane(lo, hi):
        for (_, k, g), copy in zip(plane, seconds):
            pl.when((k >= lo) & (k < hi))(copy.start)

    share_part(0, EARLY)
    for tap in range(9):
        if tap == 4:
            add_part(0, 0, EARLY)
            start_plane(0, EARLY)
        total = jnp.zeros((128, 256), F32)
        for t in range(4):
            total += dot(gpre_t[128 * t : 128 * t + 128, :], taps[tap, :, 128 * t : 128 * t + 256])
        sums[tap] = total.T
    low = iota((64, 128), 1) < 64

    def block(m):
        tap, c3 = m // 3, m % 3
        return sums[tap, 64 * c3 : 64 * c3 + 64, :], sums[tap, 64 * c3 + 64 : 64 * c3 + 128, :]

    for j in range(14):
        a0, a1 = block(2 * j)
        even = a0 + pltpu.roll(a1, 64, 1)
        if 2 * j + 1 < 27:
            b0, b1 = block(2 * j + 1)
            odd = pltpu.roll(b0, 64, 1) + b1
        else:
            odd = jnp.zeros_like(even)
        part[j // 7 * np_ + EARLY + j % 7] = jnp.where(low, even, odd)
    share_part(EARLY, 4)
    share_part(EARLY + 4, USED - EARLY - 4)
    add_part(1, EARLY, 4)
    start_plane(EARLY, EARLY + 4)
    add_part(2, EARLY + 4, USED - EARLY - 4)
    start_plane(EARLY + 4, USED)

    mine = full.at[c, me]
    thirds = [
        later(depth_out, depth_in.at[z], depth_send.at[g], depth_recv.at[g], mate) for g, mate in enumerate(depth)
    ]
    backs = [later(mine, mine, back_send.at[g], back_recv.at[g], mate) for mate, k, g in plane]
    first_share = later(mine, mine, share_send.at[0], share_recv.at[0], pair)

    @pl.when(me < USED)
    def _():
        total = plane_out[me].astype(F32)
        for g in range(1, np_):
            seconds[g - 1].wait_recv()
            total += plane_in[g].astype(F32)
        depth_out[...] = total.astype(BF)
        for copy in thirds:
            copy.start()
        depth_in[z] = total.astype(BF)
        for copy in thirds:
            copy.wait_recv()
        total = depth_in[0].astype(F32)
        for k in range(1, nz):
            total += depth_in[k].astype(F32)
        full[c, me] = total.astype(BF)
        for copy in backs:
            copy.start()
        first_share.start()

    shares = []
    for g in range(1, np_):
        k = (y + ny - g // NX) % ny * NX + (x + NX - g % NX) % NX
        home = full.at[c, k]
        share = later(home, home, share_send.at[g], share_recv.at[g], pair)
        shares.append((k, share))

        @pl.when(k < USED)
        def _(g=g, share=share):
            backs[g - 1].wait_recv()
            share.start()

    for k, share in [(me, first_share)] + shares:
        pl.when(k < USED)(share.wait)
    full_ref[...] = full[:, :USED]

    @pl.when(me < USED)
    def _():
        for copy in thirds + backs:
            copy.wait_send()

    for (_, k, g), copy in zip(plane, seconds):
        pl.when(k < USED)(copy.wait_send)
    for copy in pending:
        copy.wait_send()


def unpack_kernel(full_ref, gwc_ref, gwd_ref, gwp_ref):
    for j in range(14):
        chunk = full_ref[j // 7, EARLY + j % 7].astype(F32)
        gwc_ref[2 * j] = chunk[:, :64]
        if 2 * j + 1 < 27:
            gwc_ref[2 * j + 1] = pltpu.roll(chunk, 64, 1)[:, :64]
    for e in range(12):
        chunk = full_ref[e // EARLY, e % EARLY].astype(F32)
        if e < 8:
            gwd_ref[64 * e : 64 * e + 64, :] = chunk
        else:
            r, t = e % 2, (e - 8) // 2
            gwp_ref[64 * r : 64 * r + 64, 128 * t : 128 * t + 128] = chunk


def unpack(full):
    vmem = pl.BlockSpec(memory_space=pltpu.VMEM)
    return pl.pallas_call(
        unpack_kernel,
        out_shape=(
            jax.ShapeDtypeStruct((27, 64, 64), F32),
            jax.ShapeDtypeStruct((512, 128), F32),
            jax.ShapeDtypeStruct((128, 256), F32),
        ),
        in_specs=[vmem],
        out_specs=(vmem,) * 3,
        name="unpack",
    )(full)


def step(nz, ny, feat, cot, owners, near, occ, w, wd, wp):
    slots, cells, wide = cot.shape
    chunk = (slots, cells // NSUB, wide)
    dma = pltpu.SemaphoreType.DMA
    vmem = pl.BlockSpec(memory_space=pltpu.VMEM)
    hbm = pl.BlockSpec(memory_space=pl.ANY)
    far = nz // 2
    np_ = ny * NX
    return pl.pallas_call(
        lambda *refs: step_kernel(nz, ny, *refs),
        out_shape=jax.ShapeDtypeStruct((NC, USED, 64, 128), BF),
        in_specs=[hbm, hbm] + [vmem] * 3 + [hbm] * 3,
        out_specs=vmem,
        scratch_shapes=[
            pltpu.VMEM(feat.shape, BF),
            pltpu.VMEM(w.shape, BF),
            pltpu.VMEM(wd.shape, BF),
            pltpu.VMEM(wp.shape, BF),
            dma((4,)), dma((NSUB,)),
            pltpu.VMEM((576, 640), BF),
            pltpu.VMEM((2, 32, 640), BF),
            pltpu.VMEM((2, 32, 640), BF),
            *[pltpu.VMEM((NC, nz) + chunk, BF)] * NSUB,
            pltpu.VMEM((3, NSUB) + chunk, BF),
            pltpu.VMEM((NSUB,) + chunk, BF),
            *[pltpu.VMEM((3,) + chunk, BF)] * NSUB,
            pltpu.VMEM((NX - 1,) + owners.shape, jnp.int32),
            pltpu.SMEM((NX,) + owners.shape, jnp.int32),
            pltpu.VMEM((9, 512, 640), BF),
            pltpu.VMEM((512, 512), F32),
            pltpu.VMEM((512, 512), F32),
            pltpu.VMEM((512, 512), BF),
            pltpu.VMEM((512, 512), BF),
            pltpu.VMEM((9, 256, 128), F32),
            pltpu.VMEM((2 * np_, 64, 128), F32),
            pltpu.VMEM((slots * cells, wide), BF),
            pltpu.VMEM((512, 512), BF),
            pltpu.VMEM((np_, 64, 128), BF),
            pltpu.VMEM((np_, 64, 128), BF),
            pltpu.VMEM((np_, 64, 128), BF),
            pltpu.VMEM((np_, 64, 128), BF),
            pltpu.VMEM((64, 128), BF),
            pltpu.VMEM((nz, 64, 128), BF),
            pltpu.VMEM((NC, np_, 64, 128), BF),
            dma((2,)), dma((2,)), dma((NX - 1,)), dma((NX - 1,)), dma((NX,)),
            dma((far, NSUB)), dma((far, NSUB)), dma((far, NSUB)), dma((far, NSUB)),
            dma((nz, NSUB)), dma((nz, NSUB)), dma((NX - 1, NSUB)), dma((NX - 1, NSUB)),
            dma((4,)), dma((4,)), dma((np_,)), dma((np_,)), dma((nz,)), dma((nz,)),
            dma((np_,)), dma((np_,)), dma((np_,)), dma((np_,)),
        ],
        compiler_params=pltpu.CompilerParams(collective_id=0, has_side_effects=True),
        name="step",
    )(feat, cot, owners, near, occ, w, wd, wp)


def shards(features, occupancy, neighbours, owners, w_conv, w_down, w_point, cotangent):
    nz = lax.axis_size("brick") // (NX * NC)
    ny = lax.axis_size("dp")
    full = step(
        nz, ny, jnp.swapaxes(features[0], 1, 2), cotangent[0], owners, neighbours[0], occupancy[0],
        w_conv.reshape(9, 192, 64), w_down.reshape(512, 128), w_point,
    )
    gwc, gwd, gwp = unpack(full)
    return gwc.reshape(3, 3, 3, 64, 64), gwd.reshape(2, 2, 2, 64, 128), gwp


def solution(mesh):
    in_specs = (
        P("dp", "brick", None, None),
        P("dp", "brick", None),
        P("dp", "brick", None),
        P("dp", "brick"),
        P(),
        P(),
        P(),
        P("dp", "brick", None, None),
    )
    return jax.shard_map(shards, mesh=mesh, in_specs=in_specs, out_specs=(P(), P(), P()), check_vma=False)
```

```python
import jax
import jax.numpy as jnp
import numpy as np
from jax import lax
from jax.experimental import pallas as pl
from jax.experimental.pallas import tpu as pltpu
from jax.sharding import PartitionSpec as P

MESH = pl.DeviceIdType.MESH
NX = 4
NC = 2
NSUB = 4
NB = 8
BF = jnp.bfloat16
F32 = jnp.float32


def where_am_i():
    spot = lax.axis_index("brick")
    return spot // (NX * NC), spot // NC % NX, spot % NC


def hops(step, size):
    return min(step, size - step)


def brick_at(z, x, c):
    return (z * NX + x) * NC + c


def slope_of(v):
    g = 1.0 / (1.0 + jnp.exp(-v))
    return g * (1.0 + v * (1.0 - g))


def silu_of(v):
    return v / (1.0 + jnp.exp(-v))


def dot(a, b, ca=1, cb=0):
    return lax.dot_general(a, b, (((ca,), (cb,)), ((), ())), preferred_element_type=F32)


RIGHT = ((1, 0), (1, 1), (1, 2), (2, 0), (2, 1), (2, 2), (1, 3), (3, 0), (3, 1), (3, 2), (2, 3), (4, 0), (4, 2), (3, 3))
LEFT = tuple((s, k ^ 1) for s, k in RIGHT)
LAG = 3
EARLY = 6
USED = 13


def iota(shape, dim):
    return lax.broadcasted_iota(jnp.int32, shape, dim)


def ones_where(mask):
    return jnp.where(mask, 1.0, 0.0).astype(BF)


def brick_rows():
    return ones_where((iota((512, 8), 0) >> 4 & 7) == iota((512, 8), 1))


def tap_targets(near):
    row, tap = iota((512, 1), 0), iota((1, 16), 1)
    n = row >> 4 & 7
    third = (tap * 11) >> 5
    x = ((row >> 2 & 3) * 2 + (row >> 8)) + (third - 1)
    y = ((row & 3) * 2 + (row >> 7 & 1)) + (tap - 3 * third - 1)
    dx, dy = (x + 8) >> 3, (y + 8) >> 3
    px, py = (n >> 2) + dx - 1, (n & 3) + dy - 1
    side = py * 8 + (y & 7)
    spot = side + jnp.where(px < 0, 512, jnp.where(px > 1, 544, (x & 7) * 8 + px * 256 + py * 56))
    linked = ones_where(near >= 0)
    narrow = ones_where(iota((27, 16), 0) == 3 * iota((27, 16), 1) + 1)
    by_row = dot(brick_rows(), dot(linked, narrow).astype(BF))
    code = 3 * dx + dy
    flag = jnp.zeros((512, 16), F32)
    for d in range(9):
        flag = jnp.where(code == d, by_row[:, d : d + 1], flag)
    return jnp.where(flag > 0.5, spot.astype(F32), -1.0)


def occupied_at(occ):
    row, lane = iota((512, 1), 0), iota((1, 512), 1)
    every = dot(brick_rows(), occ.astype(F32).astype(BF))
    mine = ((row >> 2 & 3) * 2 + (row >> 8)) * 8 + (row & 3) * 2 + (row >> 7 & 1)
    own = jnp.where((lane >> 3) == mine, every, 0.0).astype(BF)
    spread = ones_where((row & 7) == (lane >> 6))
    return dot(own, spread)


def step_kernel(
    nz, ny, feat_any, cot_ref, own_v, near_ref, occ_ref, w_any, wd_any, wp_any,
    full_ref,
    feat_ref, w_ref, wd_ref, wp_ref, load_sem, fill_sem, source, halo_out, halo_in, pool0, pool1, pool2, pool3, picked, far_in, land0, land1, land2, land3, dec_in, dec_s,
    taps, pre, occ_at, hid_t, gpre_t, sums, part, cot_here, order_at,
    tosend, arrived, plane_out, plane_in, depth_out, depth_in, full,
    halo_send, halo_recv, dec_send, dec_recv, dec_sem,
    right_send, right_recv, left_send, left_recv, mate_send, mate_recv, row_send, row_recv,
    pair_send, pair_recv, plane_send, plane_recv, depth_send, depth_recv,
    back_send, back_recv, share_send, share_recv,
):
    z, x, c = where_am_i()
    y = lax.axis_index("dp")
    spot = lax.axis_index("brick")
    many = nz * NX * NC
    np_ = ny * NX
    me = y * NX + x

    def at(yy, brick):
        return {"dp": yy, "brick": brick}

    right, left = at(y, brick_at((z + 1) % nz, x, c)), at(y, brick_at((z + nz - 1) % nz, x, c))
    pair = at(y, brick_at(z, x, 1 - c))
    row = [at(y, brick_at(z, (x + g) % NX, c)) for g in range(1, NX)]
    ahead, behind = at(y, (spot + 1) % many), at(y, (spot + many - 1) % many)
    plane = []
    for g in sorted(range(1, np_), key=lambda g: -hops(g // NX, ny) - hops(g % NX, NX)):
        yy, xx = (y + g // NX) % ny, (x + g % NX) % NX
        plane.append((at(yy, brick_at(z, xx, c)), yy * NX + xx, g))
    depth = [at(y, brick_at((z + g) % nz, x, c)) for g in sorted(range(1, nz), key=lambda g: -hops(g, nz))]
    mates_all = [pair, ahead, behind] + [p[0] for p in plane] + depth
    barrier = pltpu.get_barrier_semaphore()
    for mate in mates_all:
        pl.semaphore_signal(barrier, inc=1, device_id=mate, device_id_type=MESH)
    fills = []
    for k in range(NSUB):
        quarter = cot_ref.shape[1] // NSUB
        home = (pool0, pool1, pool2, pool3)[k].at[c, z]
        fills.append(pltpu.make_async_copy(cot_ref.at[:, pl.ds(k * quarter, quarter), :], home, fill_sem.at[k]))
    pairs_in = ((feat_any, feat_ref), (w_any, w_ref), (wd_any, wd_ref), (wp_any, wp_ref))
    loads = [pltpu.make_async_copy(src, dst, load_sem.at[i]) for i, (src, dst) in enumerate(pairs_in)]
    for copy in fills + loads:
        copy.start()
    tgt = tap_targets(near_ref[...])
    pl.semaphore_wait(barrier, len(mates_all))

    lands = [land0, land1, land2, land3]
    pools = [pool0, pool1, pool2, pool3]
    pending = []

    def send(src, dst, ssem, rsem, mate):
        copy = pltpu.make_async_remote_copy(
            src_ref=src, dst_ref=dst, send_sem=ssem, recv_sem=rsem, device_id=mate, device_id_type=MESH
        )
        copy.start()
        pending.append(copy)
        return copy

    dec_copies = [send(own_v, dec_in.at[g], dec_send.at[g], dec_recv.at[g], row[g]) for g in range(NX - 1)]
    cells = cot_ref.shape[1] // NSUB
    rights, lefts, mates, rows = {}, {}, {}, {}

    def own(k):
        return cot_ref.at[:, pl.ds(k * cells, cells), :]

    def go_right(s, k):
        if s == 1:
            rights[1, k] = send(own(k), pools[k].at[c, z], right_send.at[0, k], right_recv.at[0, k], right)
            return
        rights[s - 1, k].wait_recv()
        home = pools[k].at[c, (z + nz - s + 1) % nz]
        rights[s, k] = send(home, home, right_send.at[s - 1, k], right_recv.at[s - 1, k], right)
        mates[s - 1, k] = send(home, home, mate_send.at[s - 1, k], mate_recv.at[s - 1, k], pair)

    def go_left(s, k):
        if s == 1:
            lefts[1, k] = send(own(k), pools[k].at[c, z], left_send.at[0, k], left_recv.at[0, k], left)
            return
        lefts[s - 1, k].wait_recv()
        home = pools[k].at[c, (z + s - 1) % nz]
        lefts[s, k] = send(home, home, left_send.at[s - 1, k], left_recv.at[s - 1, k], left)
        t = nz - s + 1
        mates[t, k] = send(home, home, mate_send.at[t, k], mate_recv.at[t, k], pair)

    def end_right(s, k):
        rights[s, k].wait_recv()
        home = pools[k].at[c, (z + nz - s) % nz]
        mates[s, k] = send(home, home, mate_send.at[s, k], mate_recv.at[s, k], pair)

    def end_left(s, k):
        lefts[s, k].wait_recv()
        home = pools[k].at[c, (z + s) % nz]
        t = nz - s
        mates[t, k] = send(home, home, mate_send.at[t, k], mate_recv.at[t, k], pair)

    def pick(g, k, b):
        o = dec_s[g, 0, b]
        return pools[k][o // NB % NC, o // (NB * NC * NX), o % NB]

    fars, nears = {}, {}

    def start_rows(k):
        fills[k].wait()
        for t in range(nz):
            mates[t, k].wait_recv()
        hop = 1 if k % 2 == 0 else NX - 1
        for b in range(NB):
            picked[0, k, b] = pick(NX - 1 - NX // 2, k, b)
        fars[k] = send(picked.at[0, k], far_in.at[k], row_send.at[0, k], row_recv.at[0, k], row[hop - 1])
        back = NX - hop
        for b in range(NB):
            picked[1, k, b] = pick(NX - 1 - back, k, b)
        nears[k] = send(picked.at[1, k], lands[k].at[2], row_send.at[1, k], row_recv.at[1, k], row[back - 1])
        for b in range(NB):
            lands[k][0, b] = pick(NX - 1, k, b)

    def relay(k):
        fars[k].wait_recv()
        hop = 1 if k % 2 == 0 else NX - 1
        g = NX - 1 - hop
        for b in range(NB):
            mine = dec_s[g, 0, b] // (NB * NC) % NX == x
            picked[2, k, b] = jnp.where(mine, pick(g, k, b).astype(F32), far_in[k, b].astype(F32)).astype(BF)
        rows[k] = send(picked.at[2, k], lands[k].at[1], row_send.at[2, k], row_recv.at[2, k], row[hop - 1])

    def finish(k):
        rows[k].wait_recv()
        nears[k].wait_recv()
        behind_x = (x + NX - 1) % NX if k % 2 == 1 else (x + 1) % NX
        for b in range(NB):
            source_x = dec_s[NX - 1, 0, b] // (NB * NC) % NX
            which = jnp.where(source_x == x, 0, jnp.where(source_x == behind_x, 2, 1))
            lo = b * NSUB * cells + k * cells
            cot_here[lo : lo + cells, :] = lands[k][which, b]

    hold = {}

    def ready():
        for k in range(NSUB):
            mates[0, k] = send(own(k), pools[k].at[c, z], mate_send.at[0, k], mate_recv.at[0, k], pair)

    def asks():
        for g in range(NX - 1):
            dec_copies[g].wait_recv()
        local = [pltpu.make_async_copy(dec_in.at[g], dec_s.at[g], dec_sem.at[g]) for g in range(NX - 1)]
        local.append(pltpu.make_async_copy(own_v, dec_s.at[NX - 1], dec_sem.at[NX - 1]))
        for copy in local:
            copy.start()
        for copy in local:
            copy.wait()

    def unfold(b):
        if b == 0:
            for copy in loads:
                copy.wait()
        r, q = iota((512, 1), 0), iota((1, 512), 1)
        by_z = ones_where(q == ((r & 63) << 3) + (r >> 6))
        got = dot(by_z, feat_ref[b], 1, 1)
        blank = jnp.zeros((64, 64), F32)
        for t in range(5):
            first = got[128 * t - 64 : 128 * t] if t > 0 else blank
            second = got[128 * t : 128 * t + 64] if t < 4 else blank
            tile = jnp.concatenate([first, second], axis=1).astype(BF)
            source[64 * b : 64 * b + 64, 128 * t : 128 * t + 128] = tile

    halos = []

    def faces():
        r, q = iota((32, 1), 0), iota((1, 512), 1)
        base = ((r >> 3) << 6) + (r & 7)
        for side, start in ((0, 4 * 64 + 56), (1, 0)):
            halo_out[side] = dot(ones_where(q == base + start), source[0:512]).astype(BF)
        halos.append(send(halo_out.at[0], halo_in.at[0], halo_send.at[0], halo_recv.at[0], ahead))
        halos.append(send(halo_out.at[1], halo_in.at[1], halo_send.at[1], halo_recv.at[1], behind))
        source[512:576] = jnp.zeros((64, 640), BF)

    def halo():
        for copy in halos:
            copy.wait_recv()
        source[512:544] = halo_in[0]
        source[544:576] = halo_in[1]

    def tap_step(tap):
        spots = iota((1, 576), 1).astype(F32)
        take = jnp.where(spots == tgt[:, tap : tap + 1], 1.0, 0.0).astype(BF)
        moved = dot(take, source[...]).astype(BF)
        taps[tap] = moved
        w = w_ref[tap]
        low = dot(w, ones_where(iota((64, 128), 0) == iota((64, 128), 1)))
        high = dot(w, ones_where(iota((64, 128), 0) + 64 == iota((64, 128), 1)))
        blank = jnp.zeros((64, 128), F32)
        u = (jnp.concatenate([low, blank], axis=0) + jnp.concatenate([blank, high], axis=0)).astype(BF)
        for t in range(4):
            lanes = slice(128 * t, 128 * t + 128)
            got = dot(moved[:, 128 * t : 128 * t + 256], u)
            pre[:, lanes] = got if tap == 3 else pre[:, lanes] + got

    def hide(ij):
        a = slice(128 * ij, 128 * ij + 128)
        hidden = (silu_of(pre[a, :]) * occ_at[a, :]).astype(BF)
        for r in range(4):
            hid_t[128 * r : 128 * r + 128, a] = hidden[:, 128 * r : 128 * r + 128]

    def coarsen():
        down = dot(hid_t[...], wd_ref[...])
        coarse = silu_of(down).astype(BF)
        hold["slope"] = slope_of(down)
        hold["coarse"] = coarse
        hold["point"] = slope_of(dot(coarse, wp_ref[...]))

    def reslope(ij):
        a = slice(128 * ij, 128 * ij + 128)
        pre[a, :] = occ_at[a, :] * slope_of(pre[a, :])

    def occupy():
        occ_at[...] = occupied_at(occ_ref[...])

    def ordering():
        r = iota((512, 1), 0)
        order_at[...] = ones_where(iota((1, 512), 1) == 4 * (r & 127) + (r >> 7))

    jobs = [lambda b=b: unfold(b) for b in range(8)]
    jobs += [faces, asks, occupy, ordering]
    jobs += [lambda tap=tap: tap_step(tap) for tap in (3, 4, 5)]
    jobs += [halo]
    jobs += [lambda tap=tap: tap_step(tap) for tap in (0, 1, 2, 6, 7, 8)]
    jobs += [lambda ij=ij: hide(ij) for ij in range(4)]
    jobs += [coarsen]
    jobs += [lambda ij=ij: reslope(ij) for ij in range(4)]

    def work():
        if jobs:
            jobs.pop(0)()

    ends = {}
    for i, (s, k) in enumerate(RIGHT):
        if (s + 1, k) not in RIGHT:
            ends.setdefault(i + LAG, []).append((end_right, s, k))
    for i, (s, k) in enumerate(LEFT):
        if (s + 1, k) not in LEFT:
            ends.setdefault(i + LAG, []).append((end_left, s, k))
    left_over = {k: 0 for k in range(NSUB)}
    for group in ends.values():
        for _, s, k in group:
            left_over[k] += 1
    done = dict(left_over)
    waiting, relays, finishes = [], [], []
    for i in range(len(RIGHT) + LAG):
        if i < len(RIGHT):
            go_right(*RIGHT[i])
            go_left(*LEFT[i])
        for f, s, k in ends.get(i, []):
            f(s, k)
            done[k] -= 1
            if done[k] == 0:
                waiting.append((i, k))
        if i == 2:
            ready()
        if i >= 2:
            work()
        while waiting and waiting[0][0] < i:
            k = waiting.pop(0)[1]
            start_rows(k)
            relays.append((i + LAG, k))
        while relays and relays[0][0] <= i:
            k = relays.pop(0)[1]
            relay(k)
            finishes.append(k)
    while waiting:
        k = waiting.pop(0)[1]
        start_rows(k)
        relays.append((0, k))
    for _, k in relays:
        work()
        relay(k)
        finishes.append(k)
    while jobs:
        work()
    for k in finishes:
        finish(k)

    cot = dot(order_at[...], cot_here[...])
    gpoint = (cot * hold["point"]).astype(BF)
    gwp = dot(hold["coarse"], gpoint, 0, 0)
    gplaced = dot(gpoint, wp_ref[...], 1, 1).astype(BF)
    gdown = (gplaced.astype(F32) * hold["slope"]).astype(BF)
    gwd = dot(hid_t[...], gdown, 0, 0)
    ghid = dot(gdown, wd_ref[...], 1, 1)
    for r in range(4):
        for ij in range(4):
            a = slice(128 * ij, 128 * ij + 128)
            b = slice(128 * r, 128 * r + 128)
            gpre_t[b, a] = (ghid[b, a] * pre[a, b]).astype(BF).T
    for e in range(12):
        if e < 8:
            piece = gwd[64 * e : 64 * e + 64, :]
        else:
            r, t = e % 2, (e - 8) // 2
            piece = gwp[64 * r : 64 * r + 64, 128 * t : 128 * t + 128]
        part[e // EARLY * np_ + e % EARLY] = piece

    firsts = []

    def share_part(lo, n):
        i = len(firsts)
        at_ = pl.ds(lo, n)
        tosend[at_] = part[pl.ds((1 - c) * np_ + lo, n)].astype(BF)
        firsts.append(send(tosend.at[at_], arrived.at[at_], pair_send.at[i], pair_recv.at[i], pair))

    def add_part(i, lo, n):
        firsts[i].wait_recv()
        at_ = pl.ds(lo, n)
        plane_out[at_] = (part[pl.ds(c * np_ + lo, n)] + arrived[at_].astype(F32)).astype(BF)

    def later(src, dst, ssem, rsem, mate):
        return pltpu.make_async_remote_copy(
            src_ref=src, dst_ref=dst, send_sem=ssem, recv_sem=rsem, device_id=mate, device_id_type=MESH
        )

    seconds = {
        g: later(plane_out.at[k], plane_in.at[g], plane_send.at[g], plane_recv.at[g], mate) for mate, k, g in plane
    }

    def start_plane(lo, hi):
        for _, k, g in plane:
            pl.when((k >= lo) & (k < hi))(seconds[g].start)

    share_part(0, EARLY)
    for tap in range(9):
        if tap == 4:
            add_part(0, 0, EARLY)
            start_plane(0, EARLY)
        total = jnp.zeros((128, 256), F32)
        for t in range(4):
            total += dot(gpre_t[128 * t : 128 * t + 128, :], taps[tap, :, 128 * t : 128 * t + 256])
        sums[tap] = total.T
    low = iota((64, 128), 1) < 64

    def block(m):
        tap, c3 = m // 3, m % 3
        return sums[tap, 64 * c3 : 64 * c3 + 64, :], sums[tap, 64 * c3 + 64 : 64 * c3 + 128, :]

    for j in range(14):
        a0, a1 = block(2 * j)
        even = a0 + pltpu.roll(a1, 64, 1)
        if 2 * j + 1 < 27:
            b0, b1 = block(2 * j + 1)
            odd = pltpu.roll(b0, 64, 1) + b1
        else:
            odd = jnp.zeros_like(even)
        part[j // 7 * np_ + EARLY + j % 7] = jnp.where(low, even, odd)
    share_part(EARLY, 4)
    share_part(EARLY + 4, USED - EARLY - 4)
    add_part(1, EARLY, 4)
    start_plane(EARLY, EARLY + 4)
    add_part(2, EARLY + 4, USED - EARLY - 4)
    start_plane(EARLY + 4, USED)

    mine = full.at[c, me]
    thirds = [
        later(depth_out, depth_in.at[z], depth_send.at[g], depth_recv.at[g], mate) for g, mate in enumerate(depth)
    ]
    backs = {g: later(mine, mine, back_send.at[g], back_recv.at[g], mate) for mate, k, g in plane}
    first_share = later(mine, mine, share_send.at[0], share_recv.at[0], pair)

    @pl.when(me < USED)
    def _():
        total = plane_out[me].astype(F32)
        for g in range(1, np_):
            seconds[g].wait_recv()
            total += plane_in[g].astype(F32)
        depth_out[...] = total.astype(BF)
        for copy in thirds:
            copy.start()
        depth_in[z] = total.astype(BF)
        for copy in thirds:
            copy.wait_recv()
        total = depth_in[0].astype(F32)
        for k in range(1, nz):
            total += depth_in[k].astype(F32)
        full[c, me] = total.astype(BF)
        for copy in backs.values():
            copy.start()
        first_share.start()

    shares = []
    for g in range(1, np_):
        k = (y + ny - g // NX) % ny * NX + (x + NX - g % NX) % NX
        home = full.at[c, k]
        share = later(home, home, share_send.at[g], share_recv.at[g], pair)
        shares.append((k, share))

        @pl.when(k < USED)
        def _(g=g, share=share):
            backs[g].wait_recv()
            share.start()

    for k, share in [(me, first_share)] + shares:
        pl.when(k < USED)(share.wait)
    full_ref[...] = full[:, :USED]

    @pl.when(me < USED)
    def _():
        for copy in thirds + list(backs.values()):
            copy.wait_send()

    for _, k, g in plane:
        pl.when(k < USED)(seconds[g].wait_send)
    for copy in pending:
        copy.wait_send()


def unpack_kernel(full_ref, gwc_ref, gwd_ref, gwp_ref):
    for j in range(14):
        chunk = full_ref[j // 7, EARLY + j % 7].astype(F32)
        gwc_ref[2 * j] = chunk[:, :64]
        if 2 * j + 1 < 27:
            gwc_ref[2 * j + 1] = pltpu.roll(chunk, 64, 1)[:, :64]
    for e in range(12):
        chunk = full_ref[e // EARLY, e % EARLY].astype(F32)
        if e < 8:
            gwd_ref[64 * e : 64 * e + 64, :] = chunk
        else:
            r, t = e % 2, (e - 8) // 2
            gwp_ref[64 * r : 64 * r + 64, 128 * t : 128 * t + 128] = chunk


def unpack(full):
    vmem = pl.BlockSpec(memory_space=pltpu.VMEM)
    return pl.pallas_call(
        unpack_kernel,
        out_shape=(
            jax.ShapeDtypeStruct((27, 64, 64), F32),
            jax.ShapeDtypeStruct((512, 128), F32),
            jax.ShapeDtypeStruct((128, 256), F32),
        ),
        in_specs=[vmem],
        out_specs=(vmem,) * 3,
        name="unpack",
    )(full)


def step(nz, ny, feat, cot, owners, near, occ, w, wd, wp):
    slots, cells, wide = cot.shape
    chunk = (slots, cells // NSUB, wide)
    dma = pltpu.SemaphoreType.DMA
    vmem = pl.BlockSpec(memory_space=pltpu.VMEM)
    hbm = pl.BlockSpec(memory_space=pl.ANY)
    far = nz // 2
    np_ = ny * NX
    return pl.pallas_call(
        lambda *refs: step_kernel(nz, ny, *refs),
        out_shape=jax.ShapeDtypeStruct((NC, USED, 64, 128), BF),
        in_specs=[hbm, hbm] + [vmem] * 3 + [hbm] * 3,
        out_specs=vmem,
        scratch_shapes=[
            pltpu.VMEM(feat.shape, BF),
            pltpu.VMEM(w.shape, BF),
            pltpu.VMEM(wd.shape, BF),
            pltpu.VMEM(wp.shape, BF),
            dma((4,)), dma((NSUB,)),
            pltpu.VMEM((576, 640), BF),
            pltpu.VMEM((2, 32, 640), BF),
            pltpu.VMEM((2, 32, 640), BF),
            *[pltpu.VMEM((NC, nz) + chunk, BF)] * NSUB,
            pltpu.VMEM((3, NSUB) + chunk, BF),
            pltpu.VMEM((NSUB,) + chunk, BF),
            *[pltpu.VMEM((3,) + chunk, BF)] * NSUB,
            pltpu.VMEM((NX - 1,) + owners.shape, jnp.int32),
            pltpu.SMEM((NX,) + owners.shape, jnp.int32),
            pltpu.VMEM((9, 512, 640), BF),
            pltpu.VMEM((512, 512), F32),
            pltpu.VMEM((512, 512), F32),
            pltpu.VMEM((512, 512), BF),
            pltpu.VMEM((512, 512), BF),
            pltpu.VMEM((9, 256, 128), F32),
            pltpu.VMEM((2 * np_, 64, 128), F32),
            pltpu.VMEM((slots * cells, wide), BF),
            pltpu.VMEM((512, 512), BF),
            pltpu.VMEM((np_, 64, 128), BF),
            pltpu.VMEM((np_, 64, 128), BF),
            pltpu.VMEM((np_, 64, 128), BF),
            pltpu.VMEM((np_, 64, 128), BF),
            pltpu.VMEM((64, 128), BF),
            pltpu.VMEM((nz, 64, 128), BF),
            pltpu.VMEM((NC, np_, 64, 128), BF),
            dma((2,)), dma((2,)), dma((NX - 1,)), dma((NX - 1,)), dma((NX,)),
            dma((far, NSUB)), dma((far, NSUB)), dma((far, NSUB)), dma((far, NSUB)),
            dma((nz, NSUB)), dma((nz, NSUB)), dma((NX - 1, NSUB)), dma((NX - 1, NSUB)),
            dma((4,)), dma((4,)), dma((np_,)), dma((np_,)), dma((nz,)), dma((nz,)),
            dma((np_,)), dma((np_,)), dma((np_,)), dma((np_,)),
        ],
        compiler_params=pltpu.CompilerParams(collective_id=0, has_side_effects=True),
        name="step",
    )(feat, cot, owners, near, occ, w, wd, wp)


def shards(features, occupancy, neighbours, owners, w_conv, w_down, w_point, cotangent):
    nz = lax.axis_size("brick") // (NX * NC)
    ny = lax.axis_size("dp")
    full = step(
        nz, ny, jnp.swapaxes(features[0], 1, 2), cotangent[0], owners, neighbours[0], occupancy[0],
        w_conv.reshape(9, 192, 64), w_down.reshape(512, 128), w_point,
    )
    gwc, gwd, gwp = unpack(full)
    return gwc.reshape(3, 3, 3, 64, 64), gwd.reshape(2, 2, 2, 64, 128), gwp


def solution(mesh):
    in_specs = (
        P("dp", "brick", None, None),
        P("dp", "brick", None),
        P("dp", "brick", None),
        P("dp", "brick"),
        P(),
        P(),
        P(),
        P("dp", "brick", None, None),
    )
    return jax.shard_map(shards, mesh=mesh, in_specs=in_specs, out_specs=(P(), P(), P()), check_vma=False)
```

```python
import jax
import jax.numpy as jnp
import numpy as np
from jax import lax
from jax.experimental import pallas as pl
from jax.experimental.pallas import tpu as pltpu
from jax.sharding import PartitionSpec as P

MESH = pl.DeviceIdType.MESH
NX = 4
NC = 2
NSUB = 4
NB = 8
HALF = 4
BF = jnp.bfloat16
F32 = jnp.float32


def where_am_i():
    spot = lax.axis_index("brick")
    return spot // (NX * NC), spot // NC % NX, spot % NC


def hops(step, size):
    return min(step, size - step)


def brick_at(z, x, c):
    return (z * NX + x) * NC + c


def slope_of(v):
    g = 1.0 / (1.0 + jnp.exp(-v))
    return g * (1.0 + v * (1.0 - g))


def silu_of(v):
    return v / (1.0 + jnp.exp(-v))


def dot(a, b, ca=1, cb=0):
    return lax.dot_general(a, b, (((ca,), (cb,)), ((), ())), preferred_element_type=F32)


RIGHT = ((1, 0), (1, 1), (1, 2), (2, 0), (2, 1), (2, 2), (1, 3), (3, 0), (3, 1), (3, 2), (2, 3), (4, 0), (4, 2), (3, 3))
LEFT = tuple((s, k ^ 1) for s, k in RIGHT)
LAG = 3
EARLY = 6
USED = 13


def iota(shape, dim):
    return lax.broadcasted_iota(jnp.int32, shape, dim)


def ones_where(mask):
    return jnp.where(mask, 1.0, 0.0).astype(BF)


def brick_rows():
    return ones_where((iota((512, 8), 0) >> 4 & 7) == iota((512, 8), 1))


def tap_targets(near):
    row, tap = iota((512, 1), 0), iota((1, 16), 1)
    n = row >> 4 & 7
    third = (tap * 11) >> 5
    x = ((row >> 2 & 3) * 2 + (row >> 8)) + (third - 1)
    y = ((row & 3) * 2 + (row >> 7 & 1)) + (tap - 3 * third - 1)
    dx, dy = (x + 8) >> 3, (y + 8) >> 3
    px, py = (n >> 2) + dx - 1, (n & 3) + dy - 1
    side = py * 8 + (y & 7)
    spot = side + jnp.where(px < 0, 512, jnp.where(px > 1, 544, (x & 7) * 8 + px * 256 + py * 56))
    linked = ones_where(near >= 0)
    narrow = ones_where(iota((27, 16), 0) == 3 * iota((27, 16), 1) + 1)
    by_row = dot(brick_rows(), dot(linked, narrow).astype(BF))
    code = 3 * dx + dy
    flag = jnp.zeros((512, 16), F32)
    for d in range(9):
        flag = jnp.where(code == d, by_row[:, d : d + 1], flag)
    return jnp.where(flag > 0.5, spot.astype(F32), -1.0)


def occupied_at(occ):
    row, lane = iota((512, 1), 0), iota((1, 512), 1)
    every = dot(brick_rows(), occ.astype(F32).astype(BF))
    mine = ((row >> 2 & 3) * 2 + (row >> 8)) * 8 + (row & 3) * 2 + (row >> 7 & 1)
    own = jnp.where((lane >> 3) == mine, every, 0.0).astype(BF)
    spread = ones_where((row & 7) == (lane >> 6))
    return dot(own, spread)


def step_kernel(
    nz, ny, feat_any, cot_ref, own_v, near_ref, occ_ref, w_any, wd_any, wp_any,
    full_ref,
    feat_ref, w_ref, wd_ref, wp_ref, load_sem, fill_sem, source, halo_out, halo_in, pool0, pool1, pool2, pool3, picked, far_in, land0, land1, land2, land3, dec_in, dec_s,
    taps, pre, occ_at, hid_t, gpre_t, sums, part, cot_here, order_at,
    tosend, arrived, plane_out, plane_in, depth_out, depth_in, full,
    halo_send, halo_recv, dec_send, dec_recv, dec_sem,
    right_send, right_recv, left_send, left_recv, mate_send, mate_recv, row_send, row_recv,
    pair_send, pair_recv, plane_send, plane_recv, depth_send, depth_recv,
    back_send, back_recv, share_send, share_recv,
):
    z, x, c = where_am_i()
    y = lax.axis_index("dp")
    spot = lax.axis_index("brick")
    many = nz * NX * NC
    np_ = ny * NX
    me = y * NX + x

    def at(yy, brick):
        return {"dp": yy, "brick": brick}

    right, left = at(y, brick_at((z + 1) % nz, x, c)), at(y, brick_at((z + nz - 1) % nz, x, c))
    pair = at(y, brick_at(z, x, 1 - c))
    row = [at(y, brick_at(z, (x + g) % NX, c)) for g in range(1, NX)]
    ahead, behind = at(y, (spot + 1) % many), at(y, (spot + many - 1) % many)
    plane = []
    for g in sorted(range(1, np_), key=lambda g: -hops(g // NX, ny) - hops(g % NX, NX)):
        yy, xx = (y + g // NX) % ny, (x + g % NX) % NX
        plane.append((at(yy, brick_at(z, xx, c)), yy * NX + xx, g))
    depth = [at(y, brick_at((z + g) % nz, x, c)) for g in sorted(range(1, nz), key=lambda g: -hops(g, nz))]
    mates_all = [pair, ahead, behind] + [p[0] for p in plane] + depth
    barrier = pltpu.get_barrier_semaphore()
    for mate in mates_all:
        pl.semaphore_signal(barrier, inc=1, device_id=mate, device_id_type=MESH)
    fills = []
    for k in range(NSUB):
        quarter = cot_ref.shape[1] // NSUB
        home = (pool0, pool1, pool2, pool3)[k].at[c, z]
        fills.append(pltpu.make_async_copy(cot_ref.at[:, pl.ds(k * quarter, quarter), :], home, fill_sem.at[k]))
    pairs_in = ((feat_any, feat_ref), (w_any, w_ref), (wd_any, wd_ref), (wp_any, wp_ref))
    loads = [pltpu.make_async_copy(src, dst, load_sem.at[i]) for i, (src, dst) in enumerate(pairs_in)]
    for copy in fills + loads:
        copy.start()
    tgt = tap_targets(near_ref[...])
    pl.semaphore_wait(barrier, len(mates_all))

    lands = [land0, land1, land2, land3]
    pools = [pool0, pool1, pool2, pool3]
    pending = []

    def send(src, dst, ssem, rsem, mate):
        copy = pltpu.make_async_remote_copy(
            src_ref=src, dst_ref=dst, send_sem=ssem, recv_sem=rsem, device_id=mate, device_id_type=MESH
        )
        copy.start()
        pending.append(copy)
        return copy

    dec_copies = [send(own_v, dec_in.at[g], dec_send.at[g], dec_recv.at[g], row[g]) for g in range(NX - 1)]
    cells = cot_ref.shape[1] // NSUB
    rights, lefts, mates, rows = {}, {}, {}, {}

    def own(k):
        return cot_ref.at[:, pl.ds(k * cells, cells), :]

    def go_right(s, k):
        if s == 1:
            rights[1, k] = send(own(k), pools[k].at[c, z], right_send.at[0, k], right_recv.at[0, k], right)
            return
        rights[s - 1, k].wait_recv()
        home = pools[k].at[c, (z + nz - s + 1) % nz]
        rights[s, k] = send(home, home, right_send.at[s - 1, k], right_recv.at[s - 1, k], right)
        mates[s - 1, k] = send(home, home, mate_send.at[s - 1, k], mate_recv.at[s - 1, k], pair)

    def go_left(s, k):
        if s == 1:
            lefts[1, k] = send(own(k), pools[k].at[c, z], left_send.at[0, k], left_recv.at[0, k], left)
            return
        lefts[s - 1, k].wait_recv()
        home = pools[k].at[c, (z + s - 1) % nz]
        lefts[s, k] = send(home, home, left_send.at[s - 1, k], left_recv.at[s - 1, k], left)
        t = nz - s + 1
        mates[t, k] = send(home, home, mate_send.at[t, k], mate_recv.at[t, k], pair)

    def end_right(s, k):
        rights[s, k].wait_recv()
        home = pools[k].at[c, (z + nz - s) % nz]
        mates[s, k] = send(home, home, mate_send.at[s, k], mate_recv.at[s, k], pair)

    def end_left(s, k):
        lefts[s, k].wait_recv()
        home = pools[k].at[c, (z + s) % nz]
        t = nz - s
        mates[t, k] = send(home, home, mate_send.at[t, k], mate_recv.at[t, k], pair)

    def pick(g, k, b):
        o = dec_s[g, 0, b]
        return pools[k][o // NB % NC, o // (NB * NC * NX), o % NB]

    fars, nears = {}, {}

    def start_rows(k):
        fills[k].wait()
        for t in range(nz):
            mates[t, k].wait_recv()
        hop = 1 if k % 2 == 0 else NX - 1
        for h in range(2):
            for b in range(HALF * h, HALF * h + HALF):
                picked[0, k, b] = pick(NX - 1 - NX // 2, k, b)
            part_of = pl.ds(HALF * h, HALF)
            i = 3 * h
            fars[k, h] = send(
                picked.at[0, k, part_of], far_in.at[k, part_of], row_send.at[i, k], row_recv.at[i, k], row[hop - 1]
            )
        back = NX - hop
        for b in range(NB):
            picked[1, k, b] = pick(NX - 1 - back, k, b)
        nears[k] = send(picked.at[1, k], lands[k].at[2], row_send.at[1, k], row_recv.at[1, k], row[back - 1])
        for b in range(NB):
            lands[k][0, b] = pick(NX - 1, k, b)

    def relay(k):
        hop = 1 if k % 2 == 0 else NX - 1
        g = NX - 1 - hop
        for h in range(2):
            fars[k, h].wait_recv()
            for b in range(HALF * h, HALF * h + HALF):
                mine = dec_s[g, 0, b] // (NB * NC) % NX == x
                picked[2, k, b] = jnp.where(mine, pick(g, k, b).astype(F32), far_in[k, b].astype(F32)).astype(BF)
            part_of = pl.ds(HALF * h, HALF)
            i = 2 + 2 * h
            rows[k, h] = send(
                picked.at[2, k, part_of], lands[k].at[1, part_of], row_send.at[i, k], row_recv.at[i, k], row[hop - 1]
            )

    def finish(k):
        rows[k, 0].wait_recv()
        rows[k, 1].wait_recv()
        nears[k].wait_recv()
        behind_x = (x + NX - 1) % NX if k % 2 == 1 else (x + 1) % NX
        for b in range(NB):
            source_x = dec_s[NX - 1, 0, b] // (NB * NC) % NX
            which = jnp.where(source_x == x, 0, jnp.where(source_x == behind_x, 2, 1))
            lo = b * NSUB * cells + k * cells
            cot_here[lo : lo + cells, :] = lands[k][which, b]

    hold = {}

    def ready():
        for k in range(NSUB):
            mates[0, k] = send(own(k), pools[k].at[c, z], mate_send.at[0, k], mate_recv.at[0, k], pair)

    def asks():
        for g in range(NX - 1):
            dec_copies[g].wait_recv()
        local = [pltpu.make_async_copy(dec_in.at[g], dec_s.at[g], dec_sem.at[g]) for g in range(NX - 1)]
        local.append(pltpu.make_async_copy(own_v, dec_s.at[NX - 1], dec_sem.at[NX - 1]))
        for copy in local:
            copy.start()
        for copy in local:
            copy.wait()

    def unfold(b):
        if b == 0:
            for copy in loads:
                copy.wait()
        r, q = iota((512, 1), 0), iota((1, 512), 1)
        by_z = ones_where(q == ((r & 63) << 3) + (r >> 6))
        got = dot(by_z, feat_ref[b], 1, 1)
        blank = jnp.zeros((64, 64), F32)
        for t in range(5):
            first = got[128 * t - 64 : 128 * t] if t > 0 else blank
            second = got[128 * t : 128 * t + 64] if t < 4 else blank
            tile = jnp.concatenate([first, second], axis=1).astype(BF)
            source[64 * b : 64 * b + 64, 128 * t : 128 * t + 128] = tile

    halos = []

    def faces():
        r, q = iota((32, 1), 0), iota((1, 512), 1)
        base = ((r >> 3) << 6) + (r & 7)
        for side, start in ((0, 4 * 64 + 56), (1, 0)):
            halo_out[side] = dot(ones_where(q == base + start), source[0:512]).astype(BF)
        halos.append(send(halo_out.at[0], halo_in.at[0], halo_send.at[0], halo_recv.at[0], ahead))
        halos.append(send(halo_out.at[1], halo_in.at[1], halo_send.at[1], halo_recv.at[1], behind))
        source[512:576] = jnp.zeros((64, 640), BF)

    def halo():
        for copy in halos:
            copy.wait_recv()
        source[512:544] = halo_in[0]
        source[544:576] = halo_in[1]

    def tap_step(tap):
        spots = iota((1, 576), 1).astype(F32)
        take = jnp.where(spots == tgt[:, tap : tap + 1], 1.0, 0.0).astype(BF)
        moved = dot(take, source[...]).astype(BF)
        taps[tap] = moved
        w = w_ref[tap]
        low = dot(w, ones_where(iota((64, 128), 0) == iota((64, 128), 1)))
        high = dot(w, ones_where(iota((64, 128), 0) + 64 == iota((64, 128), 1)))
        blank = jnp.zeros((64, 128), F32)
        u = (jnp.concatenate([low, blank], axis=0) + jnp.concatenate([blank, high], axis=0)).astype(BF)
        for t in range(4):
            lanes = slice(128 * t, 128 * t + 128)
            got = dot(moved[:, 128 * t : 128 * t + 256], u)
            pre[:, lanes] = got if tap == 3 else pre[:, lanes] + got

    def hide(ij):
        a = slice(128 * ij, 128 * ij + 128)
        hidden = (silu_of(pre[a, :]) * occ_at[a, :]).astype(BF)
        for r in range(4):
            hid_t[128 * r : 128 * r + 128, a] = hidden[:, 128 * r : 128 * r + 128]

    def coarsen():
        down = dot(hid_t[...], wd_ref[...])
        coarse = silu_of(down).astype(BF)
        hold["slope"] = slope_of(down)
        hold["coarse"] = coarse
        hold["point"] = slope_of(dot(coarse, wp_ref[...]))

    def reslope(ij):
        a = slice(128 * ij, 128 * ij + 128)
        pre[a, :] = occ_at[a, :] * slope_of(pre[a, :])

    def occupy():
        occ_at[...] = occupied_at(occ_ref[...])

    def ordering():
        r = iota((512, 1), 0)
        order_at[...] = ones_where(iota((1, 512), 1) == 4 * (r & 127) + (r >> 7))

    jobs = [lambda b=b: unfold(b) for b in range(8)]
    jobs += [faces, asks, occupy, ordering]
    jobs += [lambda tap=tap: tap_step(tap) for tap in (3, 4, 5)]
    jobs += [halo]
    jobs += [lambda tap=tap: tap_step(tap) for tap in (0, 1, 2, 6, 7, 8)]
    jobs += [lambda ij=ij: hide(ij) for ij in range(4)]
    jobs += [coarsen]
    jobs += [lambda ij=ij: reslope(ij) for ij in range(4)]

    def work():
        if jobs:
            jobs.pop(0)()

    ends = {}
    for i, (s, k) in enumerate(RIGHT):
        if (s + 1, k) not in RIGHT:
            ends.setdefault(i + LAG, []).append((end_right, s, k))
    for i, (s, k) in enumerate(LEFT):
        if (s + 1, k) not in LEFT:
            ends.setdefault(i + LAG, []).append((end_left, s, k))
    left_over = {k: 0 for k in range(NSUB)}
    for group in ends.values():
        for _, s, k in group:
            left_over[k] += 1
    done = dict(left_over)
    waiting, relays, finishes = [], [], []
    for i in range(len(RIGHT) + LAG):
        if i < len(RIGHT):
            go_right(*RIGHT[i])
            go_left(*LEFT[i])
        for f, s, k in ends.get(i, []):
            f(s, k)
            done[k] -= 1
            if done[k] == 0:
                waiting.append((i, k))
        if i == 2:
            ready()
        if i >= 2:
            work()
        while waiting and waiting[0][0] < i:
            k = waiting.pop(0)[1]
            start_rows(k)
            relays.append((i + LAG, k))
        while relays and relays[0][0] <= i:
            k = relays.pop(0)[1]
            relay(k)
            finishes.append(k)
    while waiting:
        k = waiting.pop(0)[1]
        start_rows(k)
        relays.append((0, k))
    for _, k in relays:
        work()
        relay(k)
        finishes.append(k)
    while jobs:
        work()
    for k in finishes:
        finish(k)

    cot = dot(order_at[...], cot_here[...])
    gpoint = (cot * hold["point"]).astype(BF)
    gwp = dot(hold["coarse"], gpoint, 0, 0)
    gplaced = dot(gpoint, wp_ref[...], 1, 1).astype(BF)
    gdown = (gplaced.astype(F32) * hold["slope"]).astype(BF)
    gwd = dot(hid_t[...], gdown, 0, 0)
    ghid = dot(gdown, wd_ref[...], 1, 1)
    for r in range(4):
        for ij in range(4):
            a = slice(128 * ij, 128 * ij + 128)
            b = slice(128 * r, 128 * r + 128)
            gpre_t[b, a] = (ghid[b, a] * pre[a, b]).astype(BF).T
    for e in range(12):
        if e < 8:
            piece = gwd[64 * e : 64 * e + 64, :]
        else:
            r, t = e % 2, (e - 8) // 2
            piece = gwp[64 * r : 64 * r + 64, 128 * t : 128 * t + 128]
        part[e // EARLY * np_ + e % EARLY] = piece

    firsts = []

    def share_part(lo, n):
        i = len(firsts)
        at_ = pl.ds(lo, n)
        tosend[at_] = part[pl.ds((1 - c) * np_ + lo, n)].astype(BF)
        firsts.append(send(tosend.at[at_], arrived.at[at_], pair_send.at[i], pair_recv.at[i], pair))

    def add_part(i, lo, n):
        firsts[i].wait_recv()
        at_ = pl.ds(lo, n)
        plane_out[at_] = (part[pl.ds(c * np_ + lo, n)] + arrived[at_].astype(F32)).astype(BF)

    def later(src, dst, ssem, rsem, mate):
        return pltpu.make_async_remote_copy(
            src_ref=src, dst_ref=dst, send_sem=ssem, recv_sem=rsem, device_id=mate, device_id_type=MESH
        )

    seconds = {
        g: later(plane_out.at[k], plane_in.at[g], plane_send.at[g], plane_recv.at[g], mate) for mate, k, g in plane
    }

    def start_plane(lo, hi):
        for _, k, g in plane:
            pl.when((k >= lo) & (k < hi))(seconds[g].start)

    share_part(0, EARLY)
    for tap in range(9):
        if tap == 4:
            add_part(0, 0, EARLY)
            start_plane(0, EARLY)
        total = jnp.zeros((128, 256), F32)
        for t in range(4):
            total += dot(gpre_t[128 * t : 128 * t + 128, :], taps[tap, :, 128 * t : 128 * t + 256])
        sums[tap] = total.T
    low = iota((64, 128), 1) < 64

    def block(m):
        tap, c3 = m // 3, m % 3
        return sums[tap, 64 * c3 : 64 * c3 + 64, :], sums[tap, 64 * c3 + 64 : 64 * c3 + 128, :]

    for j in range(14):
        a0, a1 = block(2 * j)
        even = a0 + pltpu.roll(a1, 64, 1)
        if 2 * j + 1 < 27:
            b0, b1 = block(2 * j + 1)
            odd = pltpu.roll(b0, 64, 1) + b1
        else:
            odd = jnp.zeros_like(even)
        part[j // 7 * np_ + EARLY + j % 7] = jnp.where(low, even, odd)
    share_part(EARLY, 4)
    share_part(EARLY + 4, USED - EARLY - 4)
    add_part(1, EARLY, 4)
    start_plane(EARLY, EARLY + 4)
    add_part(2, EARLY + 4, USED - EARLY - 4)
    start_plane(EARLY + 4, USED)

    mine = full.at[c, me]
    thirds = [
        later(depth_out, depth_in.at[z], depth_send.at[g], depth_recv.at[g], mate) for g, mate in enumerate(depth)
    ]
    backs = {g: later(mine, mine, back_send.at[g], back_recv.at[g], mate) for mate, k, g in plane}
    first_share = later(mine, mine, share_send.at[0], share_recv.at[0], pair)

    @pl.when(me < USED)
    def _():
        total = plane_out[me].astype(F32)
        for g in range(1, np_):
            seconds[g].wait_recv()
            total += plane_in[g].astype(F32)
        depth_out[...] = total.astype(BF)
        for copy in thirds:
            copy.start()
        depth_in[z] = total.astype(BF)
        for copy in thirds:
            copy.wait_recv()
        total = depth_in[0].astype(F32)
        for k in range(1, nz):
            total += depth_in[k].astype(F32)
        full[c, me] = total.astype(BF)
        for copy in backs.values():
            copy.start()
        first_share.start()

    shares = []
    for g in range(1, np_):
        k = (y + ny - g // NX) % ny * NX + (x + NX - g % NX) % NX
        home = full.at[c, k]
        share = later(home, home, share_send.at[g], share_recv.at[g], pair)
        shares.append((k, share))

        @pl.when(k < USED)
        def _(g=g, share=share):
            backs[g].wait_recv()
            share.start()

    for k, share in [(me, first_share)] + shares:
        pl.when(k < USED)(share.wait)
    full_ref[...] = full[:, :USED]

    @pl.when(me < USED)
    def _():
        for copy in thirds + list(backs.values()):
            copy.wait_send()

    for _, k, g in plane:
        pl.when(k < USED)(seconds[g].wait_send)
    for copy in pending:
        copy.wait_send()


def unpack_kernel(full_ref, gwc_ref, gwd_ref, gwp_ref):
    for j in range(14):
        chunk = full_ref[j // 7, EARLY + j % 7].astype(F32)
        gwc_ref[2 * j] = chunk[:, :64]
        if 2 * j + 1 < 27:
            gwc_ref[2 * j + 1] = pltpu.roll(chunk, 64, 1)[:, :64]
    for e in range(12):
        chunk = full_ref[e // EARLY, e % EARLY].astype(F32)
        if e < 8:
            gwd_ref[64 * e : 64 * e + 64, :] = chunk
        else:
            r, t = e % 2, (e - 8) // 2
            gwp_ref[64 * r : 64 * r + 64, 128 * t : 128 * t + 128] = chunk


def unpack(full):
    vmem = pl.BlockSpec(memory_space=pltpu.VMEM)
    return pl.pallas_call(
        unpack_kernel,
        out_shape=(
            jax.ShapeDtypeStruct((27, 64, 64), F32),
            jax.ShapeDtypeStruct((512, 128), F32),
            jax.ShapeDtypeStruct((128, 256), F32),
        ),
        in_specs=[vmem],
        out_specs=(vmem,) * 3,
        name="unpack",
    )(full)


def step(nz, ny, feat, cot, owners, near, occ, w, wd, wp):
    slots, cells, wide = cot.shape
    chunk = (slots, cells // NSUB, wide)
    dma = pltpu.SemaphoreType.DMA
    vmem = pl.BlockSpec(memory_space=pltpu.VMEM)
    hbm = pl.BlockSpec(memory_space=pl.ANY)
    far = nz // 2
    np_ = ny * NX
    return pl.pallas_call(
        lambda *refs: step_kernel(nz, ny, *refs),
        out_shape=jax.ShapeDtypeStruct((NC, USED, 64, 128), BF),
        in_specs=[hbm, hbm] + [vmem] * 3 + [hbm] * 3,
        out_specs=vmem,
        scratch_shapes=[
            pltpu.VMEM(feat.shape, BF),
            pltpu.VMEM(w.shape, BF),
            pltpu.VMEM(wd.shape, BF),
            pltpu.VMEM(wp.shape, BF),
            dma((4,)), dma((NSUB,)),
            pltpu.VMEM((576, 640), BF),
            pltpu.VMEM((2, 32, 640), BF),
            pltpu.VMEM((2, 32, 640), BF),
            *[pltpu.VMEM((NC, nz) + chunk, BF)] * NSUB,
            pltpu.VMEM((3, NSUB) + chunk, BF),
            pltpu.VMEM((NSUB,) + chunk, BF),
            *[pltpu.VMEM((3,) + chunk, BF)] * NSUB,
            pltpu.VMEM((NX - 1,) + owners.shape, jnp.int32),
            pltpu.SMEM((NX,) + owners.shape, jnp.int32),
            pltpu.VMEM((9, 512, 640), BF),
            pltpu.VMEM((512, 512), F32),
            pltpu.VMEM((512, 512), F32),
            pltpu.VMEM((512, 512), BF),
            pltpu.VMEM((512, 512), BF),
            pltpu.VMEM((9, 256, 128), F32),
            pltpu.VMEM((2 * np_, 64, 128), F32),
            pltpu.VMEM((slots * cells, wide), BF),
            pltpu.VMEM((512, 512), BF),
            pltpu.VMEM((np_, 64, 128), BF),
            pltpu.VMEM((np_, 64, 128), BF),
            pltpu.VMEM((np_, 64, 128), BF),
            pltpu.VMEM((np_, 64, 128), BF),
            pltpu.VMEM((64, 128), BF),
            pltpu.VMEM((nz, 64, 128), BF),
            pltpu.VMEM((NC, np_, 64, 128), BF),
            dma((2,)), dma((2,)), dma((NX - 1,)), dma((NX - 1,)), dma((NX,)),
            dma((far, NSUB)), dma((far, NSUB)), dma((far, NSUB)), dma((far, NSUB)),
            dma((nz, NSUB)), dma((nz, NSUB)), dma((NX + 1, NSUB)), dma((NX + 1, NSUB)),
            dma((4,)), dma((4,)), dma((np_,)), dma((np_,)), dma((nz,)), dma((nz,)),
            dma((np_,)), dma((np_,)), dma((np_,)), dma((np_,)),
        ],
        compiler_params=pltpu.CompilerParams(collective_id=0, has_side_effects=True),
        name="step",
    )(feat, cot, owners, near, occ, w, wd, wp)


def shards(features, occupancy, neighbours, owners, w_conv, w_down, w_point, cotangent):
    nz = lax.axis_size("brick") // (NX * NC)
    ny = lax.axis_size("dp")
    full = step(
        nz, ny, jnp.swapaxes(features[0], 1, 2), cotangent[0], owners, neighbours[0], occupancy[0],
        w_conv.reshape(9, 192, 64), w_down.reshape(512, 128), w_point,
    )
    gwc, gwd, gwp = unpack(full)
    return gwc.reshape(3, 3, 3, 64, 64), gwd.reshape(2, 2, 2, 64, 128), gwp


def solution(mesh):
    in_specs = (
        P("dp", "brick", None, None),
        P("dp", "brick", None),
        P("dp", "brick", None),
        P("dp", "brick"),
        P(),
        P(),
        P(),
        P("dp", "brick", None, None),
    )
    return jax.shard_map(shards, mesh=mesh, in_specs=in_specs, out_specs=(P(), P(), P()), check_vma=False)
```
